512 devices in a mesh: gx: 8 (over y, core), gy: 4 (over x), gz: 16 (over z).
Axes of the slice: x: 4, y: 4, z: 16, core: 2. Of those that a mesh axis runs over, the one named last changes fastest.
Arguments:
- conc: float32 [128, 64, 2048], P('gx', 'gy', 'gz'), may hold values from 0 to 1
- right_side: float32 [128, 64, 2048], P('gx', 'gy', 'gz'), may hold values from -6144 to 6144
- order_field: bfloat16 [8, 128, 64, 2048], P(None, 'gx', 'gy', 'gz'), may hold values from 0 to 1
- grain_ids: int32 [8, 4, 128, 8], P('gx', 'gy', 'gz'), may hold values from 0 to 4095, as said below
Outputs:
- solution: float32 [128, 64, 2048], P('gx', 'gy', 'gz')
- mobility: float32 [128, 64, 2048], P('gx', 'gy', 'gz')
The draws below stay inside these ranges and needn't reach their ends.
Inputs may be any that keep to these rules, and one draw needn't show every extreme that they name: `grain_ids`: the 8 ids of one block are distinct; neighbouring blocks share some grains, usually in other slots.
All inputs are finite; a program needn't handle non-finite values.
Results may differ from the reference program's by a relative error of at most 0.0019.
Values may be sent and summed in bfloat16 or wider, within the bound.
No kernel may reach another device: no remote copies, remote signals or barrier semaphores. Data moves between devices by JAX's collectives and lax.ppermute only.
A program may use at most 128 MiB of HBM per device.

```python
import jax
import jax.numpy as jnp

SLOTS = 8
BRICK = 16
SMOOTH = 2
COARSE_SWEEPS = 8
NX = 128
NY = 64
NZ = 2048
NBX = 8
NBY = 4
NBZ = 128


def draw_grain_ids(key, part):
    slot = jnp.arange(SLOTS, dtype=jnp.int32)
    step_x = slot % 2
    step_y = slot // 2 % 2
    step_z = slot // 4 % 2
    brick_x = jnp.arange(NBX, dtype=jnp.int32)[:, None, None, None]
    brick_y = jnp.arange(NBY, dtype=jnp.int32)[None, :, None, None]
    brick_z = jnp.arange(NBZ, dtype=jnp.int32)[None, None, :, None]
    grain = (brick_x + step_x) % NBX * (NBY * NBZ) + (brick_y + step_y) % NBY * NBZ + (brick_z + step_z) % NBZ
    grain = jnp.broadcast_to(grain, (NBX, NBY, NBZ, SLOTS))
    scores = jax.random.randint(key, (NBX, NBY, NBZ, SLOTS), 0, 1 << 20) * SLOTS + slot
    order = jnp.argsort(scores, axis=-1)
    return jnp.take_along_axis(grain, order, axis=-1).astype(jnp.int32)


def shard_levels(own_key, shape, shards, low, high):
    gain = 1.0
    for dim, shards_of in shards:
        draws = jax.random.uniform(jax.random.fold_in(jax.random.fold_in(own_key, 6), dim), (shards_of,), jnp.float32, low / len(shards), high / len(shards))
        gain = gain * jnp.repeat(jnp.exp(draws), shape[dim] // shards_of).reshape((-1,) + (1,) * (len(shape) - 1 - dim))
    return gain


def noise(stream_key, dims, deviation, limit, cuts=(), kind=jnp.bfloat16):
    values = jax.random.normal(stream_key, dims, jnp.float32) * deviation
    if len(cuts) > 0:
        values = shard_levels(stream_key, dims, cuts, -0.22, 0.18) * values
    return jnp.clip(values, min=-limit, max=limit).astype(kind)


def setup_inputs(seed: int = 0) -> dict:
    seeds = jax.random.split(jax.random.key(seed), 5)
    return {
        "conc": jnp.clip(1.0 * jax.random.uniform(seeds[0], (NX, NY, NZ), jnp.float32) ** shard_levels(seeds[0], (NX, NY, NZ), ((0, 8), (1, 4), (2, 16)), -0.2, 0.2), 0.0, 1.0),
        "right_side": noise(seeds[1], (NX, NY, NZ), 1000.0, 6144.0, ((0, 8), (1, 4), (2, 16)), jnp.float32),
        "order_field": jnp.clip(1.0 * jax.random.uniform(seeds[2], (SLOTS, NX, NY, NZ), jnp.float32) ** shard_levels(seeds[2], (SLOTS, NX, NY, NZ), ((1, 8), (2, 4), (3, 16)), -0.2, 0.2), 0.0, 1.0).astype(jnp.bfloat16),
        "grain_ids": draw_grain_ids(jax.random.fold_in(seeds[4], 71), 0),
    }


OMEGA = 0.8
TAU_FINE = 256.0


def mobility_field(conc, order_field, grain_ids):
    blocks = (BRICK, BRICK, BRICK)
    summed = jnp.zeros(conc.shape, jnp.float32)
    for spatial in range(3):
        for direction in (1, -1):
            edge = blocks[spatial] - 1 if direction == 1 else 0
            source = 0 if direction == 1 else blocks[spatial] - 1
            extent = order_field.shape
            split = extent[:spatial + 1] + (extent[spatial + 1] // blocks[spatial], blocks[spatial]) + extent[spatial + 2:]
            facing = jnp.take(order_field.reshape(split), source, axis=spatial + 2).astype(jnp.float32)
            facing = jnp.roll(facing, -direction, axis=spatial + 1)
            beside_ids = jnp.roll(grain_ids, -direction, axis=spatial)
            for slot in range(SLOTS):
                matches = (grain_ids[..., slot:slot + 1] == beside_ids).astype(jnp.float32)
                remapped = jnp.zeros(facing.shape[1:], jnp.float32)
                for other in range(SLOTS):
                    weight = matches[..., other]
                    for across in range(3):
                        if across != spatial:
                            weight = jnp.repeat(weight, blocks[across], axis=across)
                    remapped = remapped + weight * facing[other]
                field = order_field[slot].astype(jnp.float32)
                shifted = jnp.roll(field, -direction, axis=spatial)
                cell_split = field.shape[:spatial] + (field.shape[spatial] // blocks[spatial], blocks[spatial]) + field.shape[spatial + 1:]
                marker = (jnp.arange(blocks[spatial]) == edge).reshape((blocks[spatial],) + (1,) * (2 - spatial))
                shifted = jnp.where(marker, jnp.expand_dims(remapped, spatial + 1), shifted.reshape(cell_split)).reshape(field.shape)
                summed = summed + (shifted - field) ** 2
    return 1.0 + 8.0 * (conc * (1.0 - conc)) ** 2 + summed


def face_coeffs(mobility):
    result = []
    for spatial in range(3):
        result.append(0.5 * (mobility + jnp.roll(mobility, -1, axis=spatial)))
        result.append(0.5 * (mobility + jnp.roll(mobility, 1, axis=spatial)))
    return tuple(result)


def apply_operator(values, coeffs, diag, step):
    summed = None
    for spatial in range(3):
        plus_cell = jnp.roll(values, -1, axis=spatial)
        minus_cell = jnp.roll(values, 1, axis=spatial)
        term = coeffs[2 * spatial] * plus_cell + coeffs[2 * spatial + 1] * minus_cell
        summed = term if summed is None else summed + term
    return diag * values - step * summed


def diagonal_of(coeffs, step):
    summed = coeffs[0]
    for coeff in coeffs[1:]:
        summed = summed + coeff
    return 1.0 + step * summed


def jacobi_sweep(values, source, coeffs, diag, step):
    if values is None:
        return OMEGA * source / diag
    return values + OMEGA * (source - apply_operator(values, coeffs, diag, step)) / diag


def restrict_field(field):
    extent = field.shape
    grouped = field.reshape(extent[0] // 2, 2, extent[1] // 2, 2, extent[2] // 2, 2)
    return jnp.mean(grouped, axis=(1, 3, 5))


def restrict_coeffs(coeffs):
    result = []
    for position, coeff in enumerate(coeffs):
        spatial = position // 2
        pick = 1 if position % 2 == 0 else 0
        extent = coeff.shape
        grouped = coeff.reshape(extent[0] // 2, 2, extent[1] // 2, 2, extent[2] // 2, 2)
        chosen = jnp.take(grouped, pick, axis=2 * spatial + 1)
        remaining = tuple(pair_axis if pair_axis < 2 * spatial + 1 else pair_axis - 1 for pair_axis in (1, 3, 5) if pair_axis != 2 * spatial + 1)
        result.append(jnp.mean(chosen, axis=remaining))
    return tuple(result)


def prolong_field(field):
    return jnp.repeat(jnp.repeat(jnp.repeat(field, 2, axis=0), 2, axis=1), 2, axis=2)


def reference(conc, right_side, order_field, grain_ids):
    mobility = mobility_field(conc, order_field, grain_ids)
    coeffs_fine = face_coeffs(mobility)
    step_fine = TAU_FINE
    diag_fine = diagonal_of(coeffs_fine, step_fine)
    solution = conc
    for sweep_index in range(SMOOTH):
        solution = jacobi_sweep(solution, right_side, coeffs_fine, diag_fine, step_fine)
    fine_residual = right_side - apply_operator(solution, coeffs_fine, diag_fine, step_fine)
    source_mid = restrict_field(fine_residual)
    coeffs_mid = restrict_coeffs(coeffs_fine)
    step_mid = TAU_FINE / 4.0
    diag_mid = diagonal_of(coeffs_mid, step_mid)
    error_mid = None
    for sweep_index in range(SMOOTH):
        error_mid = jacobi_sweep(error_mid, source_mid, coeffs_mid, diag_mid, step_mid)
    mid_residual = source_mid - apply_operator(error_mid, coeffs_mid, diag_mid, step_mid)
    source_low = restrict_field(mid_residual)
    coeffs_low = restrict_coeffs(coeffs_mid)
    step_low = TAU_FINE / 16.0
    diag_low = diagonal_of(coeffs_low, step_low)
    error_low = None
    for sweep_index in range(COARSE_SWEEPS):
        error_low = jacobi_sweep(error_low, source_low, coeffs_low, diag_low, step_low)
    error_mid = error_mid + prolong_field(error_low)
    for sweep_index in range(SMOOTH):
        error_mid = jacobi_sweep(error_mid, source_mid, coeffs_mid, diag_mid, step_mid)
    solution = solution + prolong_field(error_mid)
    for sweep_index in range(SMOOTH):
        solution = jacobi_sweep(solution, right_side, coeffs_fine, diag_fine, step_fine)
    return solution, mobility
```

```python
import functools

import jax
import jax.numpy as jnp
from jax import lax
from jax.experimental import pallas as pl
from jax.experimental.pallas import tpu as pltpu
from jax.sharding import PartitionSpec as P

SLOTS = 8
BRICK = 16
OMEGA = 0.8
TAU = 256.0
LANES = 128
RING = 256
F32 = jnp.float32
BF16 = jnp.bfloat16
HIGH = lax.Precision.HIGHEST
VMEM = pl.BlockSpec(memory_space=pltpu.VMEM)
SMEM = pl.BlockSpec(memory_space=pltpu.SMEM)
COARSE = 51
COARSE_LOW = 10
MIDDLE = 70
MIDDLE_LOW = 3


def call(kernel, outs, args, scratch=(), specs=None):
    return pl.pallas_call(
        kernel,
        out_shape=[jax.ShapeDtypeStruct(shape, dtype) for shape, dtype in outs],
        in_specs=specs or [VMEM] * len(args),
        out_specs=[VMEM] * len(outs),
        scratch_shapes=[pltpu.VMEM(shape, dtype) for shape, dtype in scratch],
        compiler_params=pltpu.CompilerParams(vmem_limit_bytes=48 << 20),
    )(*args)


def roll(x, shift, axis):
    return pltpu.roll(x, shift % x.shape[axis], axis)


def iota(shape, axis):
    return lax.broadcasted_iota(jnp.int32, shape, axis)


def dot(a, b):
    return jnp.dot(a, b, precision=HIGH, preferred_element_type=F32)


def lane_ids(ids_ref):
    ids = ids_ref[0, 0].astype(F32)
    spread = (iota((8, LANES), 1) // BRICK == iota((8, LANES), 0)).astype(F32)
    grains = lax.dot_general(
        ids, spread, (((0,), (0,)), ((), ())), precision=HIGH, preferred_element_type=F32
    )
    return jnp.floor(grains + 0.5)


def split_ids(grains):
    high = jnp.floor(grains * (1.0 / 64.0))
    return jnp.concatenate([high, grains - 64.0 * high], axis=0).astype(BF16)


def join_ids(rows):
    rows = rows.astype(F32)
    return rows[:8] * 64.0 + rows[8:]


def faces_kernel(order_ref, ids_ref, xm_ref, xp_ref, ym_ref, yp_ref, zm_ref, zp_ref):
    grains = lane_ids(ids_ref)
    packed = split_ids(grains)
    for ref in (xm_ref, xp_ref, ym_ref, yp_ref):
        ref[SLOTS] = packed
    zm_ref[16] = split_ids(jnp.broadcast_to(grains[:, 0:1], (8, LANES)))
    zp_ref[16] = split_ids(jnp.broadcast_to(grains[:, LANES - 1 :], (8, LANES)))
    lane = iota((16, LANES), 1)
    low = [jnp.zeros((16, LANES), F32)] * 16
    high = [jnp.zeros((16, LANES), F32)] * 16
    for slot in range(SLOTS):
        cells = order_ref[slot].astype(F32)
        xm_ref[slot] = order_ref[slot, 0]
        xp_ref[slot] = order_ref[slot, 15]
        ym_ref[slot] = cells[:, 0, :].astype(BF16)
        yp_ref[slot] = cells[:, 15, :].astype(BF16)
        for x in range(16):
            low[x] = jnp.where(lane == slot, cells[x, :, 0:1], low[x])
            high[x] = jnp.where(lane == slot, cells[x, :, LANES - 1 :], high[x])
    for x in range(16):
        zm_ref[x] = low[x].astype(BF16)
        zp_ref[x] = high[x].astype(BF16)


def square(x):
    return x * x


def mobility_kernel(
    conc_ref, side_ref, order_ref, ids_ref, xm_ref, xp_ref, ym_ref, yp_ref, zm_ref, zp_ref,
    own_ym_ref, own_yp_ref, mob_ref, low_ref, high_ref, work, weights,
):
    own = lane_ids(ids_ref)
    lane = iota((16, LANES), 1)
    row = iota((16, LANES), 0)
    last = lane % BRICK == BRICK - 1
    edge = last | (lane % BRICK == 0)

    lane8 = iota((8, LANES), 1)
    after = jnp.where(
        lane8 >= LANES - BRICK, join_ids(zp_ref[16]), roll(own, -BRICK, 1)
    )
    before = jnp.where(lane8 < BRICK, join_ids(zm_ref[16]), roll(own, BRICK, 1))
    beside = jnp.where(lane8 % BRICK == BRICK - 1, after, before)
    for other in range(SLOTS):
        match = (own == beside[other : other + 1]).astype(F32)
        for slot in range(SLOTS):
            weights[slot * SLOTS + other] = jnp.broadcast_to(match[slot : slot + 1], (8, LANES))

    def across(face_ref, ids, center):
        facing = [face_ref[other].astype(F32) for other in range(SLOTS)]
        total = None
        for slot in range(SLOTS):
            value = None
            for other in range(SLOTS):
                match = (own[slot : slot + 1] == ids[other : other + 1]).astype(F32)
                term = match * facing[other]
                value = term if value is None else value + term
            part = square(value - center(slot))
            total = part if total is None else total + part
        return total

    def doubled(block):
        return jnp.concatenate([block, block], axis=0)

    def plane(x, below, carry_in):
        conc = conc_ref[x]
        base = 1.0 + 8.0 * square(conc * (1.0 - conc))
        zlow = zm_ref[x].astype(F32)
        zhigh = zp_ref[x].astype(F32)
        along_y = jnp.zeros((16, LANES), F32)
        along_z = jnp.zeros((16, LANES), F32)
        along_x = jnp.zeros((16, LANES), F32)
        centers = []
        facing = []
        above = jnp.minimum(x + 1, 15)
        for slot in range(SLOTS):
            here = order_ref[slot, x].astype(F32)
            there = order_ref[slot, above].astype(F32)
            centers.append(here)
            along_x = along_x + square(there - here)
            along_y = along_y + square(roll(here, -1, 0) - here)
            right = roll(here, -1, 1)
            along_z = along_z + square(right - here)
            right = jnp.where(lane == LANES - 1, zhigh[:, slot : slot + 1], right)
            left = jnp.where(lane == 0, zlow[:, slot : slot + 1], roll(here, 1, 1))
            facing.append(jnp.where(last, right, left))
        along_y = jnp.where(row == 15, 0.0, along_y)
        along_z = jnp.where(last, 0.0, along_z)
        remapped = jnp.zeros((16, LANES), F32)
        for slot in range(SLOTS):
            value = None
            for other in range(SLOTS):
                term = doubled(weights[slot * SLOTS + other]) * facing[other]
                value = term if value is None else value + term
            remapped = remapped + square(value - centers[slot])
        total = base + along_y + roll(along_y, 1, 0) + along_z + roll(along_z, 1, 1)
        total = total + jnp.where(edge, remapped, 0.0) + along_x + carry_in
        work[x] = total
        return along_x

    lax.fori_loop(0, 16, lambda x, c: plane(x, None, c), jnp.zeros((16, LANES), F32))
    work[0] = work[0] + across(
        xm_ref, join_ids(xm_ref[SLOTS]), lambda s: order_ref[s, 0].astype(F32)
    )
    work[15] = work[15] + across(
        xp_ref, join_ids(xp_ref[SLOTS]), lambda s: order_ref[s, 15].astype(F32)
    )
    bottom = across(ym_ref, join_ids(ym_ref[SLOTS]), lambda s: own_ym_ref[s].astype(F32))
    top = across(yp_ref, join_ids(yp_ref[SLOTS]), lambda s: own_yp_ref[s].astype(F32))
    for x in range(16):
        value = work[x]
        value = value + jnp.where(row == 0, bottom[x : x + 1], 0.0)
        value = value + jnp.where(row == 15, top[x : x + 1], 0.0)
        mob_ref[x] = value
        low_ref[0, x] = value[:8]
        high_ref[0, x] = value[8:]
        low_ref[1, x] = conc_ref[x, :8]
        high_ref[1, x] = conc_ref[x, 8:]
        low_ref[2, x] = side_ref[x, :8]
        high_ref[2, x] = side_ref[x, 8:]


def rows_kernel(below_ref, low_ref, high_ref, above_ref, xl_ref, xh_ref):
    for place, ref in enumerate((below_ref, low_ref, high_ref, above_ref)):
        rows = pl.ds(8 * place, 8)
        xl_ref[:, :, rows, :] = ref[:, :8]
        xh_ref[:, :, rows, :] = ref[:, 8:]


def lanes_kernel(xm_ref, xl_ref, xh_ref, xp_ref, zm_ref, zp_ref):
    lane = iota((32, LANES), 1)
    for place, ref in enumerate((xm_ref, xl_ref, xh_ref, xp_ref)):
        for x in range(8):
            mob, conc, side = ref[0, x], ref[1, x], ref[2, x]
            zm_ref[8 * place + x] = jnp.where(
                lane < 43, mob, jnp.where(lane < 86, roll(conc, 43, 1), roll(side, 86, 1))
            )
            zp_ref[8 * place + x] = jnp.where(
                lane >= 85, mob, jnp.where(lane >= 42, roll(conc, -43, 1), roll(side, -86, 1))
            )


def partner(x, step, axis):
    upper = (iota(x.shape, axis) & step) != 0
    return jnp.where(upper, roll(x, step, axis), roll(x, -step, axis))


def pair_sum(x, step, axis):
    return x + partner(x, step, axis)


def upper_of(x, step, axis):
    upper = (iota(x.shape, axis) & step) != 0
    return jnp.where(upper, x, roll(x, -step, axis))


def residual(value, source, flux_x, flux_x_before, ky, kz, step):
    flux_y = ky * (roll(value, -step, 0) - value)
    flux_z = kz * (roll(value, -step, 1) - value)
    total = (source - value) + (flux_x - flux_x_before)
    total = total + (flux_y - roll(flux_y, step, 0))
    return total + (flux_z - roll(flux_z, step, 1))


def sweep_planes(first, last, values, source, kx, ky, kz, step, use):
    before = kx[first - 1] * (values[first] - values[first - 1])

    def plane(x, flux_before):
        value = values[x]
        flux = kx[x] * (values[x + 1] - value)
        use(x, value, residual(value, source[x], flux, flux_before, ky[x], kz[x], step))
        return flux

    lax.fori_loop(first, last + 1, plane, before)


def down_kernel(
    xm_ref, xl_ref, xh_ref, xp_ref, zm_ref, zp_ref,
    v_ref, side_ref, kx_ref, ky_ref, kz_ref, wd_ref,
    f1_ref, k1x_ref, k1y_ref, k1z_ref, wd1_ref, chunk_ref,
    mob, v0, res, e0, e1, r1,
):
    lane = iota((32, LANES), 1)
    for place, ref in enumerate((xm_ref, xl_ref, xh_ref, xp_ref)):
        for i in range(8):
            x = 8 * place + i
            up, down = zp_ref[x], zm_ref[x]
            mob[x, :, :LANES] = ref[0, i]
            mob[x, :, LANES:] = jnp.where(lane < 43, up, jnp.where(lane >= 85, down, 1.0))
            v0[x, :, :LANES] = ref[1, i]
            v0[x, :, LANES:] = jnp.where(
                lane < 43, roll(up, -43, 1), jnp.where(lane >= 85, roll(down, 43, 1), 0.0)
            )
            side_ref[x, :, :LANES] = ref[2, i]
            side_ref[x, :, LANES:] = jnp.where(
                lane < 42, roll(up, -86, 1), jnp.where(lane >= 86, roll(down, 86, 1), 0.0)
            )

    half = TAU / 2

    def face_planes(x, before):
        here = mob[x]
        kx = half * (here + mob[x + 1])
        ky = half * (here + roll(here, -1, 0))
        kz = half * (here + roll(here, -1, 1))
        kx_ref[x] = kx
        ky_ref[x] = ky
        kz_ref[x] = kz
        total = (kx + before) + (ky + roll(ky, 1, 0)) + (kz + roll(kz, 1, 1))
        wd_ref[x] = OMEGA / (1.0 + total)
        return kx

    first = half * (mob[1] + mob[2])
    kx_ref[1] = first
    lax.fori_loop(2, 30, face_planes, first)

    def smooth(target, weight):
        def use(x, value, left):
            target[x] = value + weight[x] * left

        return use

    v_ref[1] = v0[1]
    for x in (0, 2, 29, 30, 31):
        v_ref[x] = v0[x]
    sweep_planes(2, 29, v0, side_ref, kx_ref, ky_ref, kz_ref, 1, smooth(res, wd_ref))
    sweep_planes(3, 28, res, side_ref, kx_ref, ky_ref, kz_ref, 1, smooth(v_ref, wd_ref))

    def keep(x, value, left):
        res[x] = left

    sweep_planes(4, 27, v_ref, side_ref, kx_ref, ky_ref, kz_ref, 1, keep)

    def pool(x):
        return pair_sum(pair_sum(x, 1, 0), 1, 1)

    for i in range(1, 14):
        x = 2 * i
        k1x_ref[i] = pool(kx_ref[x + 1]) * (1.0 / 16.0)
        if i == 1:
            continue
        f1_ref[i] = pool(res[x] + res[x + 1]) * 0.125
        along_y = pair_sum(ky_ref[x] + ky_ref[x + 1], 1, 1)
        k1y = upper_of(along_y, 1, 0) * (1.0 / 16.0)
        along_z = pair_sum(kz_ref[x] + kz_ref[x + 1], 1, 0)
        k1z = upper_of(along_z, 1, 1) * (1.0 / 16.0)
        k1y_ref[i] = k1y
        k1z_ref[i] = k1z
        total = (k1x_ref[i] + k1x_ref[i - 1]) + (k1y + roll(k1y, 2, 0)) + (k1z + roll(k1z, 2, 1))
        weight = OMEGA / (1.0 + total)
        wd1_ref[i] = weight
        e0[i] = weight * f1_ref[i]
    for ref in (f1_ref, k1x_ref, k1y_ref, k1z_ref, wd1_ref):
        for i in (0, 1, 14, 15):
            if i != 1 or ref is not k1x_ref:
                ref[i] = jnp.zeros((32, RING), F32)

    sweep_planes(3, 12, e0, f1_ref, k1x_ref, k1y_ref, k1z_ref, 2, smooth(e1, wd1_ref))

    def keep_middle(x, value, left):
        r1[x] = left

    sweep_planes(4, 11, e1, f1_ref, k1x_ref, k1y_ref, k1z_ref, 2, keep_middle)

    src = iota((RING, LANES), 0)
    dst = iota((RING, LANES), 1)
    cell = jnp.where(src < 192, src, src - RING)
    pick_low = (cell == 4 * (dst - COARSE_LOW)) & (dst < COARSE)
    pick_high = (cell == 4 * (dst - 64 - COARSE_LOW)) & (dst >= 64) & (dst < 64 + COARSE)
    pick_low = pick_low.astype(F32)
    pick_high = pick_high.astype(F32)
    pick_middle = ((cell == 2 * (dst - MIDDLE_LOW)) & (dst < MIDDLE)).astype(F32)
    for j in range(4):
        i = 4 + 2 * j
        f2 = pair_sum(pair_sum(r1[i] + r1[i + 1], 2, 0), 2, 1) * 0.125
        k2x = pair_sum(pair_sum(k1x_ref[i + 1], 2, 0), 2, 1) * (1.0 / 16.0)
        k2y = pair_sum(k1y_ref[i] + k1y_ref[i + 1], 2, 1)
        k2y = upper_of(k2y, 2, 0) * (1.0 / 16.0)
        k2z = pair_sum(k1z_ref[i] + k1z_ref[i + 1], 2, 0)
        k2z = upper_of(k2z, 2, 1) * (1.0 / 16.0)
        first = dot(f2, pick_low) + dot(k2x, pick_high)
        second = dot(k2y, pick_low) + dot(k2z, pick_high)
        for k in range(4):
            line = pl.ds(8 + 4 * k, 1)
            chunk_ref[0, pl.ds(4 * j + k, 1), :] = first[8 + 4 * k : 9 + 4 * k]
            chunk_ref[0, pl.ds(16 + 4 * j + k, 1), :] = second[8 + 4 * k : 9 + 4 * k]
    for i in range(8):
        middle = dot(e1[4 + i], pick_middle)
        for k in range(8):
            chunk_ref[0, pl.ds(32 + 8 * i + k, 1), :] = middle[8 + 2 * k : 9 + 2 * k]
    for k in range(1, 32):
        chunk_ref[k] = chunk_ref[0]


def up_kernel(
    place_ref, all_ref, v_ref, side_ref, kx_ref, ky_ref, kz_ref, wd_ref,
    f1_ref, k1x_ref, k1y_ref, k1z_ref, wd1_ref,
    out_ref,
    pair0, pair1, c2x, c2y, c2z, wd2, f2, ea, eb, mid, e1a, e1b, va, vb,
):
    gx = place_ref[0]
    gy = place_ref[1]

    def source(dx, dy):
        return ((gx + dx + 8) & 7) * 4 + ((gy + dy + 4) & 3)

    for p in range(8):
        for q in range(4):
            s = source(p - 1, q - 1)
            for i in range(4):
                pair0[4 * p + i, pl.ds(4 * q, 4), :] = all_ref[s, pl.ds(4 * i, 4), :]
                pair1[4 * p + i, pl.ds(4 * q, 4), :] = all_ref[s, pl.ds(16 + 4 * i, 4), :]
    for p in (-1, 0, 1):
        for q in (-1, 0, 1):
            s = source(p, q)
            for i in range(16):
                if (i - 4) // 8 != p or not 1 <= i <= 14:
                    continue
                start = 32 + 8 * ((i - 4) % 8)
                if q == -1:
                    mid[i, pl.ds(0, 4), :] = all_ref[s, pl.ds(start + 4, 4), :]
                elif q == 0:
                    mid[i, pl.ds(4, 8), :] = all_ref[s, pl.ds(start, 8), :]
                else:
                    mid[i, pl.ds(12, 4), :] = all_ref[s, pl.ds(start, 4), :]

    used = iota((16, LANES), 1) < COARSE
    for x in range(32):
        first = pair0[x]
        second = pair1[x]
        f2[x] = jnp.where(used, first, 0.0)
        c2x[x] = jnp.where(used, roll(first, 64, 1), 0.0)
        c2y[x] = jnp.where(used, second, 0.0)
        c2z[x] = jnp.where(used, roll(second, 64, 1), 0.0)
    for x in range(32):
        ky = c2y[x]
        kz = c2z[x]
        total = (c2x[x] + c2x[(x + 31) % 32]) + (ky + roll(ky, 1, 0)) + (kz + roll(kz, 1, 1))
        weight = OMEGA / (1.0 + total)
        wd2[x] = weight
        ea[x] = weight * f2[x]

    def coarse_sweep(old, new):
        before = c2x[31] * (old[0] - old[31])
        for x in range(32):
            value = old[x]
            flux = c2x[x] * (old[(x + 1) % 32] - value)
            left = residual(value, f2[x], flux, before, c2y[x], c2z[x], 1)
            new[x] = value + wd2[x] * left
            before = flux

    def two(_, c):
        coarse_sweep(ea, eb)
        coarse_sweep(eb, ea)
        return c

    lax.fori_loop(0, 3, two, 0)
    coarse_sweep(ea, eb)

    src = iota((LANES, RING), 0)
    dst = iota((LANES, RING), 1)
    cell = jnp.where(dst < 192, dst, dst - RING)
    spread2 = ((cell + 4 * COARSE_LOW) // 4 == src) & (src < COARSE) & (cell >= -4 * COARSE_LOW)
    spread2 = spread2.astype(F32)
    spread1 = ((cell + 2 * MIDDLE_LOW) // 2 == src) & (src < MIDDLE) & (cell >= -2 * MIDDLE_LOW)
    spread1 = spread1.astype(F32)
    line = iota((32, 16), 0)
    pick = iota((32, 16), 1)
    rows2 = (line // 4 + 2 == pick).astype(F32)
    rows1 = (line // 2 == pick).astype(F32)
    for j in range(8):
        coarse = dot(rows2, dot(eb[2 + j], spread2))
        for i in (2 * j, 2 * j + 1):
            if 1 <= i <= 14:
                e1a[i] = coarse + dot(rows1, dot(mid[i], spread1))

    def smooth(target, weight):
        def use(x, value, left):
            target[x] = value + weight[x] * left

        return use

    sweep_planes(2, 13, e1a, f1_ref, k1x_ref, k1y_ref, k1z_ref, 2, smooth(e1b, wd1_ref))
    sweep_planes(3, 12, e1b, f1_ref, k1x_ref, k1y_ref, k1z_ref, 2, smooth(e1a, wd1_ref))
    for x in range(6, 26):
        va[x] = v_ref[x] + e1a[x // 2]
    sweep_planes(7, 24, va, side_ref, kx_ref, ky_ref, kz_ref, 1, smooth(vb, wd_ref))

    def finish(x, value, left):
        new = value + wd_ref[x] * left
        out_ref[x - 8] = new[8:24, :LANES]

    sweep_planes(8, 23, vb, side_ref, kx_ref, ky_ref, kz_ref, 1, finish)


def shift(x, axis, direction):
    count = lax.axis_size(axis)
    return lax.ppermute(x, axis, [(i, (i + direction) % count) for i in range(count)])


def body(conc, right_side, order_field, grain_ids):
    face = ((9, 16, LANES), BF16)
    zface = ((17, 16, LANES), BF16)
    xm, xp, ym, yp, zm, zp = call(
        faces_kernel, [face] * 4 + [zface] * 2, (order_field, grain_ids)
    )
    faces = (
        shift(xp, "gx", 1), shift(xm, "gx", -1),
        shift(yp, "gy", 1), shift(ym, "gy", -1),
        shift(zp, "gz", 1), shift(zm, "gz", -1),
    )
    half = ((3, 16, 8, LANES), F32)
    mobility, low, high = call(
        mobility_kernel,
        [((16, 16, LANES), F32), half, half],
        (conc, right_side, order_field, grain_ids) + faces + (ym, yp),
        scratch=[((16, 16, LANES), F32), ((64, 8, LANES), F32)],
    )
    below = shift(high, "gy", 1)
    above = shift(low, "gy", -1)
    slab = ((3, 8, 32, LANES), F32)
    xl, xh = call(rows_kernel, [slab, slab], (below, low, high, above))
    before = shift(xh, "gx", 1)
    after = shift(xl, "gx", -1)
    wide = ((32, 32, LANES), F32)
    sm, sp = call(lanes_kernel, [wide, wide], (before, xl, xh, after))
    left = shift(sp, "gz", 1)
    right = shift(sm, "gz", -1)
    fine = ((32, 32, RING), F32)
    middle = ((16, 32, RING), F32)
    results = call(
        down_kernel,
        [fine] * 6 + [middle] * 5 + [((32, 96, LANES), F32)],
        (before, xl, xh, after, left, right),
        scratch=[fine] * 3 + [middle] * 3,
    )
    chunks = lax.all_to_all(results[-1], ("gx", "gy"), 0, 0, tiled=True)
    place = jnp.stack([lax.axis_index("gx"), lax.axis_index("gy")]).astype(jnp.int32)
    plane = ((32, 16, LANES), F32)
    (out,) = call(
        up_kernel,
        [((16, 16, LANES), F32)],
        (place, chunks) + tuple(results[:-1]),
        scratch=[plane] * 9 + [((16, 16, LANES), F32)] + [middle] * 2 + [fine] * 2,
        specs=[SMEM] + [VMEM] * 12,
    )
    return out, mobility


def solution(mesh):
    return jax.shard_map(
        body,
        mesh=mesh,
        in_specs=(
            P("gx", "gy", "gz"),
            P("gx", "gy", "gz"),
            P(None, "gx", "gy", "gz"),
            P("gx", "gy", "gz", None),
        ),
        out_specs=(P("gx", "gy", "gz"), P("gx", "gy", "gz")),
        check_vma=False,
    )
```

```python
import functools

import jax
import jax.numpy as jnp
from jax import lax
from jax.experimental import pallas as pl
from jax.experimental.pallas import tpu as pltpu
from jax.sharding import PartitionSpec as P

SLOTS = 8
BRICK = 16
OMEGA = 0.8
TAU = 256.0
LANES = 128
RING = 256
F32 = jnp.float32
BF16 = jnp.bfloat16
HIGH = lax.Precision.HIGHEST
VMEM = pl.BlockSpec(memory_space=pltpu.VMEM)
HBM = pl.BlockSpec(memory_space=pltpu.MemorySpace.HBM)
SMEM = pl.BlockSpec(memory_space=pltpu.SMEM)
COARSE = 51
COARSE_LOW = 10
MIDDLE = 70
MIDDLE_LOW = 3
FINE_PLANES = pl.ds(6, 20)
MIDDLE_PLANES = pl.ds(1, 13)


def call(kernel, outs, args, scratch=(), specs=None, places=None, limit=16, semaphores=0):
    specs = specs or [VMEM] * len(args)
    places = places or [VMEM] * len(outs)
    args = [
        pltpu.with_memory_space_constraint(arg, pltpu.MemorySpace.HBM) if spec is HBM else arg
        for arg, spec in zip(args, specs)
    ]
    scratches = [pltpu.VMEM(shape, dtype) for shape, dtype in scratch]
    if semaphores:
        scratches.append(pltpu.SemaphoreType.DMA((semaphores,)))
    return pl.pallas_call(
        kernel,
        out_shape=[
            pltpu.MemorySpace.HBM(*out) if place is HBM else jax.ShapeDtypeStruct(*out)
            for out, place in zip(outs, places)
        ],
        in_specs=specs,
        out_specs=places,
        scratch_shapes=scratches,
        compiler_params=pltpu.CompilerParams(vmem_limit_bytes=limit << 20),
    )(*args)


def roll(x, shift, axis):
    return pltpu.roll(x, shift % x.shape[axis], axis)


def iota(shape, axis):
    return lax.broadcasted_iota(jnp.int32, shape, axis)


def select_dot(a, picks):
    picks = picks.astype(BF16)
    total = None
    for _ in range(3):
        part = a.astype(BF16)
        a = a - part.astype(F32)
        term = jnp.dot(part, picks, preferred_element_type=F32)
        total = term if total is None else total + term
    return total


def lane_ids(ids_ref):
    ids = ids_ref[0, 0].astype(F32)
    spread = (iota((8, LANES), 1) // BRICK == iota((8, LANES), 0)).astype(F32)
    grains = lax.dot_general(
        ids, spread, (((0,), (0,)), ((), ())), precision=HIGH, preferred_element_type=F32
    )
    return jnp.floor(grains + 0.5)


def split_ids(grains):
    high = jnp.floor(grains * (1.0 / 64.0))
    return jnp.concatenate([high, grains - 64.0 * high], axis=0).astype(BF16)


def join_ids(rows):
    rows = rows.astype(F32)
    return rows[:8] * 64.0 + rows[8:]


def faces_kernel(
    conc_in, side_in, order_in, ids_in,
    conc_ref, side_ref, order_ref, ids_ref, xm_ref, xp_ref, ym_ref, yp_ref, zm_ref, zp_ref, sems,
):
    pairs = (
        (ids_in, ids_ref), (order_in, order_ref), (conc_in, conc_ref), (side_in, side_ref),
    )
    copies = [pltpu.make_async_copy(a, b, sems.at[k]) for k, (a, b) in enumerate(pairs)]
    for copy in copies:
        copy.start()
    copies[0].wait()
    copies[1].wait()
    grains = lane_ids(ids_ref)
    packed = split_ids(grains)
    for ref in (xm_ref, xp_ref, ym_ref, yp_ref):
        ref[SLOTS] = packed
    zm_ref[16] = split_ids(jnp.broadcast_to(grains[:, 0:1], (8, LANES)))
    zp_ref[16] = split_ids(jnp.broadcast_to(grains[:, LANES - 1 :], (8, LANES)))
    lane = iota((16, LANES), 1)
    low = [jnp.zeros((16, LANES), F32)] * 16
    high = [jnp.zeros((16, LANES), F32)] * 16
    for slot in range(SLOTS):
        cells = order_ref[slot].astype(F32)
        xm_ref[slot] = order_ref[slot, 0]
        xp_ref[slot] = order_ref[slot, 15]
        ym_ref[slot] = cells[:, 0, :].astype(BF16)
        yp_ref[slot] = cells[:, 15, :].astype(BF16)
        for x in range(16):
            low[x] = jnp.where(lane == slot, cells[x, :, 0:1], low[x])
            high[x] = jnp.where(lane == slot, cells[x, :, LANES - 1 :], high[x])
    for x in range(16):
        zm_ref[x] = low[x].astype(BF16)
        zp_ref[x] = high[x].astype(BF16)
    copies[2].wait()
    copies[3].wait()


def square(x):
    return x * x


def mobility_kernel(
    conc_ref, side_ref, order_ref, ids_ref, xm_ref, xp_ref, ym_ref, yp_ref, zm_ref, zp_ref,
    own_ym_ref, own_yp_ref, mob_ref, keep_ref, zm_out, zp_out, work, weights,
):
    own = lane_ids(ids_ref)
    lane = iota((16, LANES), 1)
    row = iota((16, LANES), 0)
    last = lane % BRICK == BRICK - 1
    edge = last | (lane % BRICK == 0)

    lane8 = iota((8, LANES), 1)
    after = jnp.where(
        lane8 >= LANES - BRICK, join_ids(zp_ref[16]), roll(own, -BRICK, 1)
    )
    before = jnp.where(lane8 < BRICK, join_ids(zm_ref[16]), roll(own, BRICK, 1))
    beside = jnp.where(lane8 % BRICK == BRICK - 1, after, before)
    for other in range(SLOTS):
        match = (own == beside[other : other + 1]).astype(F32)
        for slot in range(SLOTS):
            weights[slot * SLOTS + other] = jnp.broadcast_to(match[slot : slot + 1], (8, LANES))

    def across(face_ref, ids, center):
        facing = [face_ref[other].astype(F32) for other in range(SLOTS)]
        total = None
        for slot in range(SLOTS):
            value = None
            for other in range(SLOTS):
                match = (own[slot : slot + 1] == ids[other : other + 1]).astype(F32)
                term = match * facing[other]
                value = term if value is None else value + term
            part = square(value - center(slot))
            total = part if total is None else total + part
        return total

    def doubled(block):
        return jnp.concatenate([block, block], axis=0)

    def plane(x, carry_in):
        conc = conc_ref[x]
        base = 1.0 + 8.0 * square(conc * (1.0 - conc))
        zlow = zm_ref[x].astype(F32)
        zhigh = zp_ref[x].astype(F32)
        along_y = jnp.zeros((16, LANES), F32)
        along_z = jnp.zeros((16, LANES), F32)
        along_x = jnp.zeros((16, LANES), F32)
        centers = []
        facing = []
        above = min(x + 1, 15)
        for slot in range(SLOTS):
            here = order_ref[slot, x].astype(F32)
            there = order_ref[slot, above].astype(F32)
            centers.append(here)
            along_x = along_x + square(there - here)
            along_y = along_y + square(roll(here, -1, 0) - here)
            right = roll(here, -1, 1)
            along_z = along_z + square(right - here)
            right = jnp.where(lane == LANES - 1, zhigh[:, slot : slot + 1], right)
            left = jnp.where(lane == 0, zlow[:, slot : slot + 1], roll(here, 1, 1))
            facing.append(jnp.where(last, right, left))
        along_y = jnp.where(row == 15, 0.0, along_y)
        along_z = jnp.where(last, 0.0, along_z)
        remapped = jnp.zeros((16, LANES), F32)
        for slot in range(SLOTS):
            value = None
            for other in range(SLOTS):
                term = doubled(weights[slot * SLOTS + other]) * facing[other]
                value = term if value is None else value + term
            remapped = remapped + square(value - centers[slot])
        total = base + along_y + roll(along_y, 1, 0) + along_z + roll(along_z, 1, 1)
        total = total + jnp.where(edge, remapped, 0.0) + along_x + carry_in
        work[x] = total
        return along_x

    carry = jnp.zeros((16, LANES), F32)
    for x in range(16):
        carry = plane(x, carry)
    work[0] = work[0] + across(
        xm_ref, join_ids(xm_ref[SLOTS]), lambda s: order_ref[s, 0].astype(F32)
    )
    work[15] = work[15] + across(
        xp_ref, join_ids(xp_ref[SLOTS]), lambda s: order_ref[s, 15].astype(F32)
    )
    bottom = across(ym_ref, join_ids(ym_ref[SLOTS]), lambda s: own_ym_ref[s].astype(F32))
    top = across(yp_ref, join_ids(yp_ref[SLOTS]), lambda s: own_yp_ref[s].astype(F32))
    for x in range(16):
        value = work[x]
        value = value + jnp.where(row == 0, bottom[x : x + 1], 0.0)
        value = value + jnp.where(row == 15, top[x : x + 1], 0.0)
        mob_ref[x] = value
        keep_ref[x] = value
        conc, side = conc_ref[x], side_ref[x]
        zm_out[x] = jnp.where(
            lane < 43, value, jnp.where(lane < 86, roll(conc, 43, 1), roll(side, 86, 1))
        )
        zp_out[x] = jnp.where(
            lane >= 85, value, jnp.where(lane >= 42, roll(conc, -43, 1), roll(side, -86, 1))
        )


def split_kernel(mob_ref, conc_ref, side_ref, zm_ref, zp_ref, low_ref, high_ref):
    for place, ref in enumerate((mob_ref, conc_ref, side_ref, zm_ref, zp_ref)):
        low_ref[place] = ref[:, :8]
        high_ref[place] = ref[:, 8:]


def rows_kernel(below_ref, low_ref, high_ref, above_ref, xl_ref, xh_ref):
    for place, ref in enumerate((below_ref, low_ref, high_ref, above_ref)):
        rows = pl.ds(8 * place, 8)
        xl_ref[:, :, rows, :] = ref[:, :8]
        xh_ref[:, :, rows, :] = ref[:, 8:]


def partner(x, step, axis):
    upper = (iota(x.shape, axis) & step) != 0
    return jnp.where(upper, roll(x, step, axis), roll(x, -step, axis))


def pair_sum(x, step, axis):
    return x + partner(x, step, axis)


def upper_of(x, step, axis):
    upper = (iota(x.shape, axis) & step) != 0
    return jnp.where(upper, x, roll(x, -step, axis))


def residual(value, source, flux_x, flux_x_before, ky, kz, step):
    flux_y = ky * (roll(value, -step, 0) - value)
    flux_z = kz * (roll(value, -step, 1) - value)
    total = (source - value) + (flux_x - flux_x_before)
    total = total + (flux_y - roll(flux_y, step, 0))
    return total + (flux_z - roll(flux_z, step, 1))


def sweep_planes(first, last, values, source, kx, ky, kz, step, use):
    before = kx[first - 1] * (values[first] - values[first - 1])

    value = values[first]
    for x in range(first, last + 1):
        above = values[x + 1]
        flux = kx[x] * (above - value)
        use(x, value, residual(value, source[x], flux, before, ky[x], kz[x], step))
        before = flux
        value = above


def down_kernel(
    xm_ref, xl_ref, xh_ref, xp_ref,
    own_ref, chunk_ref, side_out, kx_out, ky_out, kz_out, wd_out, v_out,
    k1x_out, k1y_out, k1z_out, wd1_out, f1_out,
    mob, v0, res, v_ref, side_ref, kx_ref, ky_ref, kz_ref, wd_ref,
    f1_ref, k1x_ref, k1y_ref, k1z_ref, wd1_ref, e0, e1, r1, rows, sems,
):
    copies = []

    def store(source, target, planes):
        copy = pltpu.make_async_copy(source.at[planes], target.at[planes], sems.at[len(copies)])
        copy.start()
        copies.append(copy)

    lane = iota((32, LANES), 1)
    for place, ref in enumerate((xm_ref, xl_ref, xh_ref, xp_ref)):
        for i in range(8):
            x = 8 * place + i
            down, up = ref[3, i], ref[4, i]
            mob[x, :, :LANES] = ref[0, i]
            mob[x, :, LANES:] = jnp.where(lane < 43, up, jnp.where(lane >= 85, down, 1.0))
            v0[x, :, :LANES] = ref[1, i]
            v0[x, :, LANES:] = jnp.where(
                lane < 43, roll(up, -43, 1), jnp.where(lane >= 85, roll(down, 43, 1), 0.0)
            )
            side_ref[x, :, :LANES] = ref[2, i]
            side_ref[x, :, LANES:] = jnp.where(
                lane < 42, roll(up, -86, 1), jnp.where(lane >= 86, roll(down, 86, 1), 0.0)
            )

    half = TAU / 2

    before = half * (mob[1] + mob[2])
    kx_ref[1] = before
    for x in range(2, 30):
        here = mob[x]
        kx = half * (here + mob[x + 1])
        ky = half * (here + roll(here, -1, 0))
        kz = half * (here + roll(here, -1, 1))
        kx_ref[x] = kx
        ky_ref[x] = ky
        kz_ref[x] = kz
        total = (kx + before) + (ky + roll(ky, 1, 0)) + (kz + roll(kz, 1, 1))
        wd_ref[x] = OMEGA / (1.0 + total)
        before = kx

    store(side_ref, side_out, FINE_PLANES)
    store(kx_ref, kx_out, FINE_PLANES)
    store(ky_ref, ky_out, FINE_PLANES)
    store(kz_ref, kz_out, FINE_PLANES)
    store(wd_ref, wd_out, FINE_PLANES)

    def smooth(target, weight):
        def use(x, value, left):
            target[x] = value + weight[x] * left

        return use

    sweep_planes(2, 29, v0, side_ref, kx_ref, ky_ref, kz_ref, 1, smooth(res, wd_ref))
    sweep_planes(3, 28, res, side_ref, kx_ref, ky_ref, kz_ref, 1, smooth(v_ref, wd_ref))

    store(v_ref, v_out, FINE_PLANES)

    def keep(x, value, left):
        res[x] = left

    sweep_planes(4, 27, v_ref, side_ref, kx_ref, ky_ref, kz_ref, 1, keep)

    def pool(x):
        return pair_sum(pair_sum(x, 1, 0), 1, 1)

    for i in range(1, 14):
        x = 2 * i
        k1x_ref[i] = pool(kx_ref[x + 1]) * (1.0 / 16.0)
        if i == 1:
            for ref in (f1_ref, k1y_ref, k1z_ref, wd1_ref):
                ref[i] = jnp.zeros((32, RING), F32)
            continue
        f1_ref[i] = pool(res[x] + res[x + 1]) * 0.125
        along_y = pair_sum(ky_ref[x] + ky_ref[x + 1], 1, 1)
        k1y = upper_of(along_y, 1, 0) * (1.0 / 16.0)
        along_z = pair_sum(kz_ref[x] + kz_ref[x + 1], 1, 0)
        k1z = upper_of(along_z, 1, 1) * (1.0 / 16.0)
        k1y_ref[i] = k1y
        k1z_ref[i] = k1z
        total = (k1x_ref[i] + k1x_ref[i - 1]) + (k1y + roll(k1y, 2, 0)) + (k1z + roll(k1z, 2, 1))
        weight = OMEGA / (1.0 + total)
        wd1_ref[i] = weight
        e0[i] = weight * f1_ref[i]
    store(k1x_ref, k1x_out, MIDDLE_PLANES)
    store(k1y_ref, k1y_out, MIDDLE_PLANES)
    store(k1z_ref, k1z_out, MIDDLE_PLANES)
    store(wd1_ref, wd1_out, MIDDLE_PLANES)
    store(f1_ref, f1_out, MIDDLE_PLANES)
    sweep_planes(3, 12, e0, f1_ref, k1x_ref, k1y_ref, k1z_ref, 2, smooth(e1, wd1_ref))

    def keep_middle(x, value, left):
        r1[x] = left

    sweep_planes(4, 11, e1, f1_ref, k1x_ref, k1y_ref, k1z_ref, 2, keep_middle)

    src = iota((RING, LANES), 0)
    dst = iota((RING, LANES), 1)
    cell = jnp.where(src < 192, src, src - RING)
    pick_low = (cell == 4 * (dst - COARSE_LOW)) & (dst < COARSE)
    pick_high = (cell == 4 * (dst - 64 - COARSE_LOW)) & (dst >= 64) & (dst < 64 + COARSE)
    picks = jnp.concatenate([pick_low.astype(F32), pick_high.astype(F32)], axis=0)
    pick_middle = ((cell == 2 * (dst - MIDDLE_LOW)) & (dst < MIDDLE)).astype(F32)
    firsts = []
    seconds = []
    for j in range(4):
        i = 4 + 2 * j
        f2 = pair_sum(pair_sum(r1[i] + r1[i + 1], 2, 0), 2, 1) * 0.125
        k2x = pair_sum(pair_sum(k1x_ref[i + 1], 2, 0), 2, 1) * (1.0 / 16.0)
        k2y = pair_sum(k1y_ref[i] + k1y_ref[i + 1], 2, 1)
        k2y = upper_of(k2y, 2, 0) * (1.0 / 16.0)
        k2z = pair_sum(k1z_ref[i] + k1z_ref[i + 1], 2, 0)
        k2z = upper_of(k2z, 2, 1) * (1.0 / 16.0)
        firsts.append(jnp.concatenate([f2[8:24], k2x[8:24]], axis=1))
        seconds.append(jnp.concatenate([k2y[8:24], k2z[8:24]], axis=1))
    rows[...] = select_dot(jnp.concatenate(firsts + seconds, axis=0), picks)
    coarse = rows[pl.ds(0, 32, stride=4), :]
    rows[...] = select_dot(
        jnp.concatenate([e1[4 + i, 8:24] for i in range(8)], axis=0), pick_middle
    )
    middle = rows[pl.ds(0, 64, stride=2), :]
    own_ref[...] = middle
    high = coarse.astype(BF16)
    chunk = jnp.concatenate(
        [high, (coarse - high.astype(F32)).astype(BF16), middle.astype(BF16)], axis=0
    )
    for k in range(32):
        chunk_ref[k] = chunk
    for copy in copies:
        copy.wait()


def up_kernel(
    place_ref, all_ref, own_ref, side_in, kx_in, ky_in, kz_in, wd_in, v_in,
    k1x_in, k1y_in, k1z_in, wd1_in, f1_in,
    out_ref,
    side_ref, kx_ref, ky_ref, kz_ref, wd_ref, v_ref, k1x_ref, k1y_ref, k1z_ref, wd1_ref, f1_ref,
    pair0, pair1, c2x, c2y, c2z, wd2, f2, ea, eb, mid, tall, lean, e1a, e1b, va, vb, sems,
):
    copies = []
    for planes, moves in (
        (MIDDLE_PLANES, (
            (k1x_in, k1x_ref), (k1y_in, k1y_ref), (k1z_in, k1z_ref), (wd1_in, wd1_ref),
            (f1_in, f1_ref),
        )),
        (FINE_PLANES, (
            (v_in, v_ref), (side_in, side_ref), (kx_in, kx_ref), (ky_in, ky_ref),
            (kz_in, kz_ref), (wd_in, wd_ref),
        )),
    ):
        for a, b in moves:
            copies.append(
                pltpu.make_async_copy(a.at[planes], b.at[planes], sems.at[len(copies)])
            )
    for copy in copies:
        copy.start()
    gx = place_ref[0]
    gy = place_ref[1]

    def source(dx, dy):
        return ((gx + dx + 8) & 7) * 4 + ((gy + dy + 4) & 3)

    for p in range(8):
        for q in range(4):
            s = source(p - 1, q - 1)
            cells = all_ref[s, pl.ds(0, 32), :].astype(F32)
            cells = cells + all_ref[s, pl.ds(32, 32), :].astype(F32)
            for i in range(4):
                pair0[4 * p + i, pl.ds(4 * q, 4), :] = cells[4 * i : 4 * i + 4]
                pair1[4 * p + i, pl.ds(4 * q, 4), :] = cells[16 + 4 * i : 20 + 4 * i]
    for p in (-1, 0, 1):
        for q in (-1, 0, 1):
            if p == 0 and q == 0:
                cells = own_ref[...]
            else:
                cells = all_ref[source(p, q), pl.ds(64, 64), :].astype(F32)
            for i in range(1, 15):
                if (i - 4) // 8 != p:
                    continue
                start = 8 * ((i - 4) % 8)
                block = cells[start : start + 8]
                if q == -1:
                    mid[i, pl.ds(0, 4), :] = block[4:]
                elif q == 0:
                    mid[i, pl.ds(4, 8), :] = block
                else:
                    mid[i, pl.ds(12, 4), :] = block[:4]

    used = iota((16, LANES), 1) < COARSE
    for x in range(32):
        first = pair0[x]
        second = pair1[x]
        f2[x] = jnp.where(used, first, 0.0)
        c2x[x] = jnp.where(used, roll(first, 64, 1), 0.0)
        c2y[x] = jnp.where(used, second, 0.0)
        c2z[x] = jnp.where(used, roll(second, 64, 1), 0.0)
    for x in range(32):
        ky = c2y[x]
        kz = c2z[x]
        total = (c2x[x] + c2x[(x + 31) % 32]) + (ky + roll(ky, 1, 0)) + (kz + roll(kz, 1, 1))
        weight = OMEGA / (1.0 + total)
        wd2[x] = weight
        ea[x] = weight * f2[x]

    def coarse_sweep(old, new):
        before = c2x[31] * (old[0] - old[31])
        for x in range(32):
            value = old[x]
            flux = c2x[x] * (old[(x + 1) % 32] - value)
            left = residual(value, f2[x], flux, before, c2y[x], c2z[x], 1)
            new[x] = value + wd2[x] * left
            before = flux

    def two(_, c):
        coarse_sweep(ea, eb)
        coarse_sweep(eb, ea)
        return c

    lax.fori_loop(0, 3, two, 0)
    coarse_sweep(ea, eb)

    lane = iota((8, LANES), 1)
    for j in range(8):
        line = roll(eb[2 + j, pl.ds(2, 8), :], MIDDLE, 1)
        line = jnp.where((lane >= MIDDLE) & (lane < MIDDLE + COARSE), line, 0.0)
        for k in range(4):
            lean[j, pl.ds(k, 8, stride=4), :] = line
    for i in range(1, 15):
        line = mid[i]
        for k in range(2):
            tall[i, pl.ds(k, 16, stride=2), :] = line
    src = iota((LANES, RING), 0)
    dst = iota((LANES, RING), 1)
    cell = jnp.where(dst < 192, dst, dst - RING)
    middle = (cell >= -2 * MIDDLE_LOW) & (src < MIDDLE)
    middle = middle & ((cell + 2 * MIDDLE_LOW) // 2 == src)
    coarse = (cell >= -4 * COARSE_LOW) & (src >= MIDDLE) & (src < MIDDLE + COARSE)
    coarse = coarse & ((cell + 4 * COARSE_LOW) // 4 == src - MIDDLE)
    spread = (middle | coarse).astype(F32)
    narrow = iota((32, LANES), 1) < MIDDLE
    packed = [jnp.where(narrow, tall[i], lean[i // 2]) for i in range(1, 15)]
    widened = select_dot(jnp.concatenate(packed, axis=0), spread)
    for i in range(1, 15):
        e1a[i] = widened[32 * (i - 1) : 32 * i]

    def smooth(target, weight):
        def use(x, value, left):
            target[x] = value + weight[x] * left

        return use

    for copy in copies:
        copy.wait()
    sweep_planes(2, 13, e1a, f1_ref, k1x_ref, k1y_ref, k1z_ref, 2, smooth(e1b, wd1_ref))
    sweep_planes(3, 12, e1b, f1_ref, k1x_ref, k1y_ref, k1z_ref, 2, smooth(e1a, wd1_ref))
    for x in range(6, 26):
        va[x] = v_ref[x] + e1a[x // 2]
    sweep_planes(7, 24, va, side_ref, kx_ref, ky_ref, kz_ref, 1, smooth(vb, wd_ref))

    def finish(x, value, left):
        new = value + wd_ref[x] * left
        out_ref[x - 8] = new[8:24, :LANES]

    sweep_planes(8, 23, vb, side_ref, kx_ref, ky_ref, kz_ref, 1, finish)


def shift(x, axis, direction):
    count = lax.axis_size(axis)
    return lax.ppermute(x, axis, [(i, (i + direction) % count) for i in range(count)])


def body(conc, right_side, order_field, grain_ids):
    face = ((9, 16, LANES), BF16)
    zface = ((17, 16, LANES), BF16)
    brick = ((16, 16, LANES), F32)
    conc, side, order, ids, xm, xp, ym, yp, zm, zp = call(
        faces_kernel,
        [brick, brick, ((8, 16, 16, LANES), BF16), ((1, 1, 8, 8), jnp.int32)]
        + [face] * 4
        + [zface] * 2,
        (conc, right_side, order_field, grain_ids),
        specs=[HBM] * 4,
        semaphores=4,
    )
    faces = (
        shift(xp, "gx", 1), shift(xm, "gx", -1),
        shift(yp, "gy", 1), shift(ym, "gy", -1),
        shift(zp, "gz", 1), shift(zm, "gz", -1),
    )
    mobility, keep, zm, zp = call(
        mobility_kernel,
        [brick] * 4,
        (conc, side, order, ids) + faces + (ym, yp),
        scratch=[brick, ((64, 8, LANES), F32)],
    )
    left = shift(zp, "gz", 1)
    right = shift(zm, "gz", -1)
    half = ((5, 16, 8, LANES), F32)
    low, high = call(split_kernel, [half, half], (keep, conc, side, left, right))
    below = shift(high, "gy", 1)
    above = shift(low, "gy", -1)
    slab = ((5, 8, 32, LANES), F32)
    xl, xh = call(rows_kernel, [slab, slab], (below, low, high, above))
    before = shift(xh, "gx", 1)
    after = shift(xl, "gx", -1)
    fine = ((32, 32, RING), F32)
    middle = ((16, 32, RING), F32)
    own, chunk, *kept = call(
        down_kernel,
        [((64, LANES), F32), ((32, LANES, LANES), BF16)] + [fine] * 6 + [middle] * 5,
        (before, xl, xh, after),
        scratch=[fine] * 9 + [middle] * 8 + [((LANES, LANES), F32)],
        places=[VMEM] * 2 + [HBM] * 11,
        limit=24,
        semaphores=11,
    )
    chunks = lax.all_to_all(chunk, ("gx", "gy"), 0, 0, tiled=True)
    place = jnp.stack([lax.axis_index("gx"), lax.axis_index("gy")]).astype(jnp.int32)
    plane = ((32, 16, LANES), F32)
    (out,) = call(
        up_kernel,
        [brick],
        (place, chunks, own) + tuple(kept),
        scratch=[fine] * 6
        + [middle] * 5
        + [plane] * 9
        + [brick, ((16, 32, LANES), F32), ((8, 32, LANES), F32)]
        + [middle] * 2
        + [fine] * 2,
        specs=[SMEM] + [VMEM] * 2 + [HBM] * 11,
        limit=24,
        semaphores=11,
    )
    return out, mobility


def solution(mesh):
    return jax.shard_map(
        body,
        mesh=mesh,
        in_specs=(
            P("gx", "gy", "gz"),
            P("gx", "gy", "gz"),
            P(None, "gx", "gy", "gz"),
            P("gx", "gy", "gz", None),
        ),
        out_specs=(P("gx", "gy", "gz"), P("gx", "gy", "gz")),
        check_vma=False,
    )
```

```python
import functools

import jax
import jax.numpy as jnp
from jax import lax
from jax.experimental import pallas as pl
from jax.experimental.pallas import tpu as pltpu
from jax.sharding import PartitionSpec as P

SLOTS = 8
BRICK = 16
OMEGA = 0.8
TAU = 256.0
LANES = 128
RING = 256
F32 = jnp.float32
BF16 = jnp.bfloat16
HIGH = lax.Precision.HIGHEST
VMEM = pl.BlockSpec(memory_space=pltpu.VMEM)
HBM = pl.BlockSpec(memory_space=pltpu.MemorySpace.HBM)
SMEM = pl.BlockSpec(memory_space=pltpu.SMEM)
COARSE = 51
COARSE_LOW = 10
MIDDLE = 70
MIDDLE_LOW = 3
CHUNK = 112
FINE_PLANES = pl.ds(6, 20)
MIDDLE_PLANES = pl.ds(1, 13)


def call(kernel, outs, args, scratch=(), specs=None, places=None, limit=16, semaphores=0):
    specs = specs or [VMEM] * len(args)
    places = places or [VMEM] * len(outs)
    args = [
        pltpu.with_memory_space_constraint(arg, pltpu.MemorySpace.HBM) if spec is HBM else arg
        for arg, spec in zip(args, specs)
    ]
    scratches = [pltpu.VMEM(shape, dtype) for shape, dtype in scratch]
    if semaphores:
        scratches.append(pltpu.SemaphoreType.DMA((semaphores,)))
    return pl.pallas_call(
        kernel,
        out_shape=[
            pltpu.MemorySpace.HBM(*out) if place is HBM else jax.ShapeDtypeStruct(*out)
            for out, place in zip(outs, places)
        ],
        in_specs=specs,
        out_specs=places,
        scratch_shapes=scratches,
        compiler_params=pltpu.CompilerParams(vmem_limit_bytes=limit << 20),
    )(*args)


def roll(x, shift, axis):
    return pltpu.roll(x, shift % x.shape[axis], axis)


def iota(shape, axis):
    return lax.broadcasted_iota(jnp.int32, shape, axis)


def select_dot(a, picks):
    picks = picks.astype(BF16)
    total = None
    for _ in range(3):
        part = a.astype(BF16)
        a = a - part.astype(F32)
        term = jnp.dot(part, picks, preferred_element_type=F32)
        total = term if total is None else total + term
    return total


def lane_ids(ids_ref):
    ids = ids_ref[0, 0].astype(F32)
    spread = (iota((8, LANES), 1) // BRICK == iota((8, LANES), 0)).astype(F32)
    grains = lax.dot_general(
        ids, spread, (((0,), (0,)), ((), ())), precision=HIGH, preferred_element_type=F32
    )
    return jnp.floor(grains + 0.5)


def split_ids(grains):
    high = jnp.floor(grains * (1.0 / 64.0))
    return jnp.concatenate([high, grains - 64.0 * high], axis=0).astype(BF16)


def join_ids(rows):
    rows = rows.astype(F32)
    return rows[:8] * 64.0 + rows[8:]


def faces_kernel(
    conc_in, side_in, order_in, ids_in,
    conc_ref, side_ref, order_ref, ids_ref, xm_ref, xp_ref, ym_ref, yp_ref, zm_ref, zp_ref, sems,
):
    pairs = (
        (ids_in, ids_ref), (order_in, order_ref), (conc_in, conc_ref), (side_in, side_ref),
    )
    copies = [pltpu.make_async_copy(a, b, sems.at[k]) for k, (a, b) in enumerate(pairs)]
    for copy in copies:
        copy.start()
    copies[0].wait()
    copies[1].wait()
    grains = lane_ids(ids_ref)
    packed = split_ids(grains)
    for ref in (xm_ref, xp_ref, ym_ref, yp_ref):
        ref[SLOTS] = packed
    zm_ref[16] = split_ids(jnp.broadcast_to(grains[:, 0:1], (8, LANES)))
    zp_ref[16] = split_ids(jnp.broadcast_to(grains[:, LANES - 1 :], (8, LANES)))
    lane = iota((16, LANES), 1)
    low = [jnp.zeros((16, LANES), F32)] * 16
    high = [jnp.zeros((16, LANES), F32)] * 16
    for slot in range(SLOTS):
        cells = order_ref[slot].astype(F32)
        xm_ref[slot] = order_ref[slot, 0]
        xp_ref[slot] = order_ref[slot, 15]
        ym_ref[slot] = cells[:, 0, :].astype(BF16)
        yp_ref[slot] = cells[:, 15, :].astype(BF16)
        for x in range(16):
            low[x] = jnp.where(lane == slot, cells[x, :, 0:1], low[x])
            high[x] = jnp.where(lane == slot, cells[x, :, LANES - 1 :], high[x])
    for x in range(16):
        zm_ref[x] = low[x].astype(BF16)
        zp_ref[x] = high[x].astype(BF16)
    copies[2].wait()
    copies[3].wait()


def square(x):
    return x * x


def mobility_kernel(
    conc_ref, side_ref, order_ref, ids_ref, xm_ref, xp_ref, ym_ref, yp_ref, zm_ref, zp_ref,
    own_ym_ref, own_yp_ref, mob_ref, keep_ref, zm_out, zp_out, work, weights,
):
    own = lane_ids(ids_ref)
    lane = iota((16, LANES), 1)
    row = iota((16, LANES), 0)
    last = lane % BRICK == BRICK - 1
    edge = last | (lane % BRICK == 0)

    lane8 = iota((8, LANES), 1)
    after = jnp.where(
        lane8 >= LANES - BRICK, join_ids(zp_ref[16]), roll(own, -BRICK, 1)
    )
    before = jnp.where(lane8 < BRICK, join_ids(zm_ref[16]), roll(own, BRICK, 1))
    beside = jnp.where(lane8 % BRICK == BRICK - 1, after, before)
    for other in range(SLOTS):
        match = (own == beside[other : other + 1]).astype(F32)
        for slot in range(SLOTS):
            weights[slot * SLOTS + other] = jnp.broadcast_to(match[slot : slot + 1], (8, LANES))

    def across(face_ref, ids, center):
        facing = [face_ref[other].astype(F32) for other in range(SLOTS)]
        total = None
        for slot in range(SLOTS):
            value = None
            for other in range(SLOTS):
                match = (own[slot : slot + 1] == ids[other : other + 1]).astype(F32)
                term = match * facing[other]
                value = term if value is None else value + term
            part = square(value - center(slot))
            total = part if total is None else total + part
        return total

    def doubled(block):
        return jnp.concatenate([block, block], axis=0)

    def plane(x, carry_in):
        conc = conc_ref[x]
        base = 1.0 + 8.0 * square(conc * (1.0 - conc))
        zlow = zm_ref[x].astype(F32)
        zhigh = zp_ref[x].astype(F32)
        along_y = jnp.zeros((16, LANES), F32)
        along_z = jnp.zeros((16, LANES), F32)
        along_x = jnp.zeros((16, LANES), F32)
        centers = []
        facing = []
        above = min(x + 1, 15)
        for slot in range(SLOTS):
            here = order_ref[slot, x].astype(F32)
            there = order_ref[slot, above].astype(F32)
            centers.append(here)
            along_x = along_x + square(there - here)
            along_y = along_y + square(roll(here, -1, 0) - here)
            right = roll(here, -1, 1)
            along_z = along_z + square(right - here)
            right = jnp.where(lane == LANES - 1, zhigh[:, slot : slot + 1], right)
            left = jnp.where(lane == 0, zlow[:, slot : slot + 1], roll(here, 1, 1))
            facing.append(jnp.where(last, right, left))
        along_y = jnp.where(row == 15, 0.0, along_y)
        along_z = jnp.where(last, 0.0, along_z)
        remapped = jnp.zeros((16, LANES), F32)
        for slot in range(SLOTS):
            value = None
            for other in range(SLOTS):
                term = doubled(weights[slot * SLOTS + other]) * facing[other]
                value = term if value is None else value + term
            remapped = remapped + square(value - centers[slot])
        total = base + along_y + roll(along_y, 1, 0) + along_z + roll(along_z, 1, 1)
        total = total + jnp.where(edge, remapped, 0.0) + along_x + carry_in
        work[x] = total
        return along_x

    carry = jnp.zeros((16, LANES), F32)
    for x in range(16):
        carry = plane(x, carry)
    work[0] = work[0] + across(
        xm_ref, join_ids(xm_ref[SLOTS]), lambda s: order_ref[s, 0].astype(F32)
    )
    work[15] = work[15] + across(
        xp_ref, join_ids(xp_ref[SLOTS]), lambda s: order_ref[s, 15].astype(F32)
    )
    bottom = across(ym_ref, join_ids(ym_ref[SLOTS]), lambda s: own_ym_ref[s].astype(F32))
    top = across(yp_ref, join_ids(yp_ref[SLOTS]), lambda s: own_yp_ref[s].astype(F32))
    for x in range(16):
        value = work[x]
        value = value + jnp.where(row == 0, bottom[x : x + 1], 0.0)
        value = value + jnp.where(row == 15, top[x : x + 1], 0.0)
        mob_ref[x] = value
        keep_ref[x] = value
        conc, side = conc_ref[x], side_ref[x]
        first = jnp.where(
            lane < 43, value, jnp.where(lane < 86, roll(conc, 43, 1), roll(side, 86, 1))
        )
        zm_out[x] = first.astype(BF16)
        final = jnp.where(
            lane >= 85, value, jnp.where(lane >= 42, roll(conc, -43, 1), roll(side, -86, 1))
        )
        zp_out[x] = final.astype(BF16)


def split_kernel(mob_ref, conc_ref, side_ref, zm_ref, zp_ref, low_ref, high_ref):
    for place, ref in enumerate((mob_ref, conc_ref, side_ref, zm_ref, zp_ref)):
        low_ref[place] = ref[:, :8].astype(BF16)
        high_ref[place] = ref[:, 8:].astype(BF16)


def rows_kernel(below_ref, low_ref, high_ref, above_ref, xl_ref, xh_ref):
    for place, ref in enumerate((below_ref, low_ref, high_ref, above_ref)):
        rows = pl.ds(8 * place, 8)
        xl_ref[:, :, rows, :] = ref[:, :8]
        xh_ref[:, :, rows, :] = ref[:, 8:]


def partner(x, step, axis):
    upper = (iota(x.shape, axis) & step) != 0
    return jnp.where(upper, roll(x, step, axis), roll(x, -step, axis))


def pair_sum(x, step, axis):
    return x + partner(x, step, axis)


def upper_of(x, step, axis):
    upper = (iota(x.shape, axis) & step) != 0
    return jnp.where(upper, x, roll(x, -step, axis))


def residual(value, source, flux_x, flux_x_before, ky, kz, step):
    flux_y = ky * (roll(value, -step, 0) - value)
    flux_z = kz * (roll(value, -step, 1) - value)
    total = (source - value) + (flux_x - flux_x_before)
    total = total + (flux_y - roll(flux_y, step, 0))
    return total + (flux_z - roll(flux_z, step, 1))


def sweep_planes(first, last, values, source, kx, ky, kz, step, use):
    before = kx[first - 1] * (values[first] - values[first - 1])

    value = values[first]
    for x in range(first, last + 1):
        above = values[x + 1]
        flux = kx[x] * (above - value)
        use(x, value, residual(value, source[x], flux, before, ky[x], kz[x], step))
        before = flux
        value = above


def down_kernel(
    mob_in, conc_in, side_in, zm_ref, zp_ref, below_ref, above_ref, xm_ref, xp_ref,
    own_ref, chunk_ref, side_out, kx_out, ky_out, kz_out, wd_out, v_out,
    k1x_out, k1y_out, k1z_out, wd1_out, f1_out,
    mob, v0, res, v_ref, side_ref, kx_ref, ky_ref, kz_ref, wd_ref,
    f1_ref, k1x_ref, k1y_ref, k1z_ref, wd1_ref, e0, e1, r1, rows, sems,
):
    copies = []

    def store(source, target, planes):
        copy = pltpu.make_async_copy(source.at[planes], target.at[planes], sems.at[len(copies)])
        copy.start()
        copies.append(copy)

    lane = iota((32, LANES), 1)

    def own_plane(x, place, ref):
        parts = (below_ref[place, x], ref[x], above_ref[place, x])
        return jnp.concatenate([part.astype(F32) for part in parts], axis=0)

    own = (mob_in, conc_in, side_in, zm_ref, zp_ref)
    for x in range(32):
        if 8 <= x < 24:
            parts = [own_plane(x - 8, place, ref) for place, ref in enumerate(own)]
        else:
            ref = xm_ref if x < 8 else xp_ref
            parts = [ref[place, x % 8].astype(F32) for place in range(5)]
        mob[x, :, :LANES] = parts[0]
        v0[x, :, :LANES] = parts[1]
        side_ref[x, :, :LANES] = parts[2]
        down, up = parts[3], parts[4]
        mob[x, :, LANES:] = jnp.where(lane < 43, up, jnp.where(lane >= 85, down, 1.0))
        v0[x, :, LANES:] = jnp.where(
            lane < 43, roll(up, -43, 1), jnp.where(lane >= 85, roll(down, 43, 1), 0.0)
        )
        side_ref[x, :, LANES:] = jnp.where(
            lane < 42, roll(up, -86, 1), jnp.where(lane >= 86, roll(down, 86, 1), 0.0)
        )

    half = TAU / 2

    before = half * (mob[1] + mob[2])
    kx_ref[1] = before
    for x in range(2, 30):
        here = mob[x]
        kx = half * (here + mob[x + 1])
        ky = half * (here + roll(here, -1, 0))
        kz = half * (here + roll(here, -1, 1))
        kx_ref[x] = kx
        ky_ref[x] = ky
        kz_ref[x] = kz
        total = (kx + before) + (ky + roll(ky, 1, 0)) + (kz + roll(kz, 1, 1))
        wd_ref[x] = OMEGA / (1.0 + total)
        before = kx

    store(side_ref, side_out, FINE_PLANES)
    store(kx_ref, kx_out, FINE_PLANES)
    store(ky_ref, ky_out, FINE_PLANES)
    store(kz_ref, kz_out, FINE_PLANES)
    store(wd_ref, wd_out, FINE_PLANES)

    def smooth(target, weight):
        def use(x, value, left):
            target[x] = value + weight[x] * left

        return use

    sweep_planes(2, 29, v0, side_ref, kx_ref, ky_ref, kz_ref, 1, smooth(res, wd_ref))
    sweep_planes(3, 28, res, side_ref, kx_ref, ky_ref, kz_ref, 1, smooth(v_ref, wd_ref))

    store(v_ref, v_out, FINE_PLANES)

    def keep(x, value, left):
        res[x] = left

    sweep_planes(4, 27, v_ref, side_ref, kx_ref, ky_ref, kz_ref, 1, keep)

    def pool(x):
        return pair_sum(pair_sum(x, 1, 0), 1, 1)

    for i in range(1, 14):
        x = 2 * i
        k1x_ref[i] = pool(kx_ref[x + 1]) * (1.0 / 16.0)
        if i == 1:
            for ref in (f1_ref, k1y_ref, k1z_ref, wd1_ref):
                ref[i] = jnp.zeros((32, RING), F32)
            continue
        f1_ref[i] = pool(res[x] + res[x + 1]) * 0.125
        along_y = pair_sum(ky_ref[x] + ky_ref[x + 1], 1, 1)
        k1y = upper_of(along_y, 1, 0) * (1.0 / 16.0)
        along_z = pair_sum(kz_ref[x] + kz_ref[x + 1], 1, 0)
        k1z = upper_of(along_z, 1, 1) * (1.0 / 16.0)
        k1y_ref[i] = k1y
        k1z_ref[i] = k1z
        total = (k1x_ref[i] + k1x_ref[i - 1]) + (k1y + roll(k1y, 2, 0)) + (k1z + roll(k1z, 2, 1))
        weight = OMEGA / (1.0 + total)
        wd1_ref[i] = weight
        e0[i] = weight * f1_ref[i]
    store(k1x_ref, k1x_out, MIDDLE_PLANES)
    store(k1y_ref, k1y_out, MIDDLE_PLANES)
    store(k1z_ref, k1z_out, MIDDLE_PLANES)
    store(wd1_ref, wd1_out, MIDDLE_PLANES)
    store(f1_ref, f1_out, MIDDLE_PLANES)
    sweep_planes(3, 12, e0, f1_ref, k1x_ref, k1y_ref, k1z_ref, 2, smooth(e1, wd1_ref))

    def keep_middle(x, value, left):
        r1[x] = left

    sweep_planes(4, 11, e1, f1_ref, k1x_ref, k1y_ref, k1z_ref, 2, keep_middle)

    src = iota((RING, LANES), 0)
    dst = iota((RING, LANES), 1)
    cell = jnp.where(src < 192, src, src - RING)
    pick_low = (cell == 4 * (dst - COARSE_LOW)) & (dst < COARSE)
    pick_high = (cell == 4 * (dst - 64 - COARSE_LOW)) & (dst >= 64) & (dst < 64 + COARSE)
    picks = jnp.concatenate([pick_low.astype(F32), pick_high.astype(F32)], axis=0)
    pick_middle = ((cell == 2 * (dst - MIDDLE_LOW)) & (dst < MIDDLE)).astype(F32)
    firsts = []
    seconds = []
    for j in range(4):
        i = 4 + 2 * j
        f2 = pair_sum(pair_sum(r1[i] + r1[i + 1], 2, 0), 2, 1) * 0.125
        k2x = pair_sum(pair_sum(k1x_ref[i + 1], 2, 0), 2, 1) * (1.0 / 16.0)
        k2y = pair_sum(k1y_ref[i] + k1y_ref[i + 1], 2, 1)
        k2y = upper_of(k2y, 2, 0) * (1.0 / 16.0)
        k2z = pair_sum(k1z_ref[i] + k1z_ref[i + 1], 2, 0)
        k2z = upper_of(k2z, 2, 1) * (1.0 / 16.0)
        firsts.append(jnp.concatenate([f2[8:24], k2x[8:24]], axis=1))
        seconds.append(jnp.concatenate([k2y[8:24], k2z[8:24]], axis=1))
    rows[...] = select_dot(jnp.concatenate(firsts + seconds, axis=0), picks)
    coarse = rows[pl.ds(0, 32, stride=4), :]
    rows[...] = select_dot(
        jnp.concatenate([e1[4 + i, 8:24] for i in range(8)], axis=0), pick_middle
    )
    middle = rows[pl.ds(0, 64, stride=2), :]
    own_ref[...] = middle
    high = coarse.astype(BF16)
    low = (coarse[:16] - high[:16].astype(F32)).astype(BF16)
    chunk = jnp.concatenate([high, low, middle.astype(BF16)], axis=0)
    for k in range(32):
        chunk_ref[k] = chunk
    for copy in copies:
        copy.wait()


def up_kernel(
    place_ref, all_ref, own_ref, side_in, kx_in, ky_in, kz_in, wd_in, v_in,
    k1x_in, k1y_in, k1z_in, wd1_in, f1_in,
    out_ref,
    side_ref, kx_ref, ky_ref, kz_ref, wd_ref, v_ref, k1x_ref, k1y_ref, k1z_ref, wd1_ref, f1_ref,
    pair0, pair1, c2x, c2y, c2z, wd2, f2, ea, eb, mid, tall, lean, e1a, e1b, va, vb, sems,
):
    copies = []
    for planes, moves in (
        (MIDDLE_PLANES, (
            (k1x_in, k1x_ref), (k1y_in, k1y_ref), (k1z_in, k1z_ref), (wd1_in, wd1_ref),
            (f1_in, f1_ref),
        )),
        (FINE_PLANES, (
            (v_in, v_ref), (side_in, side_ref), (kx_in, kx_ref), (ky_in, ky_ref),
            (kz_in, kz_ref), (wd_in, wd_ref),
        )),
    ):
        for a, b in moves:
            copies.append(
                pltpu.make_async_copy(a.at[planes], b.at[planes], sems.at[len(copies)])
            )
    for copy in copies:
        copy.start()
    gx = place_ref[0]
    gy = place_ref[1]

    def source(dx, dy):
        return ((gx + dx + 8) & 7) * 4 + ((gy + dy + 4) & 3)

    for p in (0, 1, 2, 3, 4, 6, 7):
        for q in range(4):
            s = source(p - 1, q - 1)
            first = all_ref[s, pl.ds(0, 16), :].astype(F32)
            first = first + all_ref[s, pl.ds(32, 16), :].astype(F32)
            second = all_ref[s, pl.ds(16, 16), :].astype(F32)
            for i in range(4):
                pair0[4 * p + i, pl.ds(4 * q, 4), :] = first[4 * i : 4 * i + 4]
                pair1[4 * p + i, pl.ds(4 * q, 4), :] = second[4 * i : 4 * i + 4]
    for p in (-1, 0, 1):
        for q in (-1, 0, 1):
            if p == 0 and q == 0:
                cells = own_ref[...]
            else:
                cells = all_ref[source(p, q), pl.ds(48, 64), :].astype(F32)
            for i in range(1, 15):
                if (i - 4) // 8 != p:
                    continue
                start = 8 * ((i - 4) % 8)
                block = cells[start : start + 8]
                if q == -1:
                    mid[i, pl.ds(0, 4), :] = block[4:]
                elif q == 0:
                    mid[i, pl.ds(4, 8), :] = block
                else:
                    mid[i, pl.ds(12, 4), :] = block[:4]

    used = iota((16, LANES), 1) < COARSE
    for x in range(-6, 17):
        k = x % 32
        first = pair0[k]
        second = pair1[k]
        f2[k] = jnp.where(used, first, 0.0)
        c2x[k] = jnp.where(used, roll(first, 64, 1), 0.0)
        c2y[k] = jnp.where(used, second, 0.0)
        c2z[k] = jnp.where(used, roll(second, 64, 1), 0.0)
    for x in range(-5, 17):
        k = x % 32
        ky = c2y[k]
        kz = c2z[k]
        total = (c2x[k] + c2x[(x - 1) % 32]) + (ky + roll(ky, 1, 0)) + (kz + roll(kz, 1, 1))
        weight = OMEGA / (1.0 + total)
        wd2[k] = weight
        ea[k] = weight * f2[k]

    old, new = ea, eb
    for reach in range(6, -1, -1):
        first = 2 - reach
        value = old[first % 32]
        below = (first - 1) % 32
        before = c2x[below] * (value - old[below])
        for x in range(first, 10 + reach):
            k = x % 32
            above = old[(x + 1) % 32]
            flux = c2x[k] * (above - value)
            left = residual(value, f2[k], flux, before, c2y[k], c2z[k], 1)
            new[k] = value + wd2[k] * left
            before = flux
            value = above
        old, new = new, old

    lane = iota((8, LANES), 1)
    for j in range(8):
        line = roll(old[2 + j, pl.ds(2, 8), :], MIDDLE, 1)
        line = jnp.where((lane >= MIDDLE) & (lane < MIDDLE + COARSE), line, 0.0)
        for k in range(4):
            lean[j, pl.ds(k, 8, stride=4), :] = line
    for i in range(1, 15):
        line = mid[i]
        for k in range(2):
            tall[i, pl.ds(k, 16, stride=2), :] = line
    src = iota((LANES, RING), 0)
    dst = iota((LANES, RING), 1)
    cell = jnp.where(dst < 192, dst, dst - RING)
    middle = (cell >= -2 * MIDDLE_LOW) & (src < MIDDLE)
    middle = middle & ((cell + 2 * MIDDLE_LOW) // 2 == src)
    coarse = (cell >= -4 * COARSE_LOW) & (src >= MIDDLE) & (src < MIDDLE + COARSE)
    coarse = coarse & ((cell + 4 * COARSE_LOW) // 4 == src - MIDDLE)
    spread = (middle | coarse).astype(F32)
    narrow = iota((32, LANES), 1) < MIDDLE
    packed = [jnp.where(narrow, tall[i], lean[i // 2]) for i in range(1, 15)]
    widened = select_dot(jnp.concatenate(packed, axis=0), spread)
    for i in range(1, 15):
        e1a[i] = widened[32 * (i - 1) : 32 * i]

    def smooth(target, weight):
        def use(x, value, left):
            target[x] = value + weight[x] * left

        return use

    for copy in copies:
        copy.wait()
    sweep_planes(2, 13, e1a, f1_ref, k1x_ref, k1y_ref, k1z_ref, 2, smooth(e1b, wd1_ref))
    sweep_planes(3, 12, e1b, f1_ref, k1x_ref, k1y_ref, k1z_ref, 2, smooth(e1a, wd1_ref))
    for x in range(6, 26):
        va[x] = v_ref[x] + e1a[x // 2]
    sweep_planes(7, 24, va, side_ref, kx_ref, ky_ref, kz_ref, 1, smooth(vb, wd_ref))

    def finish(x, value, left):
        new = value + wd_ref[x] * left
        out_ref[x - 8] = new[8:24, :LANES]

    sweep_planes(8, 23, vb, side_ref, kx_ref, ky_ref, kz_ref, 1, finish)


def shift(x, axis, direction):
    count = lax.axis_size(axis)
    return lax.ppermute(x, axis, [(i, (i + direction) % count) for i in range(count)])


def body(conc, right_side, order_field, grain_ids):
    face = ((9, 16, LANES), BF16)
    zface = ((17, 16, LANES), BF16)
    brick = ((16, 16, LANES), F32)
    conc, side, order, ids, xm, xp, ym, yp, zm, zp = call(
        faces_kernel,
        [brick, brick, ((8, 16, 16, LANES), BF16), ((1, 1, 8, 8), jnp.int32)]
        + [face] * 4
        + [zface] * 2,
        (conc, right_side, order_field, grain_ids),
        specs=[HBM] * 4,
        semaphores=4,
    )
    faces = (
        shift(xp, "gx", 1), shift(xm, "gx", -1),
        shift(yp, "gy", 1), shift(ym, "gy", -1),
        shift(zp, "gz", 1), shift(zm, "gz", -1),
    )
    pack = ((16, 16, LANES), BF16)
    mobility, keep, zm, zp = call(
        mobility_kernel,
        [brick, brick, pack, pack],
        (conc, side, order, ids) + faces + (ym, yp),
        scratch=[brick, ((64, 8, LANES), F32)],
    )
    left = shift(zp, "gz", 1)
    right = shift(zm, "gz", -1)
    half = ((5, 16, 8, LANES), BF16)
    low, high = call(split_kernel, [half, half], (keep, conc, side, left, right))
    below = shift(high, "gy", 1)
    above = shift(low, "gy", -1)
    slab = ((5, 8, 32, LANES), BF16)
    xl, xh = call(rows_kernel, [slab, slab], (below, low, high, above))
    before = shift(xh, "gx", 1)
    after = shift(xl, "gx", -1)
    fine = ((32, 32, RING), F32)
    middle = ((16, 32, RING), F32)
    own, chunk, *kept = call(
        down_kernel,
        [((64, LANES), F32), ((32, CHUNK, LANES), BF16)] + [fine] * 6 + [middle] * 5,
        (keep, conc, side, left, right, below, above, before, after),
        scratch=[fine] * 9 + [middle] * 8 + [((LANES, LANES), F32)],
        places=[VMEM] * 2 + [HBM] * 11,
        limit=24,
        semaphores=11,
    )
    place = jnp.stack([lax.axis_index("gx"), lax.axis_index("gy")]).astype(jnp.int32)
    chunk, place = lax.optimization_barrier((chunk, place))
    chunks = lax.all_to_all(chunk, ("gx", "gy"), 0, 0, tiled=True)
    plane = ((32, 16, LANES), F32)
    (out,) = call(
        up_kernel,
        [brick],
        (place, chunks, own) + tuple(kept),
        scratch=[fine] * 6
        + [middle] * 5
        + [plane] * 9
        + [brick, ((16, 32, LANES), F32), ((8, 32, LANES), F32)]
        + [middle] * 2
        + [fine] * 2,
        specs=[SMEM] + [VMEM] * 2 + [HBM] * 11,
        limit=24,
        semaphores=11,
    )
    return out, mobility


def solution(mesh):
    return jax.shard_map(
        body,
        mesh=mesh,
        in_specs=(
            P("gx", "gy", "gz"),
            P("gx", "gy", "gz"),
            P(None, "gx", "gy", "gz"),
            P("gx", "gy", "gz", None),
        ),
        out_specs=(P("gx", "gy", "gz"), P("gx", "gy", "gz")),
        check_vma=False,
    )
```

```python
import functools

import jax
import jax.numpy as jnp
from jax import lax
from jax.experimental import pallas as pl
from jax.experimental.pallas import tpu as pltpu
from jax.sharding import PartitionSpec as P

SLOTS = 8
BRICK = 16
OMEGA = 0.8
TAU = 256.0
LANES = 128
RING = 256
F32 = jnp.float32
BF16 = jnp.bfloat16
HIGH = lax.Precision.HIGHEST
VMEM = pl.BlockSpec(memory_space=pltpu.VMEM)
HBM = pl.BlockSpec(memory_space=pltpu.MemorySpace.HBM)
SMEM = pl.BlockSpec(memory_space=pltpu.SMEM)
COARSE = 51
COARSE_LOW = 10
MIDDLE = 70
MIDDLE_LOW = 3
CHUNK = 112
FINE_PLANES = pl.ds(6, 20)
MIDDLE_PLANES = pl.ds(1, 13)


def call(kernel, outs, args, scratch=(), specs=None, places=None, limit=16, semaphores=0):
    specs = specs or [VMEM] * len(args)
    places = places or [VMEM] * len(outs)
    args = [
        pltpu.with_memory_space_constraint(arg, pltpu.MemorySpace.HBM) if spec is HBM else arg
        for arg, spec in zip(args, specs)
    ]
    scratches = [pltpu.VMEM(shape, dtype) for shape, dtype in scratch]
    if semaphores:
        scratches.append(pltpu.SemaphoreType.DMA((semaphores,)))
    return pl.pallas_call(
        kernel,
        out_shape=[
            pltpu.MemorySpace.HBM(*out) if place is HBM else jax.ShapeDtypeStruct(*out)
            for out, place in zip(outs, places)
        ],
        in_specs=specs,
        out_specs=places,
        scratch_shapes=scratches,
        compiler_params=pltpu.CompilerParams(vmem_limit_bytes=limit << 20),
    )(*args)


def roll(x, shift, axis):
    return pltpu.roll(x, shift % x.shape[axis], axis)


def iota(shape, axis):
    return lax.broadcasted_iota(jnp.int32, shape, axis)


def select_dot(a, picks):
    picks = picks.astype(BF16)
    total = None
    for _ in range(3):
        part = a.astype(BF16)
        a = a - part.astype(F32)
        term = jnp.dot(part, picks, preferred_element_type=F32)
        total = term if total is None else total + term
    return total


def lane_ids(ids_ref):
    ids = ids_ref[0, 0].astype(F32)
    spread = (iota((8, LANES), 1) // BRICK == iota((8, LANES), 0)).astype(F32)
    grains = lax.dot_general(
        ids, spread, (((0,), (0,)), ((), ())), precision=HIGH, preferred_element_type=F32
    )
    return jnp.floor(grains + 0.5)


def split_ids(grains):
    high = jnp.floor(grains * (1.0 / 64.0))
    return jnp.concatenate([high, grains - 64.0 * high], axis=0).astype(BF16)


def join_ids(rows):
    rows = rows.astype(F32)
    return rows[:8] * 64.0 + rows[8:]


def faces_kernel(
    conc_in, side_in, order_in, ids_in,
    conc_ref, side_ref, order_ref, ids_ref, xm_ref, xp_ref, ym_ref, yp_ref, zm_ref, zp_ref, sems,
):
    pairs = (
        (ids_in, ids_ref), (order_in, order_ref), (conc_in, conc_ref), (side_in, side_ref),
    )
    copies = [pltpu.make_async_copy(a, b, sems.at[k]) for k, (a, b) in enumerate(pairs)]
    for copy in copies:
        copy.start()
    copies[0].wait()
    copies[1].wait()
    grains = lane_ids(ids_ref)
    packed = split_ids(grains)
    for ref in (xm_ref, xp_ref, ym_ref, yp_ref):
        ref[SLOTS] = packed
    zm_ref[16] = split_ids(jnp.broadcast_to(grains[:, 0:1], (8, LANES)))
    zp_ref[16] = split_ids(jnp.broadcast_to(grains[:, LANES - 1 :], (8, LANES)))
    lane = iota((16, LANES), 1)
    low = [jnp.zeros((16, LANES), F32)] * 16
    high = [jnp.zeros((16, LANES), F32)] * 16
    for slot in range(SLOTS):
        cells = order_ref[slot].astype(F32)
        xm_ref[slot] = order_ref[slot, 0]
        xp_ref[slot] = order_ref[slot, 15]
        ym_ref[slot] = cells[:, 0, :].astype(BF16)
        yp_ref[slot] = cells[:, 15, :].astype(BF16)
        for x in range(16):
            low[x] = jnp.where(lane == slot, cells[x, :, 0:1], low[x])
            high[x] = jnp.where(lane == slot, cells[x, :, LANES - 1 :], high[x])
    for x in range(16):
        zm_ref[x] = low[x].astype(BF16)
        zp_ref[x] = high[x].astype(BF16)
    copies[2].wait()
    copies[3].wait()


def square(x):
    return x * x


def mobility_kernel(
    conc_ref, side_ref, order_ref, ids_ref, xm_ref, xp_ref, ym_ref, yp_ref, zm_ref, zp_ref,
    own_ym_ref, own_yp_ref, mob_ref, keep_ref, zm_out, zp_out, work, weights,
):
    own = lane_ids(ids_ref)
    lane = iota((16, LANES), 1)
    row = iota((16, LANES), 0)
    last = lane % BRICK == BRICK - 1
    edge = last | (lane % BRICK == 0)

    lane8 = iota((8, LANES), 1)
    after = jnp.where(
        lane8 >= LANES - BRICK, join_ids(zp_ref[16]), roll(own, -BRICK, 1)
    )
    before = jnp.where(lane8 < BRICK, join_ids(zm_ref[16]), roll(own, BRICK, 1))
    beside = jnp.where(lane8 % BRICK == BRICK - 1, after, before)
    for other in range(SLOTS):
        match = (own == beside[other : other + 1]).astype(F32)
        for slot in range(SLOTS):
            weights[slot * SLOTS + other] = jnp.broadcast_to(match[slot : slot + 1], (8, LANES))

    def across(face_ref, ids, center):
        facing = [face_ref[other].astype(F32) for other in range(SLOTS)]
        total = None
        for slot in range(SLOTS):
            value = None
            for other in range(SLOTS):
                match = (own[slot : slot + 1] == ids[other : other + 1]).astype(F32)
                term = match * facing[other]
                value = term if value is None else value + term
            part = square(value - center(slot))
            total = part if total is None else total + part
        return total

    def doubled(block):
        return jnp.concatenate([block, block], axis=0)

    def plane(x, carry_in):
        conc = conc_ref[x]
        base = 1.0 + 8.0 * square(conc * (1.0 - conc))
        zlow = zm_ref[x].astype(F32)
        zhigh = zp_ref[x].astype(F32)
        along_y = jnp.zeros((16, LANES), F32)
        along_z = jnp.zeros((16, LANES), F32)
        along_x = jnp.zeros((16, LANES), F32)
        centers = []
        facing = []
        above = min(x + 1, 15)
        for slot in range(SLOTS):
            here = order_ref[slot, x].astype(F32)
            there = order_ref[slot, above].astype(F32)
            centers.append(here)
            along_x = along_x + square(there - here)
            along_y = along_y + square(roll(here, -1, 0) - here)
            right = roll(here, -1, 1)
            along_z = along_z + square(right - here)
            right = jnp.where(lane == LANES - 1, zhigh[:, slot : slot + 1], right)
            left = jnp.where(lane == 0, zlow[:, slot : slot + 1], roll(here, 1, 1))
            facing.append(jnp.where(last, right, left))
        along_y = jnp.where(row == 15, 0.0, along_y)
        along_z = jnp.where(last, 0.0, along_z)
        remapped = jnp.zeros((16, LANES), F32)
        for slot in range(SLOTS):
            value = None
            for other in range(SLOTS):
                term = doubled(weights[slot * SLOTS + other]) * facing[other]
                value = term if value is None else value + term
            remapped = remapped + square(value - centers[slot])
        total = base + along_y + roll(along_y, 1, 0) + along_z + roll(along_z, 1, 1)
        total = total + jnp.where(edge, remapped, 0.0) + along_x + carry_in
        work[x] = total
        return along_x

    carry = jnp.zeros((16, LANES), F32)
    for x in range(16):
        carry = plane(x, carry)
    work[0] = work[0] + across(
        xm_ref, join_ids(xm_ref[SLOTS]), lambda s: order_ref[s, 0].astype(F32)
    )
    work[15] = work[15] + across(
        xp_ref, join_ids(xp_ref[SLOTS]), lambda s: order_ref[s, 15].astype(F32)
    )
    bottom = across(ym_ref, join_ids(ym_ref[SLOTS]), lambda s: own_ym_ref[s].astype(F32))
    top = across(yp_ref, join_ids(yp_ref[SLOTS]), lambda s: own_yp_ref[s].astype(F32))
    for x in range(16):
        value = work[x]
        value = value + jnp.where(row == 0, bottom[x : x + 1], 0.0)
        value = value + jnp.where(row == 15, top[x : x + 1], 0.0)
        mob_ref[x] = value
        keep_ref[x] = value
        conc, side = conc_ref[x], side_ref[x]
        first = jnp.where(
            lane < 43, value, jnp.where(lane < 86, roll(conc, 43, 1), roll(side, 86, 1))
        )
        zm_out[x] = first.astype(BF16)
        final = jnp.where(
            lane >= 85, value, jnp.where(lane >= 42, roll(conc, -43, 1), roll(side, -86, 1))
        )
        zp_out[x] = final.astype(BF16)


def split_kernel(mob_ref, conc_ref, side_ref, zm_ref, zp_ref, low_ref, high_ref):
    for place, ref in enumerate((mob_ref, conc_ref, side_ref, zm_ref, zp_ref)):
        low_ref[place] = ref[:, :8].astype(BF16)
        high_ref[place] = ref[:, 8:].astype(BF16)


def rows_kernel(below_ref, low_ref, high_ref, above_ref, xl_ref, xh_ref):
    for place, ref in enumerate((below_ref, low_ref, high_ref, above_ref)):
        rows = pl.ds(8 * place, 8)
        xl_ref[:, :, rows, :] = ref[:, :8]
        xh_ref[:, :, rows, :] = ref[:, 8:]


def partner(x, step, axis):
    upper = (iota(x.shape, axis) & step) != 0
    return jnp.where(upper, roll(x, step, axis), roll(x, -step, axis))


def pair_sum(x, step, axis):
    return x + partner(x, step, axis)


def upper_of(x, step, axis):
    upper = (iota(x.shape, axis) & step) != 0
    return jnp.where(upper, x, roll(x, -step, axis))


def groups(items, size):
    items = list(items)
    return [items[k : k + size] for k in range(0, len(items), size)]


def sweep_planes(first, last, values, source, kx, ky, kz, step, use, size=8, planes=None):
    at = (lambda x: x) if planes is None else (lambda x: x % planes)
    before = kx[at(first - 1)] * (values[at(first)] - values[at(first - 1)])
    for xs in groups(range(first, last + 1), size):
        cells = [values[at(x)] for x in xs + [xs[-1] + 1]]
        flux_z = [kz[at(x)] * (roll(v, -step, 1) - v) for x, v in zip(xs, cells)]
        back_z = [roll(flux, step, 1) for flux in flux_z]
        left = []
        for k, x in enumerate(xs):
            value = cells[k]
            flux_x = kx[at(x)] * (cells[k + 1] - value)
            flux_y = ky[at(x)] * (roll(value, -step, 0) - value)
            total = (source[at(x)] - value) + (flux_x - before)
            total = total + (flux_y - roll(flux_y, step, 0))
            left.append(total + (flux_z[k] - back_z[k]))
            before = flux_x
        for k, x in enumerate(xs):
            use(at(x), cells[k], left[k])


def down_kernel(
    mob_in, conc_in, side_in, zm_ref, zp_ref, below_ref, above_ref, xm_ref, xp_ref,
    own_ref, chunk_ref, side_out, kx_out, ky_out, kz_out, wd_out, v_out,
    k1x_out, k1y_out, k1z_out, wd1_out, f1_out,
    mob, v0, res, v_ref, side_ref, kx_ref, ky_ref, kz_ref, wd_ref,
    f1_ref, k1x_ref, k1y_ref, k1z_ref, wd1_ref, e0, e1, r1, rows, sems,
):
    copies = []

    def store(source, target, planes):
        copy = pltpu.make_async_copy(source.at[planes], target.at[planes], sems.at[len(copies)])
        copy.start()
        copies.append(copy)

    lane = iota((32, LANES), 1)

    def own_plane(x, place, ref):
        parts = (below_ref[place, x], ref[x], above_ref[place, x])
        return jnp.concatenate([part.astype(F32) for part in parts], axis=0)

    own = (mob_in, conc_in, side_in, zm_ref, zp_ref)
    for xs in groups(range(32), 8):
        planes = []
        for x in xs:
            if 8 <= x < 24:
                parts = [own_plane(x - 8, place, ref) for place, ref in enumerate(own)]
            else:
                ref = xm_ref if x < 8 else xp_ref
                parts = [ref[place, x % 8].astype(F32) for place in range(5)]
            down, up = parts[3], parts[4]
            beyond = jnp.where(lane < 43, up, jnp.where(lane >= 85, down, 1.0))
            iterate = jnp.where(
                lane < 43, roll(up, -43, 1), jnp.where(lane >= 85, roll(down, 43, 1), 0.0)
            )
            right = jnp.where(
                lane < 42, roll(up, -86, 1), jnp.where(lane >= 86, roll(down, 86, 1), 0.0)
            )
            planes.append((parts, beyond, iterate, right))
        for x, (parts, beyond, iterate, right) in zip(xs, planes):
            mob[x, :, :LANES] = parts[0]
            v0[x, :, :LANES] = parts[1]
            side_ref[x, :, :LANES] = parts[2]
            mob[x, :, LANES:] = beyond
            v0[x, :, LANES:] = iterate
            side_ref[x, :, LANES:] = right

    half = TAU / 2

    before = half * (mob[1] + mob[2])
    kx_ref[1] = before
    for xs in groups(range(2, 30), 7):
        here = [mob[x] for x in xs + [xs[-1] + 1]]
        kz = [half * (cells + roll(cells, -1, 1)) for cells in here[:-1]]
        back = [roll(k, 1, 1) for k in kz]
        done = []
        for k, x in enumerate(xs):
            kx = half * (here[k] + here[k + 1])
            ky = half * (here[k] + roll(here[k], -1, 0))
            total = (kx + before) + (ky + roll(ky, 1, 0)) + (kz[k] + back[k])
            done.append((kx, ky, OMEGA / (1.0 + total)))
            before = kx
        for k, x in enumerate(xs):
            kx_ref[x], ky_ref[x], wd_ref[x] = done[k]
            kz_ref[x] = kz[k]

    store(side_ref, side_out, FINE_PLANES)
    store(kx_ref, kx_out, FINE_PLANES)
    store(ky_ref, ky_out, FINE_PLANES)
    store(kz_ref, kz_out, FINE_PLANES)
    store(wd_ref, wd_out, FINE_PLANES)

    def smooth(target, weight):
        def use(x, value, left):
            target[x] = value + weight[x] * left

        return use

    sweep_planes(2, 29, v0, side_ref, kx_ref, ky_ref, kz_ref, 1, smooth(res, wd_ref))
    sweep_planes(3, 28, res, side_ref, kx_ref, ky_ref, kz_ref, 1, smooth(v_ref, wd_ref))

    store(v_ref, v_out, FINE_PLANES)

    def keep(x, value, left):
        res[x] = left

    sweep_planes(4, 27, v_ref, side_ref, kx_ref, ky_ref, kz_ref, 1, keep)

    def pool(x):
        return pair_sum(pair_sum(x, 1, 0), 1, 1)

    for xs in groups(range(1, 14), 7):
        done = [pool(kx_ref[2 * i + 1]) * (1.0 / 16.0) for i in xs]
        for i, value in zip(xs, done):
            k1x_ref[i] = value
    for ref in (f1_ref, k1y_ref, k1z_ref, wd1_ref):
        ref[1] = jnp.zeros((32, RING), F32)
    for xs in groups(range(2, 14), 6):
        done = []
        for i in xs:
            x = 2 * i
            f1 = pool(res[x] + res[x + 1]) * 0.125
            along_y = pair_sum(ky_ref[x] + ky_ref[x + 1], 1, 1)
            k1y = upper_of(along_y, 1, 0) * (1.0 / 16.0)
            along_z = pair_sum(kz_ref[x] + kz_ref[x + 1], 1, 0)
            k1z = upper_of(along_z, 1, 1) * (1.0 / 16.0)
            total = k1x_ref[i] + k1x_ref[i - 1]
            total = total + (k1y + roll(k1y, 2, 0)) + (k1z + roll(k1z, 2, 1))
            weight = OMEGA / (1.0 + total)
            done.append((f1, k1y, k1z, weight, weight * f1))
        for i, value in zip(xs, done):
            f1_ref[i], k1y_ref[i], k1z_ref[i], wd1_ref[i], e0[i] = value
    store(k1x_ref, k1x_out, MIDDLE_PLANES)
    store(k1y_ref, k1y_out, MIDDLE_PLANES)
    store(k1z_ref, k1z_out, MIDDLE_PLANES)
    store(wd1_ref, wd1_out, MIDDLE_PLANES)
    store(f1_ref, f1_out, MIDDLE_PLANES)
    sweep_planes(3, 12, e0, f1_ref, k1x_ref, k1y_ref, k1z_ref, 2, smooth(e1, wd1_ref))

    def keep_middle(x, value, left):
        r1[x] = left

    sweep_planes(4, 11, e1, f1_ref, k1x_ref, k1y_ref, k1z_ref, 2, keep_middle)

    src = iota((RING, LANES), 0)
    dst = iota((RING, LANES), 1)
    cell = jnp.where(src < 192, src, src - RING)
    pick_low = (cell == 4 * (dst - COARSE_LOW)) & (dst < COARSE)
    pick_high = (cell == 4 * (dst - 64 - COARSE_LOW)) & (dst >= 64) & (dst < 64 + COARSE)
    picks = jnp.concatenate([pick_low.astype(F32), pick_high.astype(F32)], axis=0)
    pick_middle = ((cell == 2 * (dst - MIDDLE_LOW)) & (dst < MIDDLE)).astype(F32)
    firsts = []
    seconds = []
    for j in range(4):
        i = 4 + 2 * j
        f2 = pair_sum(pair_sum(r1[i] + r1[i + 1], 2, 0), 2, 1) * 0.125
        k2x = pair_sum(pair_sum(k1x_ref[i + 1], 2, 0), 2, 1) * (1.0 / 16.0)
        k2y = pair_sum(k1y_ref[i] + k1y_ref[i + 1], 2, 1)
        k2y = upper_of(k2y, 2, 0) * (1.0 / 16.0)
        k2z = pair_sum(k1z_ref[i] + k1z_ref[i + 1], 2, 0)
        k2z = upper_of(k2z, 2, 1) * (1.0 / 16.0)
        firsts.append(jnp.concatenate([f2[8:24], k2x[8:24]], axis=1))
        seconds.append(jnp.concatenate([k2y[8:24], k2z[8:24]], axis=1))
    rows[...] = select_dot(jnp.concatenate(firsts + seconds, axis=0), picks)
    coarse = rows[pl.ds(0, 32, stride=4), :]
    rows[...] = select_dot(
        jnp.concatenate([e1[4 + i, 8:24] for i in range(8)], axis=0), pick_middle
    )
    middle = rows[pl.ds(0, 64, stride=2), :]
    own_ref[...] = middle
    high = coarse.astype(BF16)
    low = (coarse[:16] - high[:16].astype(F32)).astype(BF16)
    chunk = jnp.concatenate([high, low, middle.astype(BF16)], axis=0)
    for k in range(32):
        chunk_ref[k] = chunk
    for copy in copies:
        copy.wait()


def up_kernel(
    place_ref, all_ref, own_ref, side_in, kx_in, ky_in, kz_in, wd_in, v_in,
    k1x_in, k1y_in, k1z_in, wd1_in, f1_in,
    out_ref,
    side_ref, kx_ref, ky_ref, kz_ref, wd_ref, v_ref, k1x_ref, k1y_ref, k1z_ref, wd1_ref, f1_ref,
    pair0, pair1, c2x, c2y, c2z, wd2, f2, ea, eb, mid, tall, lean, e1a, e1b, va, vb, sems,
):
    copies = []
    for planes, moves in (
        (MIDDLE_PLANES, (
            (k1x_in, k1x_ref), (k1y_in, k1y_ref), (k1z_in, k1z_ref), (wd1_in, wd1_ref),
            (f1_in, f1_ref),
        )),
        (FINE_PLANES, (
            (v_in, v_ref), (side_in, side_ref), (kx_in, kx_ref), (ky_in, ky_ref),
            (kz_in, kz_ref), (wd_in, wd_ref),
        )),
    ):
        for a, b in moves:
            copies.append(
                pltpu.make_async_copy(a.at[planes], b.at[planes], sems.at[len(copies)])
            )
    for copy in copies:
        copy.start()
    gx = place_ref[0]
    gy = place_ref[1]

    def source(dx, dy):
        return ((gx + dx + 8) & 7) * 4 + ((gy + dy + 4) & 3)

    for p in (0, 1, 2, 3, 4, 6, 7):
        for q in range(4):
            s = source(p - 1, q - 1)
            first = all_ref[s, pl.ds(0, 16), :].astype(F32)
            first = first + all_ref[s, pl.ds(32, 16), :].astype(F32)
            second = all_ref[s, pl.ds(16, 16), :].astype(F32)
            for i in range(4):
                pair0[4 * p + i, pl.ds(4 * q, 4), :] = first[4 * i : 4 * i + 4]
                pair1[4 * p + i, pl.ds(4 * q, 4), :] = second[4 * i : 4 * i + 4]
    for p in (-1, 0, 1):
        for q in (-1, 0, 1):
            if p == 0 and q == 0:
                cells = own_ref[...]
            else:
                cells = all_ref[source(p, q), pl.ds(48, 64), :].astype(F32)
            for i in range(1, 15):
                if (i - 4) // 8 != p:
                    continue
                start = 8 * ((i - 4) % 8)
                block = cells[start : start + 8]
                if q == -1:
                    mid[i, pl.ds(0, 4), :] = block[4:]
                elif q == 0:
                    mid[i, pl.ds(4, 8), :] = block
                else:
                    mid[i, pl.ds(12, 4), :] = block[:4]

    used = iota((16, LANES), 1) < COARSE
    for x in range(-6, 17):
        k = x % 32
        first = pair0[k]
        second = pair1[k]
        f2[k] = jnp.where(used, first, 0.0)
        c2x[k] = jnp.where(used, roll(first, 64, 1), 0.0)
        c2y[k] = jnp.where(used, second, 0.0)
        c2z[k] = jnp.where(used, roll(second, 64, 1), 0.0)
    for xs in groups(range(-5, 17), 11):
        done = []
        for x in xs:
            k = x % 32
            ky = c2y[k]
            kz = c2z[k]
            total = c2x[k] + c2x[(x - 1) % 32]
            total = total + (ky + roll(ky, 1, 0)) + (kz + roll(kz, 1, 1))
            weight = OMEGA / (1.0 + total)
            done.append((weight, weight * f2[k]))
        for x, value in zip(xs, done):
            wd2[x % 32], ea[x % 32] = value

    def smooth(target, weight):
        def use(x, value, left):
            target[x] = value + weight[x] * left

        return use

    old, new = ea, eb
    for reach in range(6, -1, -1):
        sweep_planes(
            2 - reach, 9 + reach, old, f2, c2x, c2y, c2z, 1, smooth(new, wd2), 10, 32
        )
        old, new = new, old

    lane = iota((8, LANES), 1)
    for j in range(8):
        line = roll(old[2 + j, pl.ds(2, 8), :], MIDDLE, 1)
        line = jnp.where((lane >= MIDDLE) & (lane < MIDDLE + COARSE), line, 0.0)
        for k in range(4):
            lean[j, pl.ds(k, 8, stride=4), :] = line
    for i in range(1, 15):
        line = mid[i]
        for k in range(2):
            tall[i, pl.ds(k, 16, stride=2), :] = line
    src = iota((LANES, RING), 0)
    dst = iota((LANES, RING), 1)
    cell = jnp.where(dst < 192, dst, dst - RING)
    middle = (cell >= -2 * MIDDLE_LOW) & (src < MIDDLE)
    middle = middle & ((cell + 2 * MIDDLE_LOW) // 2 == src)
    coarse = (cell >= -4 * COARSE_LOW) & (src >= MIDDLE) & (src < MIDDLE + COARSE)
    coarse = coarse & ((cell + 4 * COARSE_LOW) // 4 == src - MIDDLE)
    spread = (middle | coarse).astype(F32)
    narrow = iota((32, LANES), 1) < MIDDLE
    packed = [jnp.where(narrow, tall[i], lean[i // 2]) for i in range(1, 15)]
    widened = select_dot(jnp.concatenate(packed, axis=0), spread)
    for i in range(1, 15):
        e1a[i] = widened[32 * (i - 1) : 32 * i]

    for copy in copies:
        copy.wait()
    sweep_planes(2, 13, e1a, f1_ref, k1x_ref, k1y_ref, k1z_ref, 2, smooth(e1b, wd1_ref))
    sweep_planes(3, 12, e1b, f1_ref, k1x_ref, k1y_ref, k1z_ref, 2, smooth(e1a, wd1_ref))
    for x in range(6, 26):
        va[x] = v_ref[x] + e1a[x // 2]
    sweep_planes(7, 24, va, side_ref, kx_ref, ky_ref, kz_ref, 1, smooth(vb, wd_ref))

    def finish(x, value, left):
        new = value + wd_ref[x] * left
        out_ref[x - 8] = new[8:24, :LANES]

    sweep_planes(8, 23, vb, side_ref, kx_ref, ky_ref, kz_ref, 1, finish)


def shift(x, axis, direction):
    count = lax.axis_size(axis)
    return lax.ppermute(x, axis, [(i, (i + direction) % count) for i in range(count)])


def body(conc, right_side, order_field, grain_ids):
    face = ((9, 16, LANES), BF16)
    zface = ((17, 16, LANES), BF16)
    brick = ((16, 16, LANES), F32)
    conc, side, order, ids, xm, xp, ym, yp, zm, zp = call(
        faces_kernel,
        [brick, brick, ((8, 16, 16, LANES), BF16), ((1, 1, 8, 8), jnp.int32)]
        + [face] * 4
        + [zface] * 2,
        (conc, right_side, order_field, grain_ids),
        specs=[HBM] * 4,
        semaphores=4,
    )
    faces = (
        shift(xp, "gx", 1), shift(xm, "gx", -1),
        shift(yp, "gy", 1), shift(ym, "gy", -1),
        shift(zp, "gz", 1), shift(zm, "gz", -1),
    )
    pack = ((16, 16, LANES), BF16)
    mobility, keep, zm, zp = call(
        mobility_kernel,
        [brick, brick, pack, pack],
        (conc, side, order, ids) + faces + (ym, yp),
        scratch=[brick, ((64, 8, LANES), F32)],
    )
    left = shift(zp, "gz", 1)
    right = shift(zm, "gz", -1)
    half = ((5, 16, 8, LANES), BF16)
    low, high = call(split_kernel, [half, half], (keep, conc, side, left, right))
    below = shift(high, "gy", 1)
    above = shift(low, "gy", -1)
    slab = ((5, 8, 32, LANES), BF16)
    xl, xh = call(rows_kernel, [slab, slab], (below, low, high, above))
    before = shift(xh, "gx", 1)
    after = shift(xl, "gx", -1)
    fine = ((32, 32, RING), F32)
    middle = ((16, 32, RING), F32)
    own, chunk, *kept = call(
        down_kernel,
        [((64, LANES), F32), ((32, CHUNK, LANES), BF16)] + [fine] * 6 + [middle] * 5,
        (keep, conc, side, left, right, below, above, before, after),
        scratch=[fine] * 9 + [middle] * 8 + [((LANES, LANES), F32)],
        places=[VMEM] * 2 + [HBM] * 11,
        limit=24,
        semaphores=11,
    )
    place = jnp.stack([lax.axis_index("gx"), lax.axis_index("gy")]).astype(jnp.int32)
    chunk, place = lax.optimization_barrier((chunk, place))
    chunks = lax.all_to_all(chunk, ("gx", "gy"), 0, 0, tiled=True)
    plane = ((32, 16, LANES), F32)
    (out,) = call(
        up_kernel,
        [brick],
        (place, chunks, own) + tuple(kept),
        scratch=[fine] * 6
        + [middle] * 5
        + [plane] * 9
        + [brick, ((16, 32, LANES), F32), ((8, 32, LANES), F32)]
        + [middle] * 2
        + [fine] * 2,
        specs=[SMEM] + [VMEM] * 2 + [HBM] * 11,
        limit=24,
        semaphores=11,
    )
    return out, mobility


def solution(mesh):
    return jax.shard_map(
        body,
        mesh=mesh,
        in_specs=(
            P("gx", "gy", "gz"),
            P("gx", "gy", "gz"),
            P(None, "gx", "gy", "gz"),
            P("gx", "gy", "gz", None),
        ),
        out_specs=(P("gx", "gy", "gz"), P("gx", "gy", "gz")),
        check_vma=False,
    )
```

```python
import functools

import jax
import jax.numpy as jnp
from jax import lax
from jax.experimental import pallas as pl
from jax.experimental.pallas import tpu as pltpu
from jax.sharding import PartitionSpec as P

SLOTS = 8
BRICK = 16
OMEGA = 0.8
TAU = 256.0
LANES = 128
RING = 256
F32 = jnp.float32
BF16 = jnp.bfloat16
HIGH = lax.Precision.HIGHEST
VMEM = pl.BlockSpec(memory_space=pltpu.VMEM)
HBM = pl.BlockSpec(memory_space=pltpu.MemorySpace.HBM)
SMEM = pl.BlockSpec(memory_space=pltpu.SMEM)
COARSE = 51
COARSE_LOW = 10
MIDDLE = 70
MIDDLE_LOW = 3
HEAD = 26
CHUNK = 96
FINE_PLANES = pl.ds(6, 20)
MIDDLE_PLANES = pl.ds(1, 13)


def call(kernel, outs, args, scratch=(), specs=None, places=None, limit=16, semaphores=0):
    specs = specs or [VMEM] * len(args)
    places = places or [VMEM] * len(outs)
    args = [
        pltpu.with_memory_space_constraint(arg, pltpu.MemorySpace.HBM) if spec is HBM else arg
        for arg, spec in zip(args, specs)
    ]
    scratches = [pltpu.VMEM(shape, dtype) for shape, dtype in scratch]
    if semaphores:
        scratches.append(pltpu.SemaphoreType.DMA((semaphores,)))
    return pl.pallas_call(
        kernel,
        out_shape=[
            pltpu.MemorySpace.HBM(*out) if place is HBM else jax.ShapeDtypeStruct(*out)
            for out, place in zip(outs, places)
        ],
        in_specs=specs,
        out_specs=places,
        scratch_shapes=scratches,
        compiler_params=pltpu.CompilerParams(vmem_limit_bytes=limit << 20),
    )(*args)


def roll(x, shift, axis):
    return pltpu.roll(x, shift % x.shape[axis], axis)


def iota(shape, axis):
    return lax.broadcasted_iota(jnp.int32, shape, axis)


def select_dot(a, picks):
    picks = picks.astype(BF16)
    total = None
    for _ in range(3):
        part = a.astype(BF16)
        a = a - part.astype(F32)
        term = jnp.dot(part, picks, preferred_element_type=F32)
        total = term if total is None else total + term
    return total


def lane_ids(ids_ref):
    ids = ids_ref[0, 0].astype(F32)
    spread = (iota((8, LANES), 1) // BRICK == iota((8, LANES), 0)).astype(F32)
    grains = lax.dot_general(
        ids, spread, (((0,), (0,)), ((), ())), precision=HIGH, preferred_element_type=F32
    )
    return jnp.floor(grains + 0.5)


def split_ids(grains):
    high = jnp.floor(grains * (1.0 / 64.0))
    return jnp.concatenate([high, grains - 64.0 * high], axis=0).astype(BF16)


def join_ids(rows):
    rows = rows.astype(F32)
    return rows[:8] * 64.0 + rows[8:]


def faces_kernel(
    conc_in, side_in, order_in, ids_in,
    conc_ref, side_ref, order_ref, ids_ref, xm_ref, xp_ref, ym_ref, yp_ref, zm_ref, zp_ref, sems,
):
    pairs = (
        (ids_in, ids_ref), (order_in, order_ref), (conc_in, conc_ref), (side_in, side_ref),
    )
    copies = [pltpu.make_async_copy(a, b, sems.at[k]) for k, (a, b) in enumerate(pairs)]
    for copy in copies:
        copy.start()
    copies[0].wait()
    copies[1].wait()
    grains = lane_ids(ids_ref)
    packed = split_ids(grains)
    for ref in (xm_ref, xp_ref, ym_ref, yp_ref):
        ref[SLOTS] = packed
    zm_ref[16] = split_ids(jnp.broadcast_to(grains[:, 0:1], (8, LANES)))
    zp_ref[16] = split_ids(jnp.broadcast_to(grains[:, LANES - 1 :], (8, LANES)))
    lane = iota((16, LANES), 1)
    low = [jnp.zeros((16, LANES), F32)] * 16
    high = [jnp.zeros((16, LANES), F32)] * 16
    for slot in range(SLOTS):
        cells = order_ref[slot].astype(F32)
        xm_ref[slot] = order_ref[slot, 0]
        xp_ref[slot] = order_ref[slot, 15]
        ym_ref[slot] = cells[:, 0, :].astype(BF16)
        yp_ref[slot] = cells[:, 15, :].astype(BF16)
        for x in range(16):
            low[x] = jnp.where(lane == slot, cells[x, :, 0:1], low[x])
            high[x] = jnp.where(lane == slot, cells[x, :, LANES - 1 :], high[x])
    for x in range(16):
        zm_ref[x] = low[x].astype(BF16)
        zp_ref[x] = high[x].astype(BF16)
    copies[2].wait()
    copies[3].wait()


def square(x):
    return x * x


def mobility_kernel(
    conc_ref, side_ref, order_ref, ids_ref, xm_ref, xp_ref, ym_ref, yp_ref,
    own_ym_ref, own_yp_ref, own_zm_ref, own_zp_ref, mob_ref, zm_out, zp_out, work, weights,
):
    own = lane_ids(ids_ref)
    lane = iota((16, LANES), 1)
    row = iota((16, LANES), 0)
    last = lane % BRICK == BRICK - 1
    edge = (last | (lane % BRICK == 0)) & (lane != 0) & (lane != LANES - 1)

    lane8 = iota((8, LANES), 1)
    beside = jnp.where(
        lane8 % BRICK == BRICK - 1, roll(own, -BRICK, 1), roll(own, BRICK, 1)
    )
    for other in range(SLOTS):
        match = (own == beside[other : other + 1]).astype(F32)
        for slot in range(SLOTS):
            weights[slot * SLOTS + other] = jnp.broadcast_to(match[slot : slot + 1], (8, LANES))

    def across(face_ref, ids, center):
        facing = [face_ref[other].astype(F32) for other in range(SLOTS)]
        total = None
        for slot in range(SLOTS):
            value = None
            for other in range(SLOTS):
                match = (own[slot : slot + 1] == ids[other : other + 1]).astype(F32)
                term = match * facing[other]
                value = term if value is None else value + term
            part = square(value - center(slot))
            total = part if total is None else total + part
        return total

    def doubled(block):
        return jnp.concatenate([block, block], axis=0)

    def plane(x, carry_in):
        conc = conc_ref[x]
        base = 1.0 + 8.0 * square(conc * (1.0 - conc))
        along_y = jnp.zeros((16, LANES), F32)
        along_z = jnp.zeros((16, LANES), F32)
        along_x = jnp.zeros((16, LANES), F32)
        centers = []
        facing = []
        above = min(x + 1, 15)
        for slot in range(SLOTS):
            here = order_ref[slot, x].astype(F32)
            there = order_ref[slot, above].astype(F32)
            centers.append(here)
            along_x = along_x + square(there - here)
            along_y = along_y + square(roll(here, -1, 0) - here)
            right = roll(here, -1, 1)
            along_z = along_z + square(right - here)
            facing.append(jnp.where(last, right, roll(here, 1, 1)))
        along_y = jnp.where(row == 15, 0.0, along_y)
        along_z = jnp.where(last, 0.0, along_z)
        remapped = jnp.zeros((16, LANES), F32)
        for slot in range(SLOTS):
            value = None
            for other in range(SLOTS):
                term = doubled(weights[slot * SLOTS + other]) * facing[other]
                value = term if value is None else value + term
            remapped = remapped + square(value - centers[slot])
        total = base + along_y + roll(along_y, 1, 0) + along_z + roll(along_z, 1, 1)
        total = total + jnp.where(edge, remapped, 0.0) + along_x + carry_in
        work[x] = total
        return along_x

    carry = jnp.zeros((16, LANES), F32)
    for x in range(16):
        carry = plane(x, carry)
    work[0] = work[0] + across(
        xm_ref, join_ids(xm_ref[SLOTS]), lambda s: order_ref[s, 0].astype(F32)
    )
    work[15] = work[15] + across(
        xp_ref, join_ids(xp_ref[SLOTS]), lambda s: order_ref[s, 15].astype(F32)
    )
    bottom = across(ym_ref, join_ids(ym_ref[SLOTS]), lambda s: own_ym_ref[s].astype(F32))
    top = across(yp_ref, join_ids(yp_ref[SLOTS]), lambda s: own_yp_ref[s].astype(F32))
    for x in range(16):
        value = work[x]
        value = value + jnp.where(row == 0, bottom[x : x + 1], 0.0)
        value = value + jnp.where(row == 15, top[x : x + 1], 0.0)
        mob_ref[x] = value
        conc, side = conc_ref[x], side_ref[x]
        first = jnp.where(
            lane < 43, value, jnp.where(lane < 86, roll(conc, 43, 1), roll(side, 86, 1))
        )
        zm_out[x] = first.astype(BF16)
        final = jnp.where(
            lane >= 85, value, jnp.where(lane >= 42, roll(conc, -43, 1), roll(side, -86, 1))
        )
        zp_out[x] = final.astype(BF16)
    zm_out[16:] = own_zm_ref[...]
    zp_out[16:] = own_zp_ref[...]


def facing_squares(near_ref, far_ref, near_lane, far_lane):
    near = near_ref[:16].reshape(256, LANES)
    far = far_ref[:16].reshape(256, LANES)
    near_ids = join_ids(near_ref[16])
    far_ids = join_ids(far_ref[16])
    diagonal = iota((8, LANES), 0) == iota((8, LANES), 1)
    slots = iota((8, LANES), 1) < SLOTS

    def squares(cells, ids, others, other_ids, target):
        along = jnp.sum(jnp.where(diagonal, ids, 0.0), axis=0, keepdims=True)
        match = ((other_ids == along) & slots).astype(F32)
        match = jnp.concatenate([match, jnp.zeros((LANES - 8, LANES), F32)], axis=0)
        seen = jnp.dot(others, match.astype(BF16), preferred_element_type=F32)
        place = (iota((LANES, LANES), 1) == target).astype(F32)
        total = select_dot(square(seen - cells.astype(F32)), place)
        return total.reshape(16, 16, LANES)

    return (
        squares(near, near_ids, far, far_ids, near_lane),
        squares(far, far_ids, near, near_ids, far_lane),
    )


def split_kernel(
    mob_ref, conc_ref, side_ref, left_ref, right_ref, zm_ref, zp_ref,
    out_ref, keep_ref, down_ref, up_ref, low_ref, high_ref,
):
    own_low, far_low = facing_squares(zm_ref, left_ref.at[16:], 0, LANES - 1)
    own_high, far_high = facing_squares(zp_ref, right_ref.at[16:], LANES - 1, 0)
    mob = mob_ref[...] + own_low + own_high
    out_ref[...] = mob
    keep_ref[...] = mob
    down = (left_ref[:16].astype(F32) + far_low).astype(BF16)
    up = (right_ref[:16].astype(F32) + far_high).astype(BF16)
    down_ref[...] = down
    up_ref[...] = up
    for place, value in enumerate((mob, conc_ref[...], side_ref[...], down, up)):
        low_ref[place] = value[:, :8].astype(BF16)
        high_ref[place] = value[:, 8:].astype(BF16)


def rows_kernel(below_ref, low_ref, high_ref, above_ref, xl_ref, xh_ref):
    for place, ref in enumerate((below_ref, low_ref, high_ref, above_ref)):
        rows = pl.ds(8 * place, 8)
        xl_ref[:, :, rows, :] = ref[:, :8]
        xh_ref[:, :, rows, :] = ref[:, 8:]


def partner(x, step, axis):
    upper = (iota(x.shape, axis) & step) != 0
    return jnp.where(upper, roll(x, step, axis), roll(x, -step, axis))


def pair_sum(x, step, axis):
    return x + partner(x, step, axis)


def upper_of(x, step, axis):
    upper = (iota(x.shape, axis) & step) != 0
    return jnp.where(upper, x, roll(x, -step, axis))


def groups(items, size):
    items = list(items)
    return [items[k : k + size] for k in range(0, len(items), size)]


def sweep_planes(first, last, values, source, kx, ky, kz, step, use, size=8, planes=None):
    at = (lambda x: x) if planes is None else (lambda x: x % planes)
    before = kx[at(first - 1)] * (values[at(first)] - values[at(first - 1)])
    for xs in groups(range(first, last + 1), size):
        cells = [values[at(x)] for x in xs + [xs[-1] + 1]]
        flux_z = [kz[at(x)] * (roll(v, -step, 1) - v) for x, v in zip(xs, cells)]
        back_z = [roll(flux, step, 1) for flux in flux_z]
        left = []
        for k, x in enumerate(xs):
            value = cells[k]
            flux_x = kx[at(x)] * (cells[k + 1] - value)
            flux_y = ky[at(x)] * (roll(value, -step, 0) - value)
            total = (source[at(x)] - value) + (flux_x - before)
            total = total + (flux_y - roll(flux_y, step, 0))
            left.append(total + (flux_z[k] - back_z[k]))
            before = flux_x
        for k, x in enumerate(xs):
            use(at(x), cells[k], left[k])


def down_kernel(
    mob_in, conc_in, side_in, zm_ref, zp_ref, below_ref, above_ref, xm_ref, xp_ref,
    own_ref, chunk_ref, side_out, kx_out, ky_out, kz_out, wd_out, v_out,
    k1x_out, k1y_out, k1z_out, wd1_out, f1_out,
    mob, v0, res, v_ref, side_ref, kx_ref, ky_ref, kz_ref, wd_ref,
    f1_ref, k1x_ref, k1y_ref, k1z_ref, wd1_ref, e0, e1, r1, rows, sems,
):
    copies = []

    def store(source, target, planes):
        copy = pltpu.make_async_copy(source.at[planes], target.at[planes], sems.at[len(copies)])
        copy.start()
        copies.append(copy)

    lane = iota((32, LANES), 1)

    def own_plane(x, place, ref):
        parts = (below_ref[place, x], ref[x], above_ref[place, x])
        return jnp.concatenate([part.astype(F32) for part in parts], axis=0)

    own = (mob_in, conc_in, side_in, zm_ref, zp_ref)
    for xs in groups(range(32), 8):
        planes = []
        for x in xs:
            if 8 <= x < 24:
                parts = [own_plane(x - 8, place, ref) for place, ref in enumerate(own)]
            else:
                ref = xm_ref if x < 8 else xp_ref
                parts = [ref[place, x % 8].astype(F32) for place in range(5)]
            down, up = parts[3], parts[4]
            beyond = jnp.where(lane < 43, up, jnp.where(lane >= 85, down, 1.0))
            iterate = jnp.where(
                lane < 43, roll(up, -43, 1), jnp.where(lane >= 85, roll(down, 43, 1), 0.0)
            )
            right = jnp.where(
                lane < 42, roll(up, -86, 1), jnp.where(lane >= 86, roll(down, 86, 1), 0.0)
            )
            planes.append((parts, beyond, iterate, right))
        for x, (parts, beyond, iterate, right) in zip(xs, planes):
            mob[x, :, :LANES] = parts[0]
            v0[x, :, :LANES] = parts[1]
            side_ref[x, :, :LANES] = parts[2]
            mob[x, :, LANES:] = beyond
            v0[x, :, LANES:] = iterate
            side_ref[x, :, LANES:] = right

    half = TAU / 2

    before = half * (mob[1] + mob[2])
    kx_ref[1] = before
    for xs in groups(range(2, 30), 7):
        here = [mob[x] for x in xs + [xs[-1] + 1]]
        kz = [half * (cells + roll(cells, -1, 1)) for cells in here[:-1]]
        back = [roll(k, 1, 1) for k in kz]
        done = []
        for k, x in enumerate(xs):
            kx = half * (here[k] + here[k + 1])
            ky = half * (here[k] + roll(here[k], -1, 0))
            total = (kx + before) + (ky + roll(ky, 1, 0)) + (kz[k] + back[k])
            done.append((kx, ky, OMEGA / (1.0 + total)))
            before = kx
        for k, x in enumerate(xs):
            kx_ref[x], ky_ref[x], wd_ref[x] = done[k]
            kz_ref[x] = kz[k]

    store(side_ref, side_out, FINE_PLANES)
    store(kx_ref, kx_out, FINE_PLANES)
    store(ky_ref, ky_out, FINE_PLANES)
    store(kz_ref, kz_out, FINE_PLANES)
    store(wd_ref, wd_out, FINE_PLANES)

    def smooth(target, weight):
        def use(x, value, left):
            target[x] = value + weight[x] * left

        return use

    sweep_planes(2, 29, v0, side_ref, kx_ref, ky_ref, kz_ref, 1, smooth(res, wd_ref))
    sweep_planes(3, 28, res, side_ref, kx_ref, ky_ref, kz_ref, 1, smooth(v_ref, wd_ref))

    store(v_ref, v_out, FINE_PLANES)

    def keep(x, value, left):
        res[x] = left

    sweep_planes(4, 27, v_ref, side_ref, kx_ref, ky_ref, kz_ref, 1, keep)

    def pool(x):
        return pair_sum(pair_sum(x, 1, 0), 1, 1)

    for xs in groups(range(1, 14), 7):
        done = [pool(kx_ref[2 * i + 1]) * (1.0 / 16.0) for i in xs]
        for i, value in zip(xs, done):
            k1x_ref[i] = value
    for ref in (f1_ref, k1y_ref, k1z_ref, wd1_ref):
        ref[1] = jnp.zeros((32, RING), F32)
    for xs in groups(range(2, 14), 6):
        done = []
        for i in xs:
            x = 2 * i
            f1 = pool(res[x] + res[x + 1]) * 0.125
            along_y = pair_sum(ky_ref[x] + ky_ref[x + 1], 1, 1)
            k1y = upper_of(along_y, 1, 0) * (1.0 / 16.0)
            along_z = pair_sum(kz_ref[x] + kz_ref[x + 1], 1, 0)
            k1z = upper_of(along_z, 1, 1) * (1.0 / 16.0)
            total = k1x_ref[i] + k1x_ref[i - 1]
            total = total + (k1y + roll(k1y, 2, 0)) + (k1z + roll(k1z, 2, 1))
            weight = OMEGA / (1.0 + total)
            done.append((f1, k1y, k1z, weight, weight * f1))
        for i, value in zip(xs, done):
            f1_ref[i], k1y_ref[i], k1z_ref[i], wd1_ref[i], e0[i] = value
    store(k1x_ref, k1x_out, MIDDLE_PLANES)
    store(k1y_ref, k1y_out, MIDDLE_PLANES)
    store(k1z_ref, k1z_out, MIDDLE_PLANES)
    store(wd1_ref, wd1_out, MIDDLE_PLANES)
    store(f1_ref, f1_out, MIDDLE_PLANES)
    sweep_planes(3, 12, e0, f1_ref, k1x_ref, k1y_ref, k1z_ref, 2, smooth(e1, wd1_ref))

    def keep_middle(x, value, left):
        r1[x] = left

    sweep_planes(4, 11, e1, f1_ref, k1x_ref, k1y_ref, k1z_ref, 2, keep_middle)

    src = iota((RING, LANES), 0)
    dst = iota((RING, LANES), 1)
    cell = jnp.where(src < 192, src, src - RING)
    coarse = (cell + 4 * COARSE_LOW) // 4
    there = ((cell & 3) == 0) & (coarse >= 0) & (coarse < COARSE)
    head = there & (coarse < HEAD)
    tail = there & (coarse >= HEAD)
    sides = [there & (coarse == dst), there & (coarse + COARSE == dst)]
    picks0 = sides + [head & (coarse + 2 * COARSE == dst)]
    picks1 = sides + [tail & (coarse + 2 * COARSE - HEAD == dst)]
    picks0 = jnp.concatenate([pick.astype(F32) for pick in picks0], axis=0).astype(BF16)
    picks1 = jnp.concatenate([pick.astype(F32) for pick in picks1], axis=0).astype(BF16)
    pick_middle = ((cell == 2 * (dst - MIDDLE_LOW)) & (dst < MIDDLE)).astype(F32)
    firsts = []
    seconds = []
    for j in range(4):
        i = 4 + 2 * j
        f2 = pair_sum(pair_sum(r1[i] + r1[i + 1], 2, 0), 2, 1) * 0.125
        k2x = pair_sum(pair_sum(k1x_ref[i + 1], 2, 0), 2, 1) * (1.0 / 16.0)
        k2y = pair_sum(k1y_ref[i] + k1y_ref[i + 1], 2, 1)
        k2y = upper_of(k2y, 2, 0) * (1.0 / 16.0)
        k2z = pair_sum(k1z_ref[i] + k1z_ref[i + 1], 2, 0)
        k2z = upper_of(k2z, 2, 1) * (1.0 / 16.0)
        f2, k2x, k2y, k2z = (cells[8:24] for cells in (f2, k2x, k2y, k2z))
        k2z = k2z.astype(BF16)
        high = f2.astype(BF16)
        low = (f2 - high.astype(F32)).astype(BF16)
        firsts.append(jnp.concatenate([high, low, k2z], axis=1))
        seconds.append(jnp.concatenate([k2x.astype(BF16), k2y.astype(BF16), k2z], axis=1))
    firsts = jnp.concatenate(firsts, axis=0)
    seconds = jnp.concatenate(seconds, axis=0)
    rows[pl.ds(0, 64), :] = jnp.dot(firsts, picks0, preferred_element_type=F32)
    rows[pl.ds(64, 64), :] = jnp.dot(seconds, picks1, preferred_element_type=F32)
    coarse = rows[pl.ds(0, 32, stride=4), :]
    rows[...] = select_dot(
        jnp.concatenate([e1[4 + i, 8:24] for i in range(8)], axis=0), pick_middle
    )
    middle = rows[pl.ds(0, 64, stride=2), :]
    own_ref[...] = middle
    chunk = jnp.concatenate([coarse.astype(BF16), middle.astype(BF16)], axis=0)
    for k in range(32):
        chunk_ref[k] = chunk
    for copy in copies:
        copy.wait()


def up_kernel(
    place_ref, all_ref, own_ref, side_in, kx_in, ky_in, kz_in, wd_in, v_in,
    k1x_in, k1y_in, k1z_in, wd1_in, f1_in,
    out_ref,
    side_ref, kx_ref, ky_ref, kz_ref, wd_ref, v_ref, k1x_ref, k1y_ref, k1z_ref, wd1_ref, f1_ref,
    pair0, pair1, c2x, c2y, c2z, wd2, f2, ea, eb, mid, tall, lean, e1a, e1b, va, vb, sems,
):
    copies = []
    for planes, moves in (
        (MIDDLE_PLANES, (
            (k1x_in, k1x_ref), (k1y_in, k1y_ref), (k1z_in, k1z_ref), (wd1_in, wd1_ref),
            (f1_in, f1_ref),
        )),
        (FINE_PLANES, (
            (v_in, v_ref), (side_in, side_ref), (kx_in, kx_ref), (ky_in, ky_ref),
            (kz_in, kz_ref), (wd_in, wd_ref),
        )),
    ):
        for a, b in moves:
            copies.append(
                pltpu.make_async_copy(a.at[planes], b.at[planes], sems.at[len(copies)])
            )
    for copy in copies:
        copy.start()
    gx = place_ref[0]
    gy = place_ref[1]

    def source(dx, dy):
        return ((gx + dx + 8) & 7) * 4 + ((gy + dy + 4) & 3)

    for p in (0, 1, 2, 3, 4, 6, 7):
        for q in range(4):
            s = source(p - 1, q - 1)
            first = all_ref[s, pl.ds(0, 16), :].astype(F32)
            second = all_ref[s, pl.ds(16, 16), :].astype(F32)
            for i in range(4):
                pair0[4 * p + i, pl.ds(4 * q, 4), :] = first[4 * i : 4 * i + 4]
                pair1[4 * p + i, pl.ds(4 * q, 4), :] = second[4 * i : 4 * i + 4]
    for p in (-1, 0, 1):
        for q in (-1, 0, 1):
            if p == 0 and q == 0:
                cells = own_ref[...]
            else:
                cells = all_ref[source(p, q), pl.ds(32, 64), :].astype(F32)
            for i in range(1, 15):
                if (i - 4) // 8 != p:
                    continue
                start = 8 * ((i - 4) % 8)
                block = cells[start : start + 8]
                if q == -1:
                    mid[i, pl.ds(0, 4), :] = block[4:]
                elif q == 0:
                    mid[i, pl.ds(4, 8), :] = block
                else:
                    mid[i, pl.ds(12, 4), :] = block[:4]

    used = iota((16, LANES), 1) < COARSE
    head = iota((16, LANES), 1) < HEAD
    for x in range(-6, 17):
        k = x % 32
        first = pair0[k]
        second = pair1[k]
        f2[k] = jnp.where(used, first + roll(first, -COARSE, 1), 0.0)
        c2x[k] = jnp.where(used, second, 0.0)
        c2y[k] = jnp.where(used, roll(second, -COARSE, 1), 0.0)
        last = jnp.where(
            head, roll(first, -2 * COARSE, 1), roll(second, HEAD - 2 * COARSE, 1)
        )
        c2z[k] = jnp.where(used, last, 0.0)
    for xs in groups(range(-5, 17), 11):
        done = []
        for x in xs:
            k = x % 32
            ky = c2y[k]
            kz = c2z[k]
            total = c2x[k] + c2x[(x - 1) % 32]
            total = total + (ky + roll(ky, 1, 0)) + (kz + roll(kz, 1, 1))
            weight = OMEGA / (1.0 + total)
            done.append((weight, weight * f2[k]))
        for x, value in zip(xs, done):
            wd2[x % 32], ea[x % 32] = value

    def smooth(target, weight):
        def use(x, value, left):
            target[x] = value + weight[x] * left

        return use

    old, new = ea, eb
    for reach in range(6, -1, -1):
        sweep_planes(
            2 - reach, 9 + reach, old, f2, c2x, c2y, c2z, 1, smooth(new, wd2), 10, 32
        )
        old, new = new, old

    lane = iota((8, LANES), 1)
    for j in range(8):
        line = roll(old[2 + j, pl.ds(2, 8), :], MIDDLE, 1)
        line = jnp.where((lane >= MIDDLE) & (lane < MIDDLE + COARSE), line, 0.0)
        for k in range(4):
            lean[j, pl.ds(k, 8, stride=4), :] = line
    for i in range(1, 15):
        line = mid[i]
        for k in range(2):
            tall[i, pl.ds(k, 16, stride=2), :] = line
    src = iota((LANES, RING), 0)
    dst = iota((LANES, RING), 1)
    cell = jnp.where(dst < 192, dst, dst - RING)
    middle = (cell >= -2 * MIDDLE_LOW) & (src < MIDDLE)
    middle = middle & ((cell + 2 * MIDDLE_LOW) // 2 == src)
    coarse = (cell >= -4 * COARSE_LOW) & (src >= MIDDLE) & (src < MIDDLE + COARSE)
    coarse = coarse & ((cell + 4 * COARSE_LOW) // 4 == src - MIDDLE)
    spread = (middle | coarse).astype(F32)
    narrow = iota((32, LANES), 1) < MIDDLE
    packed = [jnp.where(narrow, tall[i], lean[i // 2]) for i in range(1, 15)]
    widened = select_dot(jnp.concatenate(packed, axis=0), spread)
    for i in range(1, 15):
        e1a[i] = widened[32 * (i - 1) : 32 * i]

    for copy in copies:
        copy.wait()
    sweep_planes(2, 13, e1a, f1_ref, k1x_ref, k1y_ref, k1z_ref, 2, smooth(e1b, wd1_ref))
    sweep_planes(3, 12, e1b, f1_ref, k1x_ref, k1y_ref, k1z_ref, 2, smooth(e1a, wd1_ref))
    for x in range(6, 26):
        va[x] = v_ref[x] + e1a[x // 2]
    sweep_planes(7, 24, va, side_ref, kx_ref, ky_ref, kz_ref, 1, smooth(vb, wd_ref))

    def finish(x, value, left):
        new = value + wd_ref[x] * left
        out_ref[x - 8] = new[8:24, :LANES]

    sweep_planes(8, 23, vb, side_ref, kx_ref, ky_ref, kz_ref, 1, finish)


def shift(x, axis, direction):
    count = lax.axis_size(axis)
    return lax.ppermute(x, axis, [(i, (i + direction) % count) for i in range(count)])


def body(conc, right_side, order_field, grain_ids):
    face = ((9, 16, LANES), BF16)
    zface = ((17, 16, LANES), BF16)
    brick = ((16, 16, LANES), F32)
    conc, side, order, ids, xm, xp, ym, yp, zm, zp = call(
        faces_kernel,
        [brick, brick, ((8, 16, 16, LANES), BF16), ((1, 1, 8, 8), jnp.int32)]
        + [face] * 4
        + [zface] * 2,
        (conc, right_side, order_field, grain_ids),
        specs=[HBM] * 4,
        semaphores=4,
    )
    faces = (
        shift(xp, "gx", 1), shift(xm, "gx", -1),
        shift(yp, "gy", 1), shift(ym, "gy", -1),
    )
    pack = ((16, 16, LANES), BF16)
    partial, send_zm, send_zp = call(
        mobility_kernel,
        [brick, ((33, 16, LANES), BF16), ((33, 16, LANES), BF16)],
        (conc, side, order, ids) + faces + (ym, yp, zm, zp),
        scratch=[brick, ((64, 8, LANES), F32)],
    )
    left = shift(send_zp, "gz", 1)
    right = shift(send_zm, "gz", -1)
    half = ((5, 16, 8, LANES), BF16)
    mobility, keep, left, right, low, high = call(
        split_kernel,
        [brick, brick, pack, pack, half, half],
        (partial, conc, side, left, right, zm, zp),
    )
    below = shift(high, "gy", 1)
    above = shift(low, "gy", -1)
    slab = ((5, 8, 32, LANES), BF16)
    xl, xh = call(rows_kernel, [slab, slab], (below, low, high, above))
    before = shift(xh, "gx", 1)
    after = shift(xl, "gx", -1)
    fine = ((32, 32, RING), F32)
    middle = ((16, 32, RING), F32)
    own, chunk, *kept = call(
        down_kernel,
        [((64, LANES), F32), ((32, CHUNK, LANES), BF16)] + [fine] * 6 + [middle] * 5,
        (keep, conc, side, left, right, below, above, before, after),
        scratch=[fine] * 9 + [middle] * 8 + [((LANES, LANES), F32)],
        places=[VMEM] * 2 + [HBM] * 11,
        limit=24,
        semaphores=11,
    )
    place = jnp.stack([lax.axis_index("gx"), lax.axis_index("gy")]).astype(jnp.int32)
    chunk, place = lax.optimization_barrier((chunk, place))
    chunks = lax.all_to_all(chunk, ("gx", "gy"), 0, 0, tiled=True)
    plane = ((32, 16, LANES), F32)
    (out,) = call(
        up_kernel,
        [brick],
        (place, chunks, own) + tuple(kept),
        scratch=[fine] * 6
        + [middle] * 5
        + [plane] * 9
        + [brick, ((16, 32, LANES), F32), ((8, 32, LANES), F32)]
        + [middle] * 2
        + [fine] * 2,
        specs=[SMEM] + [VMEM] * 2 + [HBM] * 11,
        limit=24,
        semaphores=11,
    )
    return out, mobility


def solution(mesh):
    return jax.shard_map(
        body,
        mesh=mesh,
        in_specs=(
            P("gx", "gy", "gz"),
            P("gx", "gy", "gz"),
            P(None, "gx", "gy", "gz"),
            P("gx", "gy", "gz", None),
        ),
        out_specs=(P("gx", "gy", "gz"), P("gx", "gy", "gz")),
        check_vma=False,
    )
```

```python
import functools

import jax
import jax.numpy as jnp
from jax import lax
from jax.experimental import pallas as pl
from jax.experimental.pallas import tpu as pltpu
from jax.sharding import PartitionSpec as P

SLOTS = 8
BRICK = 16
OMEGA = 0.8
TAU = 256.0
LANES = 128
RING = 256
F32 = jnp.float32
BF16 = jnp.bfloat16
HIGH = lax.Precision.HIGHEST
VMEM = pl.BlockSpec(memory_space=pltpu.VMEM)
HBM = pl.BlockSpec(memory_space=pltpu.MemorySpace.HBM)
SMEM = pl.BlockSpec(memory_space=pltpu.SMEM)
COARSE = 51
COARSE_LOW = 10
MIDDLE = 70
HEAD = 26
CHUNK = 64
FINE_PLANES = pl.ds(6, 20)
MIDDLE_PLANES = pl.ds(1, 13)


def call(kernel, outs, args, scratch=(), specs=None, places=None, limit=16, semaphores=0):
    specs = specs or [VMEM] * len(args)
    places = places or [VMEM] * len(outs)
    args = [
        pltpu.with_memory_space_constraint(arg, pltpu.MemorySpace.HBM) if spec is HBM else arg
        for arg, spec in zip(args, specs)
    ]
    scratches = [pltpu.VMEM(shape, dtype) for shape, dtype in scratch]
    if semaphores:
        scratches.append(pltpu.SemaphoreType.DMA((semaphores,)))
    return pl.pallas_call(
        kernel,
        out_shape=[
            pltpu.MemorySpace.HBM(*out) if place is HBM else jax.ShapeDtypeStruct(*out)
            for out, place in zip(outs, places)
        ],
        in_specs=specs,
        out_specs=places,
        scratch_shapes=scratches,
        compiler_params=pltpu.CompilerParams(vmem_limit_bytes=limit << 20),
    )(*args)


def roll(x, shift, axis):
    return pltpu.roll(x, shift % x.shape[axis], axis)


def iota(shape, axis):
    return lax.broadcasted_iota(jnp.int32, shape, axis)


def select_dot(a, picks):
    picks = picks.astype(BF16)
    total = None
    for _ in range(3):
        part = a.astype(BF16)
        a = a - part.astype(F32)
        term = jnp.dot(part, picks, preferred_element_type=F32)
        total = term if total is None else total + term
    return total


def lane_ids(ids_ref):
    ids = ids_ref[0, 0].astype(F32)
    spread = (iota((8, LANES), 1) // BRICK == iota((8, LANES), 0)).astype(F32)
    grains = lax.dot_general(
        ids, spread, (((0,), (0,)), ((), ())), precision=HIGH, preferred_element_type=F32
    )
    return jnp.floor(grains + 0.5)


def split_ids(grains):
    high = jnp.floor(grains * (1.0 / 64.0))
    return jnp.concatenate([high, grains - 64.0 * high], axis=0).astype(BF16)


def join_ids(rows):
    rows = rows.astype(F32)
    return rows[:8] * 64.0 + rows[8:]


def faces_kernel(
    conc_in, side_in, order_in, ids_in,
    conc_ref, side_ref, order_ref, ids_ref, xm_ref, xp_ref, ym_ref, yp_ref, zm_ref, zp_ref, sems,
):
    pairs = (
        (ids_in, ids_ref), (order_in, order_ref), (conc_in, conc_ref), (side_in, side_ref),
    )
    copies = [pltpu.make_async_copy(a, b, sems.at[k]) for k, (a, b) in enumerate(pairs)]
    for copy in copies:
        copy.start()
    copies[0].wait()
    copies[1].wait()
    grains = lane_ids(ids_ref)
    packed = split_ids(grains)
    for ref in (xm_ref, xp_ref, ym_ref, yp_ref):
        ref[SLOTS] = packed
    zm_ref[16] = split_ids(jnp.broadcast_to(grains[:, 0:1], (8, LANES)))
    zp_ref[16] = split_ids(jnp.broadcast_to(grains[:, LANES - 1 :], (8, LANES)))
    lane = iota((16, LANES), 1)
    low = [jnp.zeros((16, LANES), F32)] * 16
    high = [jnp.zeros((16, LANES), F32)] * 16
    for slot in range(SLOTS):
        cells = order_ref[slot].astype(F32)
        xm_ref[slot] = order_ref[slot, 0]
        xp_ref[slot] = order_ref[slot, 15]
        ym_ref[slot] = cells[:, 0, :].astype(BF16)
        yp_ref[slot] = cells[:, 15, :].astype(BF16)
        for x in range(16):
            low[x] = jnp.where(lane == slot, cells[x, :, 0:1], low[x])
            high[x] = jnp.where(lane == slot, cells[x, :, LANES - 1 :], high[x])
    for x in range(16):
        zm_ref[x] = low[x].astype(BF16)
        zp_ref[x] = high[x].astype(BF16)
    copies[2].wait()
    copies[3].wait()


def square(x):
    return x * x


def mobility_kernel(
    conc_ref, side_ref, order_ref, ids_ref, xm_ref, xp_ref, yp_ref,
    own_yp_ref, own_zm_ref, own_zp_ref, mob_ref, beyond_ref, zm_out, zp_out, work, weights,
):
    own = lane_ids(ids_ref)
    lane = iota((16, LANES), 1)
    row = iota((16, LANES), 0)
    last = lane % BRICK == BRICK - 1
    edge = (last | (lane % BRICK == 0)) & (lane != 0) & (lane != LANES - 1)

    lane8 = iota((8, LANES), 1)
    beside = jnp.where(
        lane8 % BRICK == BRICK - 1, roll(own, -BRICK, 1), roll(own, BRICK, 1)
    )
    for other in range(SLOTS):
        match = (own == beside[other : other + 1]).astype(F32)
        for slot in range(SLOTS):
            weights[slot * SLOTS + other] = jnp.broadcast_to(match[slot : slot + 1], (8, LANES))

    def across(center, ids, facing, facing_ids):
        facing = [facing(other).astype(F32) for other in range(SLOTS)]
        total = None
        for slot in range(SLOTS):
            value = None
            for other in range(SLOTS):
                match = ids[slot : slot + 1] == facing_ids[other : other + 1]
                term = match.astype(F32) * facing[other]
                value = term if value is None else value + term
            part = square(value - center(slot).astype(F32))
            total = part if total is None else total + part
        return total

    def doubled(block):
        return jnp.concatenate([block, block], axis=0)

    def plane(x, carry_in):
        conc = conc_ref[x]
        base = 1.0 + 8.0 * square(conc * (1.0 - conc))
        along_y = jnp.zeros((16, LANES), F32)
        along_z = jnp.zeros((16, LANES), F32)
        along_x = jnp.zeros((16, LANES), F32)
        centers = []
        facing = []
        above = min(x + 1, 15)
        for slot in range(SLOTS):
            here = order_ref[slot, x].astype(F32)
            there = order_ref[slot, above].astype(F32)
            centers.append(here)
            along_x = along_x + square(there - here)
            along_y = along_y + square(roll(here, -1, 0) - here)
            right = roll(here, -1, 1)
            along_z = along_z + square(right - here)
            facing.append(jnp.where(last, right, roll(here, 1, 1)))
        along_y = jnp.where(row == 15, 0.0, along_y)
        along_z = jnp.where(last, 0.0, along_z)
        remapped = jnp.zeros((16, LANES), F32)
        for slot in range(SLOTS):
            value = None
            for other in range(SLOTS):
                term = doubled(weights[slot * SLOTS + other]) * facing[other]
                value = term if value is None else value + term
            remapped = remapped + square(value - centers[slot])
        total = base + along_y + roll(along_y, 1, 0) + along_z + roll(along_z, 1, 1)
        total = total + jnp.where(edge, remapped, 0.0) + along_x + carry_in
        work[x] = total
        return along_x

    carry = jnp.zeros((16, LANES), F32)
    for x in range(16):
        carry = plane(x, carry)
    work[0] = work[0] + across(
        lambda k: order_ref[k, 0], own, lambda k: xm_ref[k], join_ids(xm_ref[SLOTS])
    )
    work[15] = work[15] + across(
        lambda k: order_ref[k, 15], own, lambda k: xp_ref[k], join_ids(xp_ref[SLOTS])
    )
    above_ids = join_ids(yp_ref[SLOTS])
    top = across(lambda k: own_yp_ref[k], own, lambda k: yp_ref[k], above_ids)
    beyond = across(lambda k: yp_ref[k], above_ids, lambda k: own_yp_ref[k], own)
    beyond_ref[...] = beyond
    zm_out[33] = beyond.astype(BF16)
    zp_out[33] = beyond.astype(BF16)
    for x in range(16):
        value = work[x]
        value = value + jnp.where(row == 15, top[x : x + 1], 0.0)
        mob_ref[x] = value
        conc, side = conc_ref[x], side_ref[x]
        first = jnp.where(
            lane < 43, value, jnp.where(lane < 86, roll(conc, 43, 1), roll(side, 86, 1))
        )
        zm_out[x] = first.astype(BF16)
        final = jnp.where(
            lane >= 85, value, jnp.where(lane >= 42, roll(conc, -43, 1), roll(side, -86, 1))
        )
        zp_out[x] = final.astype(BF16)
    zm_out[16:33] = own_zm_ref[...]
    zp_out[16:33] = own_zp_ref[...]


def facing_squares(near_ref, far_ref, near_lane, far_lane):
    near = near_ref[:16].reshape(256, LANES)
    far = far_ref[:16].reshape(256, LANES)
    near_ids = join_ids(near_ref[16])
    far_ids = join_ids(far_ref[16])
    diagonal = iota((8, LANES), 0) == iota((8, LANES), 1)
    slots = iota((8, LANES), 1) < SLOTS

    def squares(cells, ids, others, other_ids, target):
        along = jnp.sum(jnp.where(diagonal, ids, 0.0), axis=0, keepdims=True)
        match = ((other_ids == along) & slots).astype(F32)
        match = jnp.concatenate([match, jnp.zeros((LANES - 8, LANES), F32)], axis=0)
        seen = jnp.dot(others, match.astype(BF16), preferred_element_type=F32)
        place = (iota((LANES, LANES), 1) == target).astype(F32)
        total = select_dot(square(seen - cells.astype(F32)), place)
        return total.reshape(16, 16, LANES)

    return (
        squares(near, near_ids, far, far_ids, near_lane),
        squares(far, far_ids, near, near_ids, far_lane),
    )


def split_kernel(
    mob_ref, conc_ref, side_ref, beyond_ref, left_ref, right_ref, zm_ref, zp_ref,
    keep_ref, beside_ref, low_ref, high_ref,
):
    own_low, far_low = facing_squares(zm_ref, left_ref.at[16:33], 0, LANES - 1)
    own_high, far_high = facing_squares(zp_ref, right_ref.at[16:33], LANES - 1, 0)
    mob = mob_ref[...] + own_low + own_high
    keep_ref[...] = mob
    down = (left_ref[:16].astype(F32) + far_low).astype(BF16)
    up = (right_ref[:16].astype(F32) + far_high).astype(BF16)
    for place, value in enumerate((mob, conc_ref[...], side_ref[...], down, up)):
        planes = pl.ds(16 * place, 16)
        low_ref[planes] = value[:, :8].astype(BF16)
        high_ref[planes] = value[:, 8:].astype(BF16)
    lane = iota((16, LANES), 1)
    down, up = left_ref[33].astype(F32), right_ref[33].astype(F32)
    beside = jnp.where(lane < 43, up, jnp.where(lane >= 85, down, 0.0))
    beside_ref[...] = beside
    beyond = beyond_ref[...]
    high = beyond.astype(BF16)
    rest = (beyond - high.astype(F32)).astype(BF16)
    for k, value in enumerate((high, rest, beside.astype(BF16))):
        high_ref[80 + 2 * k] = value[:8]
        high_ref[81 + 2 * k] = value[8:]


def rows_kernel(
    below_ref, low_ref, high_ref, above_ref, mob_ref, beyond_ref, beside_ref,
    out_ref, keep_ref, xl_ref, xh_ref,
):
    lane = iota((8, LANES), 1)
    first = iota((8, LANES), 0) == 0
    got = [
        jnp.concatenate([below_ref[80 + 2 * k], below_ref[81 + 2 * k]], axis=0).astype(F32)
        for k in range(3)
    ]
    missing = ((got[0] + got[1], got[2]), (beyond_ref[...], beside_ref[...]))
    for x in range(16):
        ref = xl_ref if x < 8 else xh_ref
        lines = []
        for main, beside in missing:
            main = jnp.where(first, main[x : x + 1], 0.0)
            beside = jnp.where(first, beside[x : x + 1], 0.0)
            down = jnp.where(lane >= 85, beside, 0.0)
            lines.append((main, None, None, down, jnp.where(lane < 43, beside, 0.0)))
        own = mob_ref[x, :8] + lines[0][0]
        for out in (out_ref, keep_ref):
            out[x, :8] = own
            out[x, 8:] = mob_ref[x, 8:]
        for place in range(5):
            plane = 16 * place + x
            near, far = low_ref[plane], above_ref[plane]
            if place == 0:
                near = own.astype(BF16)
            elif place >= 3:
                near = (near.astype(F32) + lines[0][place]).astype(BF16)
            if place in (0, 3, 4):
                far = (far.astype(F32) + lines[1][place]).astype(BF16)
            for k, value in enumerate((below_ref[plane], near, high_ref[plane], far)):
                ref[place, x % 8, pl.ds(8 * k, 8), :] = value


def partner(x, step, axis):
    upper = (iota(x.shape, axis) & step) != 0
    return jnp.where(upper, roll(x, step, axis), roll(x, -step, axis))


def pair_sum(x, step, axis):
    return x + partner(x, step, axis)


def upper_of(x, step, axis):
    upper = (iota(x.shape, axis) & step) != 0
    return jnp.where(upper, x, roll(x, -step, axis))


def middle_cell(lane):
    cell = lane
    for place, end in enumerate((-2, -1, 64, 65, -3, 66)):
        cell = jnp.where(lane == 64 + place, end, cell)
    return cell


def groups(items, size):
    items = list(items)
    return [items[k : k + size] for k in range(0, len(items), size)]


def sweep_planes(first, last, values, source, kx, ky, kz, step, use, size=8, planes=None):
    at = (lambda x: x) if planes is None else (lambda x: x % planes)
    before = kx[at(first - 1)] * (values[at(first)] - values[at(first - 1)])
    for xs in groups(range(first, last + 1), size):
        cells = [values[at(x)] for x in xs + [xs[-1] + 1]]
        flux_z = [kz[at(x)] * (roll(v, -step, 1) - v) for x, v in zip(xs, cells)]
        back_z = [roll(flux, step, 1) for flux in flux_z]
        left = []
        for k, x in enumerate(xs):
            value = cells[k]
            flux_x = kx[at(x)] * (cells[k + 1] - value)
            flux_y = ky[at(x)] * (roll(value, -step, 0) - value)
            total = (source[at(x)] - value) + (flux_x - before)
            total = total + (flux_y - roll(flux_y, step, 0))
            left.append(total + (flux_z[k] - back_z[k]))
            before = flux_x
        for k, x in enumerate(xs):
            use(at(x), cells[k], left[k])


def down_kernel(
    mob_in, conc_in, side_in, xl_ref, xh_ref, xm_ref, xp_ref,
    own_ref, chunk_ref, side_out, kx_out, ky_out, kz_out, wd_out, v_out,
    k1x_out, k1y_out, k1z_out, wd1_out, f1_out,
    mob, v0, res, v_ref, side_ref, kx_ref, ky_ref, kz_ref, wd_ref,
    f1_ref, k1x_ref, k1y_ref, k1z_ref, wd1_ref, e0, e1, r1, rows, sems,
):
    copies = []

    def store(source, target, planes):
        copy = pltpu.make_async_copy(source.at[planes], target.at[planes], sems.at[len(copies)])
        copy.start()
        copies.append(copy)

    lane = iota((32, LANES), 1)

    own = (mob_in, conc_in, side_in)
    slabs = (xm_ref, xl_ref, xh_ref, xp_ref)
    for xs in groups(range(32), 8):
        planes = []
        for x in xs:
            parts = [slabs[x // 8][place, x % 8].astype(F32) for place in range(5)]
            if 8 <= x < 24:
                for place in range(3):
                    part = parts[place]
                    part = [part[:8], own[place][x - 8], part[24:]]
                    parts[place] = jnp.concatenate(part, axis=0)
            down, up = parts[3], parts[4]
            beyond = jnp.where(lane < 43, up, jnp.where(lane >= 85, down, 1.0))
            iterate = jnp.where(
                lane < 43, roll(up, -43, 1), jnp.where(lane >= 85, roll(down, 43, 1), 0.0)
            )
            right = jnp.where(
                lane < 42, roll(up, -86, 1), jnp.where(lane >= 86, roll(down, 86, 1), 0.0)
            )
            planes.append((parts, beyond, iterate, right))
        for x, (parts, beyond, iterate, right) in zip(xs, planes):
            mob[x, :, :LANES] = parts[0]
            v0[x, :, :LANES] = parts[1]
            side_ref[x, :, :LANES] = parts[2]
            mob[x, :, LANES:] = beyond
            v0[x, :, LANES:] = iterate
            side_ref[x, :, LANES:] = right

    half = TAU / 2

    before = half * (mob[1] + mob[2])
    kx_ref[1] = before
    for xs in groups(range(2, 30), 7):
        here = [mob[x] for x in xs + [xs[-1] + 1]]
        kz = [half * (cells + roll(cells, -1, 1)) for cells in here[:-1]]
        back = [roll(k, 1, 1) for k in kz]
        done = []
        for k, x in enumerate(xs):
            kx = half * (here[k] + here[k + 1])
            ky = half * (here[k] + roll(here[k], -1, 0))
            total = (kx + before) + (ky + roll(ky, 1, 0)) + (kz[k] + back[k])
            done.append((kx, ky, OMEGA / (1.0 + total)))
            before = kx
        for k, x in enumerate(xs):
            kx_ref[x], ky_ref[x], wd_ref[x] = done[k]
            kz_ref[x] = kz[k]

    store(side_ref, side_out, FINE_PLANES)
    store(kx_ref, kx_out, FINE_PLANES)
    store(ky_ref, ky_out, FINE_PLANES)
    store(kz_ref, kz_out, FINE_PLANES)
    store(wd_ref, wd_out, FINE_PLANES)

    def smooth(target, weight):
        def use(x, value, left):
            target[x] = value + weight[x] * left

        return use

    sweep_planes(2, 29, v0, side_ref, kx_ref, ky_ref, kz_ref, 1, smooth(res, wd_ref))
    sweep_planes(3, 28, res, side_ref, kx_ref, ky_ref, kz_ref, 1, smooth(v_ref, wd_ref))

    store(v_ref, v_out, FINE_PLANES)

    def keep(x, value, left):
        res[x] = left

    sweep_planes(4, 27, v_ref, side_ref, kx_ref, ky_ref, kz_ref, 1, keep)

    def pool(x):
        return pair_sum(pair_sum(x, 1, 0), 1, 1)

    for xs in groups(range(1, 14), 7):
        done = [pool(kx_ref[2 * i + 1]) * (1.0 / 16.0) for i in xs]
        for i, value in zip(xs, done):
            k1x_ref[i] = value
    for ref in (f1_ref, k1y_ref, k1z_ref, wd1_ref):
        ref[1] = jnp.zeros((32, RING), F32)
    for xs in groups(range(2, 14), 6):
        done = []
        for i in xs:
            x = 2 * i
            f1 = pool(res[x] + res[x + 1]) * 0.125
            along_y = pair_sum(ky_ref[x] + ky_ref[x + 1], 1, 1)
            k1y = upper_of(along_y, 1, 0) * (1.0 / 16.0)
            along_z = pair_sum(kz_ref[x] + kz_ref[x + 1], 1, 0)
            k1z = upper_of(along_z, 1, 1) * (1.0 / 16.0)
            total = k1x_ref[i] + k1x_ref[i - 1]
            total = total + (k1y + roll(k1y, 2, 0)) + (k1z + roll(k1z, 2, 1))
            weight = OMEGA / (1.0 + total)
            done.append((f1, k1y, k1z, weight, weight * f1))
        for i, value in zip(xs, done):
            f1_ref[i], k1y_ref[i], k1z_ref[i], wd1_ref[i], e0[i] = value
    store(k1x_ref, k1x_out, MIDDLE_PLANES)
    store(k1y_ref, k1y_out, MIDDLE_PLANES)
    store(k1z_ref, k1z_out, MIDDLE_PLANES)
    store(wd1_ref, wd1_out, MIDDLE_PLANES)
    store(f1_ref, f1_out, MIDDLE_PLANES)
    sweep_planes(3, 12, e0, f1_ref, k1x_ref, k1y_ref, k1z_ref, 2, smooth(e1, wd1_ref))

    def keep_middle(x, value, left):
        r1[x] = left

    sweep_planes(4, 11, e1, f1_ref, k1x_ref, k1y_ref, k1z_ref, 2, keep_middle)

    src = iota((RING, LANES), 0)
    dst = iota((RING, LANES), 1)
    cell = jnp.where(src < 192, src, src - RING)
    coarse = (cell + 4 * COARSE_LOW) // 4
    there = ((cell & 3) == 0) & (coarse >= 0) & (coarse < COARSE)
    head = there & (coarse < HEAD)
    tail = there & (coarse >= HEAD)
    sides = [there & (coarse == dst), there & (coarse + COARSE == dst)]
    picks0 = sides + [head & (coarse + 2 * COARSE == dst)]
    picks1 = sides + [tail & (coarse + 2 * COARSE - HEAD == dst)]
    picks0 = jnp.concatenate([pick.astype(F32) for pick in picks0], axis=0).astype(BF16)
    picks1 = jnp.concatenate([pick.astype(F32) for pick in picks1], axis=0).astype(BF16)
    pick_middle = ((cell == 2 * middle_cell(dst)) & (dst < MIDDLE)).astype(F32)
    firsts = []
    seconds = []
    for j in range(4):
        i = 4 + 2 * j
        f2 = pair_sum(pair_sum(r1[i] + r1[i + 1], 2, 0), 2, 1) * 0.125
        k2x = pair_sum(pair_sum(k1x_ref[i + 1], 2, 0), 2, 1) * (1.0 / 16.0)
        k2y = pair_sum(k1y_ref[i] + k1y_ref[i + 1], 2, 1)
        k2y = upper_of(k2y, 2, 0) * (1.0 / 16.0)
        k2z = pair_sum(k1z_ref[i] + k1z_ref[i + 1], 2, 0)
        k2z = upper_of(k2z, 2, 1) * (1.0 / 16.0)
        f2, k2x, k2y, k2z = (cells[8:24] for cells in (f2, k2x, k2y, k2z))
        k2z = k2z.astype(BF16)
        high = f2.astype(BF16)
        low = (f2 - high.astype(F32)).astype(BF16)
        firsts.append(jnp.concatenate([high, low, k2z], axis=1))
        seconds.append(jnp.concatenate([k2x.astype(BF16), k2y.astype(BF16), k2z], axis=1))
    firsts = jnp.concatenate(firsts, axis=0)
    seconds = jnp.concatenate(seconds, axis=0)
    rows[pl.ds(0, 64), :] = jnp.dot(firsts, picks0, preferred_element_type=F32)
    rows[pl.ds(64, 64), :] = jnp.dot(seconds, picks1, preferred_element_type=F32)
    coarse = rows[pl.ds(0, 32, stride=4), :]
    rows[...] = select_dot(
        jnp.concatenate([e1[i] for i in range(3, 13)], axis=0), pick_middle
    )
    own_ref[...] = rows[pl.ds(0, 160, stride=2), :]

    blocks = [own_ref[pl.ds(16 * (1 + x) + 4, 8), :] for x in (1, 2, 5, 6)]
    for y in (1, 2):
        lines = [(x, k) for k in (y, y + 4) for x in (0, 3, 4, 7)]
        lines = [own_ref[pl.ds(16 * (1 + x) + 4 + k, 1), :] for x, k in lines]
        blocks.append(jnp.concatenate(lines, axis=0))
    narrow = iota((8, LANES), 1)
    middle = []
    for k in (0, 2, 4):
        middle.append(jnp.where(narrow < 64, blocks[k], roll(blocks[k + 1], 64, 1)))
    ends = jnp.zeros((8, LANES), F32)
    for k in range(6):
        ends = jnp.where(narrow // 4 == k, roll(blocks[k], 4 * k - 64, 1), ends)
    chunk = jnp.concatenate([coarse] + middle + [ends], axis=0).astype(BF16)
    for k in range(32):
        chunk_ref[k] = chunk
    for copy in copies:
        copy.wait()


def up_kernel(
    place_ref, all_ref, own_ref, side_in, kx_in, ky_in, kz_in, wd_in, v_in,
    k1x_in, k1y_in, k1z_in, wd1_in, f1_in,
    out_ref,
    side_ref, kx_ref, ky_ref, kz_ref, wd_ref, v_ref, k1x_ref, k1y_ref, k1z_ref, wd1_ref, f1_ref,
    pair0, pair1, c2x, c2y, c2z, wd2, f2, ea, eb, mid, tall, lean, e1a, e1b, va, vb, sems,
):
    copies = []
    for planes, moves in (
        (MIDDLE_PLANES, (
            (k1x_in, k1x_ref), (k1y_in, k1y_ref), (k1z_in, k1z_ref), (wd1_in, wd1_ref),
            (f1_in, f1_ref),
        )),
        (FINE_PLANES, (
            (v_in, v_ref), (side_in, side_ref), (kx_in, kx_ref), (ky_in, ky_ref),
            (kz_in, kz_ref), (wd_in, wd_ref),
        )),
    ):
        for a, b in moves:
            copies.append(
                pltpu.make_async_copy(a.at[planes], b.at[planes], sems.at[len(copies)])
            )
    for copy in copies:
        copy.start()
    gx = place_ref[0]
    gy = place_ref[1]

    def source(dx, dy):
        return ((gx + dx + 8) & 7) * 4 + ((gy + dy + 4) & 3)

    for p in (0, 1, 2, 3, 4, 6, 7):
        for q in range(4):
            s = source(p - 1, q - 1)
            first = all_ref[s, pl.ds(0, 16), :].astype(F32)
            second = all_ref[s, pl.ds(16, 16), :].astype(F32)
            for i in range(4):
                pair0[4 * p + i, pl.ds(4 * q, 4), :] = first[4 * i : 4 * i + 4]
                pair1[4 * p + i, pl.ds(4 * q, 4), :] = second[4 * i : 4 * i + 4]
    for i in range(3, 13):
        mid[i] = own_ref[pl.ds(16 * (i - 3), 16), :]
    narrow = iota((8, LANES), 1)
    for p in (-1, 0, 1):
        for q in (-1, 0, 1):
            if p == 0 and q == 0:
                continue
            cells = all_ref[source(p, q), pl.ds(32, 32), :].astype(F32)
            ends = cells[24:]

            def block(k):
                main = cells[8 * (k // 2) : 8 * (k // 2) + 8]
                if k % 2:
                    main = roll(main, 64, 1)
                end = jnp.where(narrow < 68, roll(ends, 64 - 4 * k, 1), 0.0)
                return jnp.where(narrow < 64, main, end)

            for k, i in {-1: ((2, 1), (3, 2)), 0: (), 1: ((0, 13), (1, 14))}[p]:
                part = block(k)
                if q == -1:
                    mid[i, pl.ds(0, 4), :] = part[4:]
                elif q == 0:
                    mid[i, pl.ds(4, 8), :] = part
                else:
                    mid[i, pl.ds(12, 4), :] = part[:4]
            if q == 0:
                continue
            for depth in (0, 1):
                row = (1 if q == -1 else 13) + depth
                half = 4 if q == -1 else 0
                thin = block(4 + depth)
                for k, x in enumerate((0, 3, 4, 7)):
                    i = 8 * p + x + 4
                    if 3 <= i <= 12:
                        mid[i, pl.ds(row, 1), :] = thin[half + k : half + k + 1]
            if p == 0:
                for k, x in enumerate((1, 2, 5, 6)):
                    line = 5 if q == -1 else 1
                    part = block(k)
                    for depth in (0, 1):
                        row = (1 if q == -1 else 13) + depth
                        mid[x + 4, pl.ds(row, 1), :] = part[line + depth : line + depth + 1]

    used = iota((16, LANES), 1) < COARSE
    head = iota((16, LANES), 1) < HEAD
    for x in range(-6, 17):
        k = x % 32
        first = pair0[k]
        second = pair1[k]
        f2[k] = jnp.where(used, first + roll(first, -COARSE, 1), 0.0)
        c2x[k] = jnp.where(used, second, 0.0)
        c2y[k] = jnp.where(used, roll(second, -COARSE, 1), 0.0)
        last = jnp.where(
            head, roll(first, -2 * COARSE, 1), roll(second, HEAD - 2 * COARSE, 1)
        )
        c2z[k] = jnp.where(used, last, 0.0)
    for xs in groups(range(-5, 17), 11):
        done = []
        for x in xs:
            k = x % 32
            ky = c2y[k]
            kz = c2z[k]
            total = c2x[k] + c2x[(x - 1) % 32]
            total = total + (ky + roll(ky, 1, 0)) + (kz + roll(kz, 1, 1))
            weight = OMEGA / (1.0 + total)
            done.append((weight, weight * f2[k]))
        for x, value in zip(xs, done):
            wd2[x % 32], ea[x % 32] = value

    def smooth(target, weight):
        def use(x, value, left):
            target[x] = value + weight[x] * left

        return use

    old, new = ea, eb
    for reach in range(6, -1, -1):
        sweep_planes(
            2 - reach, 9 + reach, old, f2, c2x, c2y, c2z, 1, smooth(new, wd2), 10, 32
        )
        old, new = new, old

    lane = iota((8, LANES), 1)
    for j in range(8):
        line = roll(old[2 + j, pl.ds(2, 8), :], MIDDLE, 1)
        line = jnp.where((lane >= MIDDLE) & (lane < MIDDLE + COARSE), line, 0.0)
        for k in range(4):
            lean[j, pl.ds(k, 8, stride=4), :] = line
    for i in range(1, 15):
        line = mid[i]
        for k in range(2):
            tall[i, pl.ds(k, 16, stride=2), :] = line
    src = iota((LANES, RING), 0)
    dst = iota((LANES, RING), 1)
    cell = jnp.where(dst < 192, dst, dst - RING)
    middle = (src < MIDDLE) & ((cell + 64) // 2 - 32 == middle_cell(src))
    coarse = (cell >= -4 * COARSE_LOW) & (src >= MIDDLE) & (src < MIDDLE + COARSE)
    coarse = coarse & ((cell + 4 * COARSE_LOW) // 4 == src - MIDDLE)
    spread = (middle | coarse).astype(F32)
    narrow = iota((32, LANES), 1) < MIDDLE
    packed = [jnp.where(narrow, tall[i], lean[i // 2]) for i in range(1, 15)]
    widened = select_dot(jnp.concatenate(packed, axis=0), spread)
    for i in range(1, 15):
        e1a[i] = widened[32 * (i - 1) : 32 * i]

    for copy in copies:
        copy.wait()
    sweep_planes(2, 13, e1a, f1_ref, k1x_ref, k1y_ref, k1z_ref, 2, smooth(e1b, wd1_ref))
    sweep_planes(3, 12, e1b, f1_ref, k1x_ref, k1y_ref, k1z_ref, 2, smooth(e1a, wd1_ref))
    for x in range(6, 26):
        va[x] = v_ref[x] + e1a[x // 2]
    sweep_planes(7, 24, va, side_ref, kx_ref, ky_ref, kz_ref, 1, smooth(vb, wd_ref))

    def finish(x, value, left):
        new = value + wd_ref[x] * left
        out_ref[x - 8] = new[8:24, :LANES]

    sweep_planes(8, 23, vb, side_ref, kx_ref, ky_ref, kz_ref, 1, finish)


def shift(x, axis, direction):
    count = lax.axis_size(axis)
    return lax.ppermute(x, axis, [(i, (i + direction) % count) for i in range(count)])


def body(conc, right_side, order_field, grain_ids):
    face = ((9, 16, LANES), BF16)
    zface = ((17, 16, LANES), BF16)
    brick = ((16, 16, LANES), F32)
    conc, side, order, ids, xm, xp, ym, yp, zm, zp = call(
        faces_kernel,
        [brick, brick, ((8, 16, 16, LANES), BF16), ((1, 1, 8, 8), jnp.int32)]
        + [face] * 4
        + [zface] * 2,
        (conc, right_side, order_field, grain_ids),
        specs=[HBM] * 4,
        semaphores=4,
    )
    above = shift(ym, "gy", -1)
    before = shift(xp, "gx", 1)
    after = shift(xm, "gx", -1)
    line = ((16, LANES), F32)
    payload = ((34, 16, LANES), BF16)
    partial, beyond, send_zm, send_zp = call(
        mobility_kernel,
        [brick, line, payload, payload],
        (conc, side, order, ids, before, after, above, yp, zm, zp),
        scratch=[brick, ((64, 8, LANES), F32)],
    )
    left = shift(send_zp, "gz", 1)
    right = shift(send_zm, "gz", -1)
    keep, beside, low, high = call(
        split_kernel,
        [brick, line, ((80, 8, LANES), BF16), ((86, 8, LANES), BF16)],
        (partial, conc, side, beyond, left, right, zm, zp),
    )
    below = shift(high, "gy", 1)
    above = shift(low, "gy", -1)
    slab = ((5, 8, 32, LANES), BF16)
    mobility, keep, xl, xh = call(
        rows_kernel,
        [brick, brick, slab, slab],
        (below, low, high, above, keep, beyond, beside),
    )
    before = shift(xh, "gx", 1)
    after = shift(xl, "gx", -1)
    fine = ((32, 32, RING), F32)
    middle = ((16, 32, RING), F32)
    own, chunk, *kept = call(
        down_kernel,
        [((160, LANES), F32), ((32, CHUNK, LANES), BF16)] + [fine] * 6 + [middle] * 5,
        (keep, conc, side, xl, xh, before, after),
        scratch=[fine] * 9 + [middle] * 8 + [((320, LANES), F32)],
        places=[VMEM] * 2 + [HBM] * 11,
        limit=24,
        semaphores=11,
    )
    place = jnp.stack([lax.axis_index("gx"), lax.axis_index("gy")]).astype(jnp.int32)
    chunk, place = lax.optimization_barrier((chunk, place))
    chunks = lax.all_to_all(chunk, ("gx", "gy"), 0, 0, tiled=True)
    plane = ((32, 16, LANES), F32)
    (out,) = call(
        up_kernel,
        [brick],
        (place, chunks, own) + tuple(kept),
        scratch=[fine] * 6
        + [middle] * 5
        + [plane] * 9
        + [brick, ((16, 32, LANES), F32), ((8, 32, LANES), F32)]
        + [middle] * 2
        + [fine] * 2,
        specs=[SMEM] + [VMEM] * 2 + [HBM] * 11,
        limit=24,
        semaphores=11,
    )
    return out, mobility


def solution(mesh):
    return jax.shard_map(
        body,
        mesh=mesh,
        in_specs=(
            P("gx", "gy", "gz"),
            P("gx", "gy", "gz"),
            P(None, "gx", "gy", "gz"),
            P("gx", "gy", "gz", None),
        ),
        out_specs=(P("gx", "gy", "gz"), P("gx", "gy", "gz")),
        check_vma=False,
    )
```

```python
import functools

import jax
import jax.numpy as jnp
from jax import lax
from jax.experimental import pallas as pl
from jax.experimental.pallas import tpu as pltpu
from jax.sharding import PartitionSpec as P

SLOTS = 8
BRICK = 16
OMEGA = 0.8
TAU = 256.0
LANES = 128
RING = 256
F32 = jnp.float32
BF16 = jnp.bfloat16
HIGH = lax.Precision.HIGHEST
VMEM = pl.BlockSpec(memory_space=pltpu.VMEM)
HBM = pl.BlockSpec(memory_space=pltpu.MemorySpace.HBM)
SMEM = pl.BlockSpec(memory_space=pltpu.SMEM)
COARSE = 51
COARSE_LOW = 10
MIDDLE = 70
HEAD = 26
CHUNK = 64


def call(kernel, outs, args, scratch=(), specs=None, places=None, limit=16, semaphores=0):
    specs = specs or [VMEM] * len(args)
    places = places or [VMEM] * len(outs)
    args = [
        pltpu.with_memory_space_constraint(arg, pltpu.MemorySpace.HBM) if spec is HBM else arg
        for arg, spec in zip(args, specs)
    ]
    scratches = [pltpu.VMEM(shape, dtype) for shape, dtype in scratch]
    if semaphores:
        scratches.append(pltpu.SemaphoreType.DMA((semaphores,)))
    return pl.pallas_call(
        kernel,
        out_shape=[
            pltpu.MemorySpace.HBM(*out) if place is HBM else jax.ShapeDtypeStruct(*out)
            for out, place in zip(outs, places)
        ],
        in_specs=specs,
        out_specs=places,
        scratch_shapes=scratches,
        compiler_params=pltpu.CompilerParams(vmem_limit_bytes=limit << 20),
    )(*args)


def roll(x, shift, axis):
    return pltpu.roll(x, shift % x.shape[axis], axis)


def iota(shape, axis):
    return lax.broadcasted_iota(jnp.int32, shape, axis)


def select_dot(a, picks):
    picks = picks.astype(BF16)
    total = None
    for _ in range(3):
        part = a.astype(BF16)
        a = a - part.astype(F32)
        term = jnp.dot(part, picks, preferred_element_type=F32)
        total = term if total is None else total + term
    return total


def lane_ids(ids_ref):
    ids = ids_ref[0, 0].astype(F32)
    spread = (iota((8, LANES), 1) // BRICK == iota((8, LANES), 0)).astype(F32)
    grains = lax.dot_general(
        ids, spread, (((0,), (0,)), ((), ())), precision=HIGH, preferred_element_type=F32
    )
    return jnp.floor(grains + 0.5)


def split_ids(grains):
    high = jnp.floor(grains * (1.0 / 64.0))
    return jnp.concatenate([high, grains - 64.0 * high], axis=0).astype(BF16)


def join_ids(rows):
    rows = rows.astype(F32)
    return rows[:8] * 64.0 + rows[8:]


def faces_kernel(
    conc_in, side_in, order_in, ids_in,
    conc_ref, side_ref, order_ref, ids_ref, xm_ref, xp_ref, ym_ref, sems,
):
    pairs = (
        (ids_in, ids_ref), (order_in, order_ref), (conc_in, conc_ref), (side_in, side_ref),
    )
    copies = [pltpu.make_async_copy(a, b, sems.at[k]) for k, (a, b) in enumerate(pairs)]
    for copy in copies:
        copy.start()
    copies[0].wait()
    copies[1].wait()
    grains = lane_ids(ids_ref)
    packed = split_ids(grains)
    for ref in (xm_ref, xp_ref, ym_ref):
        ref[SLOTS] = packed
    for slot in range(SLOTS):
        xm_ref[slot] = order_ref[slot, 0]
        xp_ref[slot] = order_ref[slot, 15]
        ym_ref[slot] = order_ref[slot].astype(F32)[:, 0, :].astype(BF16)
    copies[2].wait()
    copies[3].wait()


def square(x):
    return x * x


def inner_kernel(
    conc_ref, order_ref, ids_ref, work, yp_ref, zm_ref, zp_ref, weights,
):
    grains = lane_ids(ids_ref)
    zm_ref[16] = split_ids(jnp.broadcast_to(grains[:, 0:1], (8, LANES)))
    zp_ref[16] = split_ids(jnp.broadcast_to(grains[:, LANES - 1 :], (8, LANES)))
    slots = iota((16, LANES), 1)
    low = [jnp.zeros((16, LANES), F32)] * 16
    high = [jnp.zeros((16, LANES), F32)] * 16
    for slot in range(SLOTS):
        cells = order_ref[slot].astype(F32)
        yp_ref[slot] = cells[:, 15, :].astype(BF16)
        for x in range(16):
            low[x] = jnp.where(slots == slot, cells[x, :, 0:1], low[x])
            high[x] = jnp.where(slots == slot, cells[x, :, LANES - 1 :], high[x])
    for x in range(16):
        zm_ref[x] = low[x].astype(BF16)
        zp_ref[x] = high[x].astype(BF16)

    own = lane_ids(ids_ref)
    lane = iota((16, LANES), 1)
    row = iota((16, LANES), 0)
    last = lane % BRICK == BRICK - 1
    edge = (last | (lane % BRICK == 0)) & (lane != 0) & (lane != LANES - 1)

    lane8 = iota((8, LANES), 1)
    beside = jnp.where(
        lane8 % BRICK == BRICK - 1, roll(own, -BRICK, 1), roll(own, BRICK, 1)
    )
    for other in range(SLOTS):
        match = (own == beside[other : other + 1]).astype(F32)
        for slot in range(SLOTS):
            weights[slot * SLOTS + other] = jnp.broadcast_to(match[slot : slot + 1], (8, LANES))

    def doubled(block):
        return jnp.concatenate([block, block], axis=0)

    def plane(x, carry_in):
        conc = conc_ref[x]
        base = 1.0 + 8.0 * square(conc * (1.0 - conc))
        along_y = jnp.zeros((16, LANES), F32)
        along_z = jnp.zeros((16, LANES), F32)
        along_x = jnp.zeros((16, LANES), F32)
        centers = []
        facing = []
        above = min(x + 1, 15)
        for slot in range(SLOTS):
            here = order_ref[slot, x].astype(F32)
            there = order_ref[slot, above].astype(F32)
            centers.append(here)
            along_x = along_x + square(there - here)
            along_y = along_y + square(roll(here, -1, 0) - here)
            right = roll(here, -1, 1)
            along_z = along_z + square(right - here)
            facing.append(jnp.where(last, right, roll(here, 1, 1)))
        along_y = jnp.where(row == 15, 0.0, along_y)
        along_z = jnp.where(last, 0.0, along_z)
        remapped = jnp.zeros((16, LANES), F32)
        for slot in range(SLOTS):
            value = None
            for other in range(SLOTS):
                term = doubled(weights[slot * SLOTS + other]) * facing[other]
                value = term if value is None else value + term
            remapped = remapped + square(value - centers[slot])
        total = base + along_y + roll(along_y, 1, 0) + along_z + roll(along_z, 1, 1)
        total = total + jnp.where(edge, remapped, 0.0) + along_x + carry_in
        work[x] = total
        return along_x

    carry = jnp.zeros((16, LANES), F32)
    for x in range(16):
        carry = plane(x, carry)

def outer_kernel(
    work, conc_ref, side_ref, order_ref, ids_ref, xm_ref, xp_ref, yp_ref,
    own_yp_ref, own_zm_ref, own_zp_ref, mob_ref, beyond_ref, zm_out, zp_out,
):
    own = lane_ids(ids_ref)
    lane = iota((16, LANES), 1)
    row = iota((16, LANES), 0)

    def across(center, ids, facing, facing_ids):
        facing = [facing(other).astype(F32) for other in range(SLOTS)]
        total = None
        for slot in range(SLOTS):
            value = None
            for other in range(SLOTS):
                match = ids[slot : slot + 1] == facing_ids[other : other + 1]
                term = match.astype(F32) * facing[other]
                value = term if value is None else value + term
            part = square(value - center(slot).astype(F32))
            total = part if total is None else total + part
        return total

    first = work[0] + across(
        lambda k: order_ref[k, 0], own, lambda k: xm_ref[k], join_ids(xm_ref[SLOTS])
    )
    final = work[15] + across(
        lambda k: order_ref[k, 15], own, lambda k: xp_ref[k], join_ids(xp_ref[SLOTS])
    )
    above_ids = join_ids(yp_ref[SLOTS])
    top = across(lambda k: own_yp_ref[k], own, lambda k: yp_ref[k], above_ids)
    beyond = across(lambda k: yp_ref[k], above_ids, lambda k: own_yp_ref[k], own)
    beyond_ref[...] = beyond
    zm_out[33] = beyond.astype(BF16)
    zp_out[33] = beyond.astype(BF16)
    for x in range(16):
        value = first if x == 0 else final if x == 15 else work[x]
        value = value + jnp.where(row == 15, top[x : x + 1], 0.0)
        mob_ref[x] = value
        conc, side = conc_ref[x], side_ref[x]
        down = jnp.where(
            lane < 43, value, jnp.where(lane < 86, roll(conc, 43, 1), roll(side, 86, 1))
        )
        zm_out[x] = down.astype(BF16)
        up = jnp.where(
            lane >= 85, value, jnp.where(lane >= 42, roll(conc, -43, 1), roll(side, -86, 1))
        )
        zp_out[x] = up.astype(BF16)
    zm_out[16:33] = own_zm_ref[...]
    zp_out[16:33] = own_zp_ref[...]


def facing_squares(near_ref, far_ref, near_lane, far_lane):
    near = near_ref[:16].reshape(256, LANES)
    far = far_ref[:16].reshape(256, LANES)
    near_ids = join_ids(near_ref[16])
    far_ids = join_ids(far_ref[16])
    diagonal = iota((8, LANES), 0) == iota((8, LANES), 1)
    slots = iota((8, LANES), 1) < SLOTS

    def squares(cells, ids, others, other_ids, target):
        along = jnp.sum(jnp.where(diagonal, ids, 0.0), axis=0, keepdims=True)
        match = ((other_ids == along) & slots).astype(F32)
        match = jnp.concatenate([match, jnp.zeros((LANES - 8, LANES), F32)], axis=0)
        seen = jnp.dot(others, match.astype(BF16), preferred_element_type=F32)
        place = (iota((LANES, LANES), 1) == target).astype(F32)
        total = select_dot(square(seen - cells.astype(F32)), place)
        return total.reshape(16, 16, LANES)

    return (
        squares(near, near_ids, far, far_ids, near_lane),
        squares(far, far_ids, near, near_ids, far_lane),
    )


def split_kernel(
    mob_ref, conc_ref, side_ref, beyond_ref, left_ref, right_ref, zm_ref, zp_ref,
    keep_ref, beside_ref, low_ref, high_ref,
):
    own_low, far_low = facing_squares(zm_ref, left_ref.at[16:33], 0, LANES - 1)
    own_high, far_high = facing_squares(zp_ref, right_ref.at[16:33], LANES - 1, 0)
    mob = mob_ref[...] + own_low + own_high
    keep_ref[...] = mob
    down = (left_ref[:16].astype(F32) + far_low).astype(BF16)
    up = (right_ref[:16].astype(F32) + far_high).astype(BF16)
    for place, value in enumerate((mob, conc_ref[...], side_ref[...], down, up)):
        planes = pl.ds(16 * place, 16)
        low_ref[planes] = value[:, :8].astype(BF16)
        high_ref[planes] = value[:, 8:].astype(BF16)
    lane = iota((16, LANES), 1)
    down, up = left_ref[33].astype(F32), right_ref[33].astype(F32)
    beside = jnp.where(lane < 43, up, jnp.where(lane >= 85, down, 0.0))
    beside_ref[...] = beside
    beyond = beyond_ref[...]
    high = beyond.astype(BF16)
    rest = (beyond - high.astype(F32)).astype(BF16)
    for k, value in enumerate((high, rest, beside.astype(BF16))):
        high_ref[80 + 2 * k] = value[:8]
        high_ref[81 + 2 * k] = value[8:]


def rows_kernel(
    below_ref, low_ref, high_ref, above_ref, mob_ref, beyond_ref, beside_ref,
    out_ref, keep_ref, xl_ref, xh_ref,
):
    lane = iota((8, LANES), 1)
    first = iota((8, LANES), 0) == 0
    got = [
        jnp.concatenate([below_ref[80 + 2 * k], below_ref[81 + 2 * k]], axis=0).astype(F32)
        for k in range(3)
    ]
    missing = ((got[0] + got[1], got[2]), (beyond_ref[...], beside_ref[...]))
    for x in range(16):
        ref = xl_ref if x < 8 else xh_ref
        lines = []
        for main, beside in missing:
            main = jnp.where(first, main[x : x + 1], 0.0)
            beside = jnp.where(first, beside[x : x + 1], 0.0)
            down = jnp.where(lane >= 85, beside, 0.0)
            lines.append((main, None, None, down, jnp.where(lane < 43, beside, 0.0)))
        own = mob_ref[x, :8] + lines[0][0]
        for out in (out_ref, keep_ref):
            out[x, :8] = own
            out[x, 8:] = mob_ref[x, 8:]
        for place in range(5):
            plane = 16 * place + x
            near, far = low_ref[plane], above_ref[plane]
            if place == 0:
                near = own.astype(BF16)
            elif place >= 3:
                near = (near.astype(F32) + lines[0][place]).astype(BF16)
            if place in (0, 3, 4):
                far = (far.astype(F32) + lines[1][place]).astype(BF16)
            for k, value in enumerate((below_ref[plane], near, high_ref[plane], far)):
                ref[place, x % 8, pl.ds(8 * k, 8), :] = value


def partner(x, step, axis):
    upper = (iota(x.shape, axis) & step) != 0
    return jnp.where(upper, roll(x, step, axis), roll(x, -step, axis))


def pair_sum(x, step, axis):
    return x + partner(x, step, axis)


def upper_of(x, step, axis):
    upper = (iota(x.shape, axis) & step) != 0
    return jnp.where(upper, x, roll(x, -step, axis))


def middle_cell(lane):
    cell = lane
    for place, end in enumerate((-2, -1, 64, 65, -3, 66)):
        cell = jnp.where(lane == 64 + place, end, cell)
    return cell


def groups(items, size):
    items = list(items)
    return [items[k : k + size] for k in range(0, len(items), size)]


def sweep_planes(first, last, values, source, kx, ky, kz, step, use, size=8, planes=None):
    at = (lambda x: x) if planes is None else (lambda x: x % planes)
    before = kx[at(first - 1)] * (values[at(first)] - values[at(first - 1)])
    for xs in groups(range(first, last + 1), size):
        cells = [values[at(x)] for x in xs + [xs[-1] + 1]]
        flux_z = [kz[at(x)] * (roll(v, -step, 1) - v) for x, v in zip(xs, cells)]
        back_z = [roll(flux, step, 1) for flux in flux_z]
        left = []
        for k, x in enumerate(xs):
            value = cells[k]
            flux_x = kx[at(x)] * (cells[k + 1] - value)
            flux_y = ky[at(x)] * (roll(value, -step, 0) - value)
            total = (source[at(x)] - value) + (flux_x - before)
            total = total + (flux_y - roll(flux_y, step, 0))
            left.append(total + (flux_z[k] - back_z[k]))
            before = flux_x
        for k, x in enumerate(xs):
            use(at(x), cells[k], left[k])


def down_kernel(
    mob_in, conc_in, side_in, xl_ref, xh_ref, xm_ref, xp_ref,
    own_ref, chunk_ref, side_ref, kx_ref, ky_ref, kz_ref, wd_ref, v_ref,
    k1x_ref, k1y_ref, k1z_ref, wd1_ref, f1_ref,
    mob, v0, res, e0, e1, r1, rows,
):
    lane = iota((32, LANES), 1)

    own = (mob_in, conc_in, side_in)
    slabs = (xm_ref, xl_ref, xh_ref, xp_ref)
    for xs in groups(range(32), 8):
        planes = []
        for x in xs:
            parts = [slabs[x // 8][place, x % 8].astype(F32) for place in range(5)]
            if 8 <= x < 24:
                for place in range(3):
                    part = parts[place]
                    part = [part[:8], own[place][x - 8], part[24:]]
                    parts[place] = jnp.concatenate(part, axis=0)
            down, up = parts[3], parts[4]
            beyond = jnp.where(lane < 43, up, jnp.where(lane >= 85, down, 1.0))
            iterate = jnp.where(
                lane < 43, roll(up, -43, 1), jnp.where(lane >= 85, roll(down, 43, 1), 0.0)
            )
            right = jnp.where(
                lane < 42, roll(up, -86, 1), jnp.where(lane >= 86, roll(down, 86, 1), 0.0)
            )
            planes.append((parts, beyond, iterate, right))
        for x, (parts, beyond, iterate, right) in zip(xs, planes):
            mob[x, :, :LANES] = parts[0]
            v0[x, :, :LANES] = parts[1]
            side_ref[x, :, :LANES] = parts[2]
            mob[x, :, LANES:] = beyond
            v0[x, :, LANES:] = iterate
            side_ref[x, :, LANES:] = right

    half = TAU / 2

    before = half * (mob[1] + mob[2])
    kx_ref[1] = before
    for xs in groups(range(2, 30), 7):
        here = [mob[x] for x in xs + [xs[-1] + 1]]
        kz = [half * (cells + roll(cells, -1, 1)) for cells in here[:-1]]
        back = [roll(k, 1, 1) for k in kz]
        done = []
        for k, x in enumerate(xs):
            kx = half * (here[k] + here[k + 1])
            ky = half * (here[k] + roll(here[k], -1, 0))
            total = (kx + before) + (ky + roll(ky, 1, 0)) + (kz[k] + back[k])
            done.append((kx, ky, OMEGA / (1.0 + total)))
            before = kx
        for k, x in enumerate(xs):
            kx_ref[x], ky_ref[x], wd_ref[x] = done[k]
            kz_ref[x] = kz[k]


    def smooth(target, weight):
        def use(x, value, left):
            target[x] = value + weight[x] * left

        return use

    sweep_planes(2, 29, v0, side_ref, kx_ref, ky_ref, kz_ref, 1, smooth(res, wd_ref))
    sweep_planes(3, 28, res, side_ref, kx_ref, ky_ref, kz_ref, 1, smooth(v_ref, wd_ref))


    def keep(x, value, left):
        res[x] = left

    sweep_planes(4, 27, v_ref, side_ref, kx_ref, ky_ref, kz_ref, 1, keep)

    def pool(x):
        return pair_sum(pair_sum(x, 1, 0), 1, 1)

    for xs in groups(range(1, 14), 7):
        done = [pool(kx_ref[2 * i + 1]) * (1.0 / 16.0) for i in xs]
        for i, value in zip(xs, done):
            k1x_ref[i] = value
    for ref in (f1_ref, k1y_ref, k1z_ref, wd1_ref):
        ref[1] = jnp.zeros((32, RING), F32)
    for xs in groups(range(2, 14), 6):
        done = []
        for i in xs:
            x = 2 * i
            f1 = pool(res[x] + res[x + 1]) * 0.125
            along_y = pair_sum(ky_ref[x] + ky_ref[x + 1], 1, 1)
            k1y = upper_of(along_y, 1, 0) * (1.0 / 16.0)
            along_z = pair_sum(kz_ref[x] + kz_ref[x + 1], 1, 0)
            k1z = upper_of(along_z, 1, 1) * (1.0 / 16.0)
            total = k1x_ref[i] + k1x_ref[i - 1]
            total = total + (k1y + roll(k1y, 2, 0)) + (k1z + roll(k1z, 2, 1))
            weight = OMEGA / (1.0 + total)
            done.append((f1, k1y, k1z, weight, weight * f1))
        for i, value in zip(xs, done):
            f1_ref[i], k1y_ref[i], k1z_ref[i], wd1_ref[i], e0[i] = value
    sweep_planes(3, 12, e0, f1_ref, k1x_ref, k1y_ref, k1z_ref, 2, smooth(e1, wd1_ref))

    def keep_middle(x, value, left):
        r1[x] = left

    sweep_planes(4, 11, e1, f1_ref, k1x_ref, k1y_ref, k1z_ref, 2, keep_middle)

    src = iota((RING, LANES), 0)
    dst = iota((RING, LANES), 1)
    cell = jnp.where(src < 192, src, src - RING)
    coarse = (cell + 4 * COARSE_LOW) // 4
    there = ((cell & 3) == 0) & (coarse >= 0) & (coarse < COARSE)
    head = there & (coarse < HEAD)
    tail = there & (coarse >= HEAD)
    sides = [there & (coarse == dst), there & (coarse + COARSE == dst)]
    picks0 = sides + [head & (coarse + 2 * COARSE == dst)]
    picks1 = sides + [tail & (coarse + 2 * COARSE - HEAD == dst)]
    picks0 = jnp.concatenate([pick.astype(F32) for pick in picks0], axis=0).astype(BF16)
    picks1 = jnp.concatenate([pick.astype(F32) for pick in picks1], axis=0).astype(BF16)
    pick_middle = ((cell == 2 * middle_cell(dst)) & (dst < MIDDLE)).astype(F32)
    firsts = []
    seconds = []
    for j in range(4):
        i = 4 + 2 * j
        f2 = pair_sum(pair_sum(r1[i] + r1[i + 1], 2, 0), 2, 1) * 0.125
        k2x = pair_sum(pair_sum(k1x_ref[i + 1], 2, 0), 2, 1) * (1.0 / 16.0)
        k2y = pair_sum(k1y_ref[i] + k1y_ref[i + 1], 2, 1)
        k2y = upper_of(k2y, 2, 0) * (1.0 / 16.0)
        k2z = pair_sum(k1z_ref[i] + k1z_ref[i + 1], 2, 0)
        k2z = upper_of(k2z, 2, 1) * (1.0 / 16.0)
        f2, k2x, k2y, k2z = (cells[8:24] for cells in (f2, k2x, k2y, k2z))
        k2z = k2z.astype(BF16)
        high = f2.astype(BF16)
        low = (f2 - high.astype(F32)).astype(BF16)
        firsts.append(jnp.concatenate([high, low, k2z], axis=1))
        seconds.append(jnp.concatenate([k2x.astype(BF16), k2y.astype(BF16), k2z], axis=1))
    firsts = jnp.concatenate(firsts, axis=0)
    seconds = jnp.concatenate(seconds, axis=0)
    rows[pl.ds(0, 64), :] = jnp.dot(firsts, picks0, preferred_element_type=F32)
    rows[pl.ds(64, 64), :] = jnp.dot(seconds, picks1, preferred_element_type=F32)
    coarse = rows[pl.ds(0, 32, stride=4), :]
    rows[...] = select_dot(
        jnp.concatenate([e1[i] for i in range(3, 13)], axis=0), pick_middle
    )
    own_ref[...] = rows[pl.ds(0, 160, stride=2), :]

    blocks = [own_ref[pl.ds(16 * (1 + x) + 4, 8), :] for x in (1, 2, 5, 6)]
    for y in (1, 2):
        lines = [(x, k) for k in (y, y + 4) for x in (0, 3, 4, 7)]
        lines = [own_ref[pl.ds(16 * (1 + x) + 4 + k, 1), :] for x, k in lines]
        blocks.append(jnp.concatenate(lines, axis=0))
    narrow = iota((8, LANES), 1)
    middle = []
    for k in (0, 2, 4):
        middle.append(jnp.where(narrow < 64, blocks[k], roll(blocks[k + 1], 64, 1)))
    ends = jnp.zeros((8, LANES), F32)
    for k in range(6):
        ends = jnp.where(narrow // 4 == k, roll(blocks[k], 4 * k - 64, 1), ends)
    chunk = jnp.concatenate([coarse] + middle + [ends], axis=0).astype(BF16)
    for k in range(32):
        chunk_ref[k] = chunk


def up_kernel(
    place_ref, all_ref, own_ref, side_ref, kx_ref, ky_ref, kz_ref, wd_ref, v_ref,
    k1x_ref, k1y_ref, k1z_ref, wd1_ref, f1_ref,
    out_ref,
    pair0, pair1, c2x, c2y, c2z, wd2, f2, ea, eb, mid, tall, lean, e1a, e1b, va, vb,
):
    gx = place_ref[0]
    gy = place_ref[1]

    def source(dx, dy):
        return ((gx + dx + 8) & 7) * 4 + ((gy + dy + 4) & 3)

    for p in (0, 1, 2, 3, 4, 6, 7):
        for q in range(4):
            s = source(p - 1, q - 1)
            first = all_ref[s, pl.ds(0, 16), :].astype(F32)
            second = all_ref[s, pl.ds(16, 16), :].astype(F32)
            for i in range(4):
                pair0[4 * p + i, pl.ds(4 * q, 4), :] = first[4 * i : 4 * i + 4]
                pair1[4 * p + i, pl.ds(4 * q, 4), :] = second[4 * i : 4 * i + 4]
    for i in range(3, 13):
        mid[i] = own_ref[pl.ds(16 * (i - 3), 16), :]
    narrow = iota((8, LANES), 1)
    for p in (-1, 0, 1):
        for q in (-1, 0, 1):
            if p == 0 and q == 0:
                continue
            cells = all_ref[source(p, q), pl.ds(32, 32), :].astype(F32)
            ends = cells[24:]

            def block(k):
                main = cells[8 * (k // 2) : 8 * (k // 2) + 8]
                if k % 2:
                    main = roll(main, 64, 1)
                end = jnp.where(narrow < 68, roll(ends, 64 - 4 * k, 1), 0.0)
                return jnp.where(narrow < 64, main, end)

            for k, i in {-1: ((2, 1), (3, 2)), 0: (), 1: ((0, 13), (1, 14))}[p]:
                part = block(k)
                if q == -1:
                    mid[i, pl.ds(0, 4), :] = part[4:]
                elif q == 0:
                    mid[i, pl.ds(4, 8), :] = part
                else:
                    mid[i, pl.ds(12, 4), :] = part[:4]
            if q == 0:
                continue
            for depth in (0, 1):
                row = (1 if q == -1 else 13) + depth
                half = 4 if q == -1 else 0
                thin = block(4 + depth)
                for k, x in enumerate((0, 3, 4, 7)):
                    i = 8 * p + x + 4
                    if 3 <= i <= 12:
                        mid[i, pl.ds(row, 1), :] = thin[half + k : half + k + 1]
            if p == 0:
                for k, x in enumerate((1, 2, 5, 6)):
                    line = 5 if q == -1 else 1
                    part = block(k)
                    for depth in (0, 1):
                        row = (1 if q == -1 else 13) + depth
                        mid[x + 4, pl.ds(row, 1), :] = part[line + depth : line + depth + 1]

    used = iota((16, LANES), 1) < COARSE
    head = iota((16, LANES), 1) < HEAD
    for x in range(-6, 17):
        k = x % 32
        first = pair0[k]
        second = pair1[k]
        f2[k] = jnp.where(used, first + roll(first, -COARSE, 1), 0.0)
        c2x[k] = jnp.where(used, second, 0.0)
        c2y[k] = jnp.where(used, roll(second, -COARSE, 1), 0.0)
        last = jnp.where(
            head, roll(first, -2 * COARSE, 1), roll(second, HEAD - 2 * COARSE, 1)
        )
        c2z[k] = jnp.where(used, last, 0.0)
    for xs in groups(range(-5, 17), 11):
        done = []
        for x in xs:
            k = x % 32
            ky = c2y[k]
            kz = c2z[k]
            total = c2x[k] + c2x[(x - 1) % 32]
            total = total + (ky + roll(ky, 1, 0)) + (kz + roll(kz, 1, 1))
            weight = OMEGA / (1.0 + total)
            done.append((weight, weight * f2[k]))
        for x, value in zip(xs, done):
            wd2[x % 32], ea[x % 32] = value

    def smooth(target, weight):
        def use(x, value, left):
            target[x] = value + weight[x] * left

        return use

    old, new = ea, eb
    for reach in range(6, -1, -1):
        sweep_planes(
            2 - reach, 9 + reach, old, f2, c2x, c2y, c2z, 1, smooth(new, wd2), 10, 32
        )
        old, new = new, old

    lane = iota((8, LANES), 1)
    for j in range(8):
        line = roll(old[2 + j, pl.ds(2, 8), :], MIDDLE, 1)
        line = jnp.where((lane >= MIDDLE) & (lane < MIDDLE + COARSE), line, 0.0)
        for k in range(4):
            lean[j, pl.ds(k, 8, stride=4), :] = line
    for i in range(1, 15):
        line = mid[i]
        for k in range(2):
            tall[i, pl.ds(k, 16, stride=2), :] = line
    src = iota((LANES, RING), 0)
    dst = iota((LANES, RING), 1)
    cell = jnp.where(dst < 192, dst, dst - RING)
    middle = (src < MIDDLE) & ((cell + 64) // 2 - 32 == middle_cell(src))
    coarse = (cell >= -4 * COARSE_LOW) & (src >= MIDDLE) & (src < MIDDLE + COARSE)
    coarse = coarse & ((cell + 4 * COARSE_LOW) // 4 == src - MIDDLE)
    spread = (middle | coarse).astype(F32)
    narrow = iota((32, LANES), 1) < MIDDLE
    packed = [jnp.where(narrow, tall[i], lean[i // 2]) for i in range(1, 15)]
    widened = select_dot(jnp.concatenate(packed, axis=0), spread)
    for i in range(1, 15):
        e1a[i] = widened[32 * (i - 1) : 32 * i]

    sweep_planes(2, 13, e1a, f1_ref, k1x_ref, k1y_ref, k1z_ref, 2, smooth(e1b, wd1_ref))
    sweep_planes(3, 12, e1b, f1_ref, k1x_ref, k1y_ref, k1z_ref, 2, smooth(e1a, wd1_ref))
    for x in range(6, 26):
        va[x] = v_ref[x] + e1a[x // 2]
    sweep_planes(7, 24, va, side_ref, kx_ref, ky_ref, kz_ref, 1, smooth(vb, wd_ref))

    def finish(x, value, left):
        new = value + wd_ref[x] * left
        out_ref[x - 8] = new[8:24, :LANES]

    sweep_planes(8, 23, vb, side_ref, kx_ref, ky_ref, kz_ref, 1, finish)


def shift(x, axis, direction):
    count = lax.axis_size(axis)
    return lax.ppermute(x, axis, [(i, (i + direction) % count) for i in range(count)])


def body(conc, right_side, order_field, grain_ids):
    face = ((9, 16, LANES), BF16)
    zface = ((17, 16, LANES), BF16)
    brick = ((16, 16, LANES), F32)
    conc, side, order, ids, xm, xp, ym = call(
        faces_kernel,
        [brick, brick, ((8, 16, 16, LANES), BF16), ((1, 1, 8, 8), jnp.int32)] + [face] * 3,
        (conc, right_side, order_field, grain_ids),
        specs=[HBM] * 4,
        semaphores=4,
    )
    above = shift(ym, "gy", -1)
    before = shift(xp, "gx", 1)
    after = shift(xm, "gx", -1)
    inner, yp, zm, zp = call(
        inner_kernel,
        [brick, ((8, 16, LANES), BF16), zface, zface],
        (conc, order, ids),
        scratch=[((64, 8, LANES), F32)],
    )
    line = ((16, LANES), F32)
    payload = ((34, 16, LANES), BF16)
    partial, beyond, send_zm, send_zp = call(
        outer_kernel,
        [brick, line, payload, payload],
        (inner, conc, side, order, ids, before, after, above, yp, zm, zp),
    )
    left = shift(send_zp, "gz", 1)
    right = shift(send_zm, "gz", -1)
    keep, beside, low, high = call(
        split_kernel,
        [brick, line, ((80, 8, LANES), BF16), ((86, 8, LANES), BF16)],
        (partial, conc, side, beyond, left, right, zm, zp),
    )
    below = shift(high, "gy", 1)
    above = shift(low, "gy", -1)
    slab = ((5, 8, 32, LANES), BF16)
    mobility, keep, xl, xh = call(
        rows_kernel,
        [brick, brick, slab, slab],
        (below, low, high, above, keep, beyond, beside),
    )
    before = shift(xh, "gx", 1)
    after = shift(xl, "gx", -1)
    fine = ((32, 32, RING), F32)
    middle = ((16, 32, RING), F32)
    own, chunk, *kept = call(
        down_kernel,
        [((160, LANES), F32), ((32, CHUNK, LANES), BF16)] + [fine] * 6 + [middle] * 5,
        (keep, conc, side, xl, xh, before, after),
        scratch=[fine] * 3 + [middle] * 3 + [((320, LANES), F32)],
    )
    place = jnp.stack([lax.axis_index("gx"), lax.axis_index("gy")]).astype(jnp.int32)
    chunk, place = lax.optimization_barrier((chunk, place))
    chunks = lax.all_to_all(chunk, ("gx", "gy"), 0, 0, tiled=True)
    plane = ((32, 16, LANES), F32)
    (out,) = call(
        up_kernel,
        [brick],
        (place, chunks, own) + tuple(kept),
        scratch=[plane] * 9
        + [brick, ((16, 32, LANES), F32), ((8, 32, LANES), F32)]
        + [middle] * 2
        + [fine] * 2,
        specs=[SMEM] + [VMEM] * 13,
    )
    return out, mobility


def solution(mesh):
    return jax.shard_map(
        body,
        mesh=mesh,
        in_specs=(
            P("gx", "gy", "gz"),
            P("gx", "gy", "gz"),
            P(None, "gx", "gy", "gz"),
            P("gx", "gy", "gz", None),
        ),
        out_specs=(P("gx", "gy", "gz"), P("gx", "gy", "gz")),
        check_vma=False,
    )
```

```python
import functools

import jax
import jax.numpy as jnp
from jax import lax
from jax.experimental import pallas as pl
from jax.experimental.pallas import tpu as pltpu
from jax.sharding import PartitionSpec as P

SLOTS = 8
BRICK = 16
OMEGA = 0.8
TAU = 256.0
LANES = 128
RING = 256
F32 = jnp.float32
BF16 = jnp.bfloat16
HIGH = lax.Precision.HIGHEST
VMEM = pl.BlockSpec(memory_space=pltpu.VMEM)
HBM = pl.BlockSpec(memory_space=pltpu.MemorySpace.HBM)
SMEM = pl.BlockSpec(memory_space=pltpu.SMEM)
COARSE = 51
COARSE_LOW = 10
MIDDLE = 70
HEAD = 26
CHUNK = 64


def call(kernel, outs, args, scratch=(), specs=None, places=None, limit=16, semaphores=0):
    specs = specs or [VMEM] * len(args)
    places = places or [VMEM] * len(outs)
    args = [
        pltpu.with_memory_space_constraint(arg, pltpu.MemorySpace.HBM) if spec is HBM else arg
        for arg, spec in zip(args, specs)
    ]
    scratches = [pltpu.VMEM(shape, dtype) for shape, dtype in scratch]
    if semaphores:
        scratches.append(pltpu.SemaphoreType.DMA((semaphores,)))
    return pl.pallas_call(
        kernel,
        out_shape=[
            pltpu.MemorySpace.HBM(*out) if place is HBM else jax.ShapeDtypeStruct(*out)
            for out, place in zip(outs, places)
        ],
        in_specs=specs,
        out_specs=places,
        scratch_shapes=scratches,
        compiler_params=pltpu.CompilerParams(vmem_limit_bytes=limit << 20),
    )(*args)


def roll(x, shift, axis):
    return pltpu.roll(x, shift % x.shape[axis], axis)


def iota(shape, axis):
    return lax.broadcasted_iota(jnp.int32, shape, axis)


def select_dot(a, picks):
    picks = picks.astype(BF16)
    total = None
    for _ in range(3):
        part = a.astype(BF16)
        a = a - part.astype(F32)
        term = jnp.dot(part, picks, preferred_element_type=F32)
        total = term if total is None else total + term
    return total


def lane_ids(ids_ref):
    ids = ids_ref[0, 0].astype(F32)
    spread = (iota((8, LANES), 1) // BRICK == iota((8, LANES), 0)).astype(F32)
    grains = lax.dot_general(
        ids, spread, (((0,), (0,)), ((), ())), precision=HIGH, preferred_element_type=F32
    )
    return jnp.floor(grains + 0.5)


def split_ids(grains):
    high = jnp.floor(grains * (1.0 / 64.0))
    return jnp.concatenate([high, grains - 64.0 * high], axis=0).astype(BF16)


def join_ids(rows):
    rows = rows.astype(F32)
    return rows[:8] * 64.0 + rows[8:]


def faces_kernel(
    conc_in, side_in, order_in, ids_in,
    conc_ref, side_ref, order_ref, ids_ref, xm_ref, xp_ref, ym_ref, sems,
):
    pairs = (
        (ids_in, ids_ref), (order_in, order_ref), (conc_in, conc_ref), (side_in, side_ref),
    )
    copies = [pltpu.make_async_copy(a, b, sems.at[k]) for k, (a, b) in enumerate(pairs)]
    for copy in copies:
        copy.start()
    copies[0].wait()
    copies[1].wait()
    grains = lane_ids(ids_ref)
    packed = split_ids(grains)
    for ref in (xm_ref, xp_ref, ym_ref):
        ref[SLOTS] = packed
    for slot in range(SLOTS):
        xm_ref[slot] = order_ref[slot, 0]
        xp_ref[slot] = order_ref[slot, 15]
        ym_ref[slot] = order_ref[slot].astype(F32)[:, 0, :].astype(BF16)
    copies[2].wait()
    copies[3].wait()


def square(x):
    return x * x


def inner_kernel(
    conc_ref, order_ref, ids_ref, work, yp_ref, zm_ref, zp_ref, weights,
):
    grains = lane_ids(ids_ref)
    zm_ref[16] = split_ids(jnp.broadcast_to(grains[:, 0:1], (8, LANES)))
    zp_ref[16] = split_ids(jnp.broadcast_to(grains[:, LANES - 1 :], (8, LANES)))
    slots = iota((16, LANES), 1)
    low = [jnp.zeros((16, LANES), F32)] * 16
    high = [jnp.zeros((16, LANES), F32)] * 16
    for slot in range(SLOTS):
        cells = order_ref[slot].astype(F32)
        yp_ref[slot] = cells[:, 15, :].astype(BF16)
        for x in range(16):
            low[x] = jnp.where(slots == slot, cells[x, :, 0:1], low[x])
            high[x] = jnp.where(slots == slot, cells[x, :, LANES - 1 :], high[x])
    for x in range(16):
        zm_ref[x] = low[x].astype(BF16)
        zp_ref[x] = high[x].astype(BF16)

    own = lane_ids(ids_ref)
    lane = iota((16, LANES), 1)
    row = iota((16, LANES), 0)
    last = lane % BRICK == BRICK - 1
    edge = (last | (lane % BRICK == 0)) & (lane != 0) & (lane != LANES - 1)

    lane8 = iota((8, LANES), 1)
    beside = jnp.where(
        lane8 % BRICK == BRICK - 1, roll(own, -BRICK, 1), roll(own, BRICK, 1)
    )
    for other in range(SLOTS):
        match = (own == beside[other : other + 1]).astype(F32)
        for slot in range(SLOTS):
            weights[slot * SLOTS + other] = jnp.broadcast_to(match[slot : slot + 1], (8, LANES))

    def doubled(block):
        return jnp.concatenate([block, block], axis=0)

    def plane(x, carry_in):
        conc = conc_ref[x]
        base = 1.0 + 8.0 * square(conc * (1.0 - conc))
        along_y = jnp.zeros((16, LANES), F32)
        along_z = jnp.zeros((16, LANES), F32)
        along_x = jnp.zeros((16, LANES), F32)
        centers = []
        facing = []
        above = min(x + 1, 15)
        for slot in range(SLOTS):
            here = order_ref[slot, x].astype(F32)
            there = order_ref[slot, above].astype(F32)
            centers.append(here)
            along_x = along_x + square(there - here)
            along_y = along_y + square(roll(here, -1, 0) - here)
            right = roll(here, -1, 1)
            along_z = along_z + square(right - here)
            facing.append(jnp.where(last, right, roll(here, 1, 1)))
        along_y = jnp.where(row == 15, 0.0, along_y)
        along_z = jnp.where(last, 0.0, along_z)
        remapped = jnp.zeros((16, LANES), F32)
        for slot in range(SLOTS):
            value = None
            for other in range(SLOTS):
                term = doubled(weights[slot * SLOTS + other]) * facing[other]
                value = term if value is None else value + term
            remapped = remapped + square(value - centers[slot])
        total = base + along_y + roll(along_y, 1, 0) + along_z + roll(along_z, 1, 1)
        total = total + jnp.where(edge, remapped, 0.0) + along_x + carry_in
        work[x] = total
        return along_x

    carry = jnp.zeros((16, LANES), F32)
    for x in range(16):
        carry = plane(x, carry)

def outer_kernel(
    work, conc_ref, side_ref, order_ref, ids_ref, xm_ref, xp_ref, yp_ref,
    own_yp_ref, own_zm_ref, own_zp_ref, mob_ref, beyond_ref, zm_out, zp_out,
):
    own = lane_ids(ids_ref)
    lane = iota((16, LANES), 1)
    row = iota((16, LANES), 0)

    def across(center, ids, facing, facing_ids):
        facing = [facing(other).astype(F32) for other in range(SLOTS)]
        total = None
        for slot in range(SLOTS):
            value = None
            for other in range(SLOTS):
                match = ids[slot : slot + 1] == facing_ids[other : other + 1]
                term = match.astype(F32) * facing[other]
                value = term if value is None else value + term
            part = square(value - center(slot).astype(F32))
            total = part if total is None else total + part
        return total

    first = work[0] + across(
        lambda k: order_ref[k, 0], own, lambda k: xm_ref[k], join_ids(xm_ref[SLOTS])
    )
    final = work[15] + across(
        lambda k: order_ref[k, 15], own, lambda k: xp_ref[k], join_ids(xp_ref[SLOTS])
    )
    above_ids = join_ids(yp_ref[SLOTS])
    top = across(lambda k: own_yp_ref[k], own, lambda k: yp_ref[k], above_ids)
    beyond = across(lambda k: yp_ref[k], above_ids, lambda k: own_yp_ref[k], own)
    beyond_ref[...] = beyond
    zm_out[33] = beyond.astype(BF16)
    zp_out[33] = beyond.astype(BF16)
    for x in range(16):
        value = first if x == 0 else final if x == 15 else work[x]
        value = value + jnp.where(row == 15, top[x : x + 1], 0.0)
        mob_ref[x] = value
        conc, side = conc_ref[x], side_ref[x]
        down = jnp.where(
            lane < 43, value, jnp.where(lane < 86, roll(conc, 43, 1), roll(side, 86, 1))
        )
        zm_out[x] = down.astype(BF16)
        up = jnp.where(
            lane >= 85, value, jnp.where(lane >= 42, roll(conc, -43, 1), roll(side, -86, 1))
        )
        zp_out[x] = up.astype(BF16)
    zm_out[16:33] = own_zm_ref[...]
    zp_out[16:33] = own_zp_ref[...]


def facing_squares(near_ref, far_ref, near_lane, far_lane):
    near = near_ref[:16].reshape(256, LANES)
    far = far_ref[:16].reshape(256, LANES)
    near_ids = join_ids(near_ref[16])
    far_ids = join_ids(far_ref[16])
    diagonal = iota((8, LANES), 0) == iota((8, LANES), 1)
    slots = iota((8, LANES), 1) < SLOTS

    def squares(cells, ids, others, other_ids, target):
        along = jnp.sum(jnp.where(diagonal, ids, 0.0), axis=0, keepdims=True)
        match = ((other_ids == along) & slots).astype(F32)
        match = jnp.concatenate([match, jnp.zeros((LANES - 8, LANES), F32)], axis=0)
        seen = jnp.dot(others, match.astype(BF16), preferred_element_type=F32)
        place = (iota((LANES, LANES), 1) == target).astype(F32)
        total = select_dot(square(seen - cells.astype(F32)), place)
        return total.reshape(16, 16, LANES)

    return (
        squares(near, near_ids, far, far_ids, near_lane),
        squares(far, far_ids, near, near_ids, far_lane),
    )


def split_kernel(
    mob_ref, conc_ref, side_ref, beyond_ref, left_ref, right_ref, zm_ref, zp_ref,
    keep_ref, beside_ref, low_ref, high_ref,
):
    own_low, far_low = facing_squares(zm_ref, left_ref.at[16:33], 0, LANES - 1)
    own_high, far_high = facing_squares(zp_ref, right_ref.at[16:33], LANES - 1, 0)
    mob = mob_ref[...] + own_low + own_high
    keep_ref[...] = mob
    down = (left_ref[:16].astype(F32) + far_low).astype(BF16)
    up = (right_ref[:16].astype(F32) + far_high).astype(BF16)
    for place, value in enumerate((mob, conc_ref[...], side_ref[...], down, up)):
        planes = pl.ds(16 * place, 16)
        low_ref[planes] = value[:, :8].astype(BF16)
        high_ref[planes] = value[:, 8:].astype(BF16)
    lane = iota((16, LANES), 1)
    down, up = left_ref[33].astype(F32), right_ref[33].astype(F32)
    beside = jnp.where(lane < 43, up, jnp.where(lane >= 85, down, 0.0))
    beside_ref[...] = beside
    beyond = beyond_ref[...]
    high = beyond.astype(BF16)
    rest = (beyond - high.astype(F32)).astype(BF16)
    for k, value in enumerate((high, rest, beside.astype(BF16))):
        high_ref[80 + 2 * k] = value[:8]
        high_ref[81 + 2 * k] = value[8:]


def rows_kernel(
    below_ref, low_ref, high_ref, above_ref, mob_ref, beyond_ref, beside_ref,
    out_ref, keep_ref, xl_ref, xh_ref,
):
    lane = iota((8, LANES), 1)
    first = iota((8, LANES), 0) == 0
    got = [
        jnp.concatenate([below_ref[80 + 2 * k], below_ref[81 + 2 * k]], axis=0).astype(F32)
        for k in range(3)
    ]
    missing = ((got[0] + got[1], got[2]), (beyond_ref[...], beside_ref[...]))
    for x in range(16):
        ref = xl_ref if x < 8 else xh_ref
        lines = []
        for main, beside in missing:
            main = jnp.where(first, main[x : x + 1], 0.0)
            beside = jnp.where(first, beside[x : x + 1], 0.0)
            down = jnp.where(lane >= 85, beside, 0.0)
            lines.append((main, None, None, down, jnp.where(lane < 43, beside, 0.0)))
        own = mob_ref[x, :8] + lines[0][0]
        for out in (out_ref, keep_ref):
            out[x, :8] = own
            out[x, 8:] = mob_ref[x, 8:]
        for place in range(5):
            plane = 16 * place + x
            near, far = low_ref[plane], above_ref[plane]
            if place == 0:
                near = own.astype(BF16)
            elif place >= 3:
                near = (near.astype(F32) + lines[0][place]).astype(BF16)
            if place in (0, 3, 4):
                far = (far.astype(F32) + lines[1][place]).astype(BF16)
            for k, value in enumerate((below_ref[plane], near, high_ref[plane], far)):
                ref[place, x % 8, pl.ds(8 * k, 8), :] = value


def partner(x, step, axis):
    upper = (iota(x.shape, axis) & step) != 0
    return jnp.where(upper, roll(x, step, axis), roll(x, -step, axis))


def pair_sum(x, step, axis):
    return x + partner(x, step, axis)


def upper_of(x, step, axis):
    upper = (iota(x.shape, axis) & step) != 0
    return jnp.where(upper, x, roll(x, -step, axis))


def middle_cell(lane):
    cell = lane
    for place, end in enumerate((-2, -1, 64, 65, -3, 66)):
        cell = jnp.where(lane == 64 + place, end, cell)
    return cell


def groups(items, size):
    items = list(items)
    return [items[k : k + size] for k in range(0, len(items), size)]


def sweep_planes(first, last, values, source, kx, ky, kz, step, use, size=8, planes=None):
    at = (lambda x: x) if planes is None else (lambda x: x % planes)
    before = kx[at(first - 1)] * (values[at(first)] - values[at(first - 1)])
    for xs in groups(range(first, last + 1), size):
        cells = [values[at(x)] for x in xs + [xs[-1] + 1]]
        flux_z = [kz[at(x)] * (roll(v, -step, 1) - v) for x, v in zip(xs, cells)]
        back_z = [roll(flux, step, 1) for flux in flux_z]
        left = []
        for k, x in enumerate(xs):
            value = cells[k]
            flux_x = kx[at(x)] * (cells[k + 1] - value)
            flux_y = ky[at(x)] * (roll(value, -step, 0) - value)
            total = (source[at(x)] - value) + (flux_x - before)
            total = total + (flux_y - roll(flux_y, step, 0))
            left.append(total + (flux_z[k] - back_z[k]))
            before = flux_x
        for k, x in enumerate(xs):
            use(at(x), cells[k], left[k])


INNER = {
    "side": (8, 16), "kx": (8, 15), "ky": (9, 14), "kz": (9, 14), "wd": (9, 14), "v": (10, 12),
    "k1x": (4, 7), "k1y": (5, 6), "k1z": (5, 6), "wd1": (5, 6), "f1": (6, 4),
    "mob": (8, 16), "v0": (8, 16), "s1": (9, 14), "r0": (11, 10),
}
KEPT = ("side", "kx", "ky", "kz", "wd", "v", "k1x", "k1y", "k1z", "wd1", "f1")
MIDDLE_ARRAYS = ("k1x", "k1y", "k1z", "wd1", "f1")


class Inner:
    def __init__(self, name, ref):
        self.low, self.count = INNER[name]
        self.ref = ref

    def __contains__(self, x):
        return self.low <= x < self.low + self.count

    def __getitem__(self, x):
        return self.ref[x - self.low]

    def __setitem__(self, x, value):
        self.ref[x - self.low] = value


class Joined:
    def __init__(self, inner, outer):
        self.inner = inner
        self.outer = outer

    def __getitem__(self, x):
        return self.inner[x] if x in self.inner else self.outer[x]

    def __setitem__(self, x, value):
        self.outer[x] = value


def assemble(xs, parts_of, mob, v0, side):
    lane = iota((32, LANES), 1)
    for some in groups(xs, 8):
        planes = []
        for x in some:
            parts = parts_of(x)
            down, up = parts[3], parts[4]
            beyond = jnp.where(lane < 43, up, jnp.where(lane >= 85, down, 1.0))
            iterate = jnp.where(
                lane < 43, roll(up, -43, 1), jnp.where(lane >= 85, roll(down, 43, 1), 0.0)
            )
            right = jnp.where(
                lane < 42, roll(up, -86, 1), jnp.where(lane >= 86, roll(down, 86, 1), 0.0)
            )
            planes.append(zip(parts, (beyond, iterate, right)))
        for x, plane in zip(some, planes):
            for target, pair in zip((mob, v0, side), plane):
                target[x] = jnp.concatenate(pair, axis=1)


def descend(a, coeffs, sweeps, middle_x, middle, middle_f):
    half = TAU / 2
    mob, kx_ref, ky_ref, kz_ref, wd_ref = (a[k] for k in ("mob", "kx", "ky", "kz", "wd"))
    for first, last in coeffs:
        before = half * (mob[first - 1] + mob[first])
        kx_ref[first - 1] = before
        for xs in groups(range(first, last + 1), 7):
            here = [mob[x] for x in xs + [xs[-1] + 1]]
            kz = [half * (cells + roll(cells, -1, 1)) for cells in here[:-1]]
            back = [roll(k, 1, 1) for k in kz]
            done = []
            for k, x in enumerate(xs):
                kx = half * (here[k] + here[k + 1])
                ky = half * (here[k] + roll(here[k], -1, 0))
                total = (kx + before) + (ky + roll(ky, 1, 0)) + (kz[k] + back[k])
                done.append((kx, ky, OMEGA / (1.0 + total)))
                before = kx
            for k, x in enumerate(xs):
                kx_ref[x], ky_ref[x], wd_ref[x] = done[k]
                kz_ref[x] = kz[k]

    def smooth(target):
        def use(x, value, left):
            target[x] = value + wd_ref[x] * left

        return use

    def keep(x, value, left):
        a["r0"][x] = left

    steps = (("v0", smooth(a["s1"])), ("s1", smooth(a["v"])), ("v", keep))
    for (name, use), runs in zip(steps, sweeps):
        for first, last in runs:
            sweep_planes(first, last, a[name], a["side"], kx_ref, ky_ref, kz_ref, 1, use)

    def pool(x):
        return pair_sum(pair_sum(x, 1, 0), 1, 1)

    k1x_ref = a["k1x"]
    for xs in groups(middle_x, 7):
        done = [pool(kx_ref[2 * i + 1]) * (1.0 / 16.0) for i in xs]
        for i, value in zip(xs, done):
            k1x_ref[i] = value
    for xs in groups(middle, 6):
        done = []
        for i in xs:
            x = 2 * i
            along_y = pair_sum(ky_ref[x] + ky_ref[x + 1], 1, 1)
            k1y = upper_of(along_y, 1, 0) * (1.0 / 16.0)
            along_z = pair_sum(kz_ref[x] + kz_ref[x + 1], 1, 0)
            k1z = upper_of(along_z, 1, 1) * (1.0 / 16.0)
            total = k1x_ref[i] + k1x_ref[i - 1]
            total = total + (k1y + roll(k1y, 2, 0)) + (k1z + roll(k1z, 2, 1))
            done.append((k1y, k1z, OMEGA / (1.0 + total)))
        for i, value in zip(xs, done):
            a["k1y"][i], a["k1z"][i], a["wd1"][i] = value
    res = a["r0"]
    for xs in groups(middle_f, 8):
        done = [pool(res[2 * i] + res[2 * i + 1]) * 0.125 for i in xs]
        for i, value in zip(xs, done):
            a["f1"][i] = value


def near_kernel(mob_in, conc_in, side_in, xl_ref, xh_ref, *refs):
    a = {name: Inner(name, ref) for name, ref in zip(INNER, refs)}
    own = (mob_in, conc_in, side_in)

    def parts_of(x):
        ref = xl_ref if x < 16 else xh_ref
        parts = [ref[place, x % 8].astype(F32) for place in range(5)]
        for place in range(3):
            part = parts[place]
            part = [part[:8], own[place][x - 8], part[24:]]
            parts[place] = jnp.concatenate(part, axis=0)
        return parts

    assemble(range(8, 24), parts_of, a["mob"], a["v0"], a["side"])
    descend(
        a, [(9, 22)], [[(9, 22)], [(10, 21)], [(11, 20)]], range(4, 11), range(5, 11), range(6, 10)
    )


def down_kernel(xm_ref, xp_ref, *refs):
    count = len(INNER)
    inner, refs = refs[:count], refs[count:]
    own_ref, chunk_ref, *outer = refs[: 2 + count]
    e0, e1, r1, rows = refs[2 + count :]
    a = {
        name: Joined(Inner(name, near), far) for name, near, far in zip(INNER, inner, outer)
    }

    def parts_of(x):
        ref = xm_ref if x < 8 else xp_ref
        return [ref[place, x % 8].astype(F32) for place in range(5)]

    outside = list(range(8)) + list(range(24, 32))
    assemble(outside, parts_of, a["mob"], a["v0"], a["side"])
    descend(
        a,
        [(2, 8), (23, 29)],
        [[(2, 8), (23, 29)], [(3, 9), (22, 28)], [(4, 10), (21, 27)]],
        [1, 2, 3, 11, 12, 13],
        [2, 3, 4, 11, 12, 13],
        [2, 3, 4, 5, 10, 11, 12, 13],
    )
    f1_ref, k1x_ref, k1y_ref, k1z_ref, wd1_ref = (
        a[k] for k in ("f1", "k1x", "k1y", "k1z", "wd1")
    )
    for i in range(2, 14):
        e0[i] = wd1_ref[i] * f1_ref[i]

    def smooth(target, weight):
        def use(x, value, left):
            target[x] = value + weight[x] * left

        return use

    sweep_planes(3, 12, e0, f1_ref, k1x_ref, k1y_ref, k1z_ref, 2, smooth(e1, wd1_ref))

    def keep_middle(x, value, left):
        r1[x] = left

    sweep_planes(4, 11, e1, f1_ref, k1x_ref, k1y_ref, k1z_ref, 2, keep_middle)

    src = iota((RING, LANES), 0)
    dst = iota((RING, LANES), 1)
    cell = jnp.where(src < 192, src, src - RING)
    coarse = (cell + 4 * COARSE_LOW) // 4
    there = ((cell & 3) == 0) & (coarse >= 0) & (coarse < COARSE)
    head = there & (coarse < HEAD)
    tail = there & (coarse >= HEAD)
    sides = [there & (coarse == dst), there & (coarse + COARSE == dst)]
    picks0 = sides + [head & (coarse + 2 * COARSE == dst)]
    picks1 = sides + [tail & (coarse + 2 * COARSE - HEAD == dst)]
    picks0 = jnp.concatenate([pick.astype(F32) for pick in picks0], axis=0).astype(BF16)
    picks1 = jnp.concatenate([pick.astype(F32) for pick in picks1], axis=0).astype(BF16)
    pick_middle = ((cell == 2 * middle_cell(dst)) & (dst < MIDDLE)).astype(F32)
    firsts = []
    seconds = []
    for j in range(4):
        i = 4 + 2 * j
        f2 = pair_sum(pair_sum(r1[i] + r1[i + 1], 2, 0), 2, 1) * 0.125
        k2x = pair_sum(pair_sum(k1x_ref[i + 1], 2, 0), 2, 1) * (1.0 / 16.0)
        k2y = pair_sum(k1y_ref[i] + k1y_ref[i + 1], 2, 1)
        k2y = upper_of(k2y, 2, 0) * (1.0 / 16.0)
        k2z = pair_sum(k1z_ref[i] + k1z_ref[i + 1], 2, 0)
        k2z = upper_of(k2z, 2, 1) * (1.0 / 16.0)
        f2, k2x, k2y, k2z = (cells[8:24] for cells in (f2, k2x, k2y, k2z))
        k2z = k2z.astype(BF16)
        high = f2.astype(BF16)
        low = (f2 - high.astype(F32)).astype(BF16)
        firsts.append(jnp.concatenate([high, low, k2z], axis=1))
        seconds.append(jnp.concatenate([k2x.astype(BF16), k2y.astype(BF16), k2z], axis=1))
    firsts = jnp.concatenate(firsts, axis=0)
    seconds = jnp.concatenate(seconds, axis=0)
    rows[pl.ds(0, 64), :] = jnp.dot(firsts, picks0, preferred_element_type=F32)
    rows[pl.ds(64, 64), :] = jnp.dot(seconds, picks1, preferred_element_type=F32)
    coarse = rows[pl.ds(0, 32, stride=4), :]
    rows[...] = select_dot(
        jnp.concatenate([e1[i] for i in range(3, 13)], axis=0), pick_middle
    )
    own_ref[...] = rows[pl.ds(0, 160, stride=2), :]

    blocks = [own_ref[pl.ds(16 * (1 + x) + 4, 8), :] for x in (1, 2, 5, 6)]
    for y in (1, 2):
        lines = [(x, k) for k in (y, y + 4) for x in (0, 3, 4, 7)]
        lines = [own_ref[pl.ds(16 * (1 + x) + 4 + k, 1), :] for x, k in lines]
        blocks.append(jnp.concatenate(lines, axis=0))
    narrow = iota((8, LANES), 1)
    middle = []
    for k in (0, 2, 4):
        middle.append(jnp.where(narrow < 64, blocks[k], roll(blocks[k + 1], 64, 1)))
    ends = jnp.zeros((8, LANES), F32)
    for k in range(6):
        ends = jnp.where(narrow // 4 == k, roll(blocks[k], 4 * k - 64, 1), ends)
    chunk = jnp.concatenate([coarse] + middle + [ends], axis=0).astype(BF16)
    for k in range(32):
        chunk_ref[k] = chunk


def up_kernel(
    place_ref, all_ref, own_ref, *refs
):
    count = len(KEPT)
    joined = [
        Joined(Inner(name, near), far)
        for name, near, far in zip(KEPT, refs[:count], refs[count : 2 * count])
    ]
    side_ref, kx_ref, ky_ref, kz_ref, wd_ref, v_ref = joined[:6]
    k1x_ref, k1y_ref, k1z_ref, wd1_ref, f1_ref = joined[6:]
    out_ref, pair0, pair1, c2x, c2y, c2z, wd2, f2, ea, eb = refs[2 * count : 2 * count + 10]
    mid, tall, lean, e1a, e1b, va, vb = refs[2 * count + 10 :]
    gx = place_ref[0]
    gy = place_ref[1]

    def source(dx, dy):
        return ((gx + dx + 8) & 7) * 4 + ((gy + dy + 4) & 3)

    for p in (0, 1, 2, 3, 4, 6, 7):
        for q in range(4):
            s = source(p - 1, q - 1)
            first = all_ref[s, pl.ds(0, 16), :].astype(F32)
            second = all_ref[s, pl.ds(16, 16), :].astype(F32)
            for i in range(4):
                pair0[4 * p + i, pl.ds(4 * q, 4), :] = first[4 * i : 4 * i + 4]
                pair1[4 * p + i, pl.ds(4 * q, 4), :] = second[4 * i : 4 * i + 4]
    for i in range(3, 13):
        mid[i] = own_ref[pl.ds(16 * (i - 3), 16), :]
    narrow = iota((8, LANES), 1)
    for p in (-1, 0, 1):
        for q in (-1, 0, 1):
            if p == 0 and q == 0:
                continue
            cells = all_ref[source(p, q), pl.ds(32, 32), :].astype(F32)
            ends = cells[24:]

            def block(k):
                main = cells[8 * (k // 2) : 8 * (k // 2) + 8]
                if k % 2:
                    main = roll(main, 64, 1)
                end = jnp.where(narrow < 68, roll(ends, 64 - 4 * k, 1), 0.0)
                return jnp.where(narrow < 64, main, end)

            for k, i in {-1: ((2, 1), (3, 2)), 0: (), 1: ((0, 13), (1, 14))}[p]:
                part = block(k)
                if q == -1:
                    mid[i, pl.ds(0, 4), :] = part[4:]
                elif q == 0:
                    mid[i, pl.ds(4, 8), :] = part
                else:
                    mid[i, pl.ds(12, 4), :] = part[:4]
            if q == 0:
                continue
            for depth in (0, 1):
                row = (1 if q == -1 else 13) + depth
                half = 4 if q == -1 else 0
                thin = block(4 + depth)
                for k, x in enumerate((0, 3, 4, 7)):
                    i = 8 * p + x + 4
                    if 3 <= i <= 12:
                        mid[i, pl.ds(row, 1), :] = thin[half + k : half + k + 1]
            if p == 0:
                for k, x in enumerate((1, 2, 5, 6)):
                    line = 5 if q == -1 else 1
                    part = block(k)
                    for depth in (0, 1):
                        row = (1 if q == -1 else 13) + depth
                        mid[x + 4, pl.ds(row, 1), :] = part[line + depth : line + depth + 1]

    used = iota((16, LANES), 1) < COARSE
    head = iota((16, LANES), 1) < HEAD
    for x in range(-6, 17):
        k = x % 32
        first = pair0[k]
        second = pair1[k]
        f2[k] = jnp.where(used, first + roll(first, -COARSE, 1), 0.0)
        c2x[k] = jnp.where(used, second, 0.0)
        c2y[k] = jnp.where(used, roll(second, -COARSE, 1), 0.0)
        last = jnp.where(
            head, roll(first, -2 * COARSE, 1), roll(second, HEAD - 2 * COARSE, 1)
        )
        c2z[k] = jnp.where(used, last, 0.0)
    for xs in groups(range(-5, 17), 11):
        done = []
        for x in xs:
            k = x % 32
            ky = c2y[k]
            kz = c2z[k]
            total = c2x[k] + c2x[(x - 1) % 32]
            total = total + (ky + roll(ky, 1, 0)) + (kz + roll(kz, 1, 1))
            weight = OMEGA / (1.0 + total)
            done.append((weight, weight * f2[k]))
        for x, value in zip(xs, done):
            wd2[x % 32], ea[x % 32] = value

    def smooth(target, weight):
        def use(x, value, left):
            target[x] = value + weight[x] * left

        return use

    old, new = ea, eb
    for reach in range(6, -1, -1):
        sweep_planes(
            2 - reach, 9 + reach, old, f2, c2x, c2y, c2z, 1, smooth(new, wd2), 10, 32
        )
        old, new = new, old

    lane = iota((8, LANES), 1)
    for j in range(8):
        line = roll(old[2 + j, pl.ds(2, 8), :], MIDDLE, 1)
        line = jnp.where((lane >= MIDDLE) & (lane < MIDDLE + COARSE), line, 0.0)
        for k in range(4):
            lean[j, pl.ds(k, 8, stride=4), :] = line
    for i in range(1, 15):
        line = mid[i]
        for k in range(2):
            tall[i, pl.ds(k, 16, stride=2), :] = line
    src = iota((LANES, RING), 0)
    dst = iota((LANES, RING), 1)
    cell = jnp.where(dst < 192, dst, dst - RING)
    middle = (src < MIDDLE) & ((cell + 64) // 2 - 32 == middle_cell(src))
    coarse = (cell >= -4 * COARSE_LOW) & (src >= MIDDLE) & (src < MIDDLE + COARSE)
    coarse = coarse & ((cell + 4 * COARSE_LOW) // 4 == src - MIDDLE)
    spread = (middle | coarse).astype(F32)
    narrow = iota((32, LANES), 1) < MIDDLE
    packed = [jnp.where(narrow, tall[i], lean[i // 2]) for i in range(1, 15)]
    widened = select_dot(jnp.concatenate(packed, axis=0), spread)
    for i in range(1, 15):
        e1a[i] = widened[32 * (i - 1) : 32 * i]

    sweep_planes(2, 13, e1a, f1_ref, k1x_ref, k1y_ref, k1z_ref, 2, smooth(e1b, wd1_ref))
    sweep_planes(3, 12, e1b, f1_ref, k1x_ref, k1y_ref, k1z_ref, 2, smooth(e1a, wd1_ref))
    for x in range(6, 26):
        va[x] = v_ref[x] + e1a[x // 2]
    sweep_planes(7, 24, va, side_ref, kx_ref, ky_ref, kz_ref, 1, smooth(vb, wd_ref))

    def finish(x, value, left):
        new = value + wd_ref[x] * left
        out_ref[x - 8] = new[8:24, :LANES]

    sweep_planes(8, 23, vb, side_ref, kx_ref, ky_ref, kz_ref, 1, finish)


def shift(x, axis, direction):
    count = lax.axis_size(axis)
    return lax.ppermute(x, axis, [(i, (i + direction) % count) for i in range(count)])


def body(conc, right_side, order_field, grain_ids):
    face = ((9, 16, LANES), BF16)
    zface = ((17, 16, LANES), BF16)
    brick = ((16, 16, LANES), F32)
    conc, side, order, ids, xm, xp, ym = call(
        faces_kernel,
        [brick, brick, ((8, 16, 16, LANES), BF16), ((1, 1, 8, 8), jnp.int32)] + [face] * 3,
        (conc, right_side, order_field, grain_ids),
        specs=[HBM] * 4,
        semaphores=4,
    )
    above = shift(ym, "gy", -1)
    before = shift(xp, "gx", 1)
    after = shift(xm, "gx", -1)
    inner, yp, zm, zp = call(
        inner_kernel,
        [brick, ((8, 16, LANES), BF16), zface, zface],
        (conc, order, ids),
        scratch=[((64, 8, LANES), F32)],
    )
    line = ((16, LANES), F32)
    payload = ((34, 16, LANES), BF16)
    partial, beyond, send_zm, send_zp = call(
        outer_kernel,
        [brick, line, payload, payload],
        (inner, conc, side, order, ids, before, after, above, yp, zm, zp),
    )
    left = shift(send_zp, "gz", 1)
    right = shift(send_zm, "gz", -1)
    keep, beside, low, high = call(
        split_kernel,
        [brick, line, ((80, 8, LANES), BF16), ((86, 8, LANES), BF16)],
        (partial, conc, side, beyond, left, right, zm, zp),
    )
    below = shift(high, "gy", 1)
    above = shift(low, "gy", -1)
    slab = ((5, 8, 32, LANES), BF16)
    mobility, keep, xl, xh = call(
        rows_kernel,
        [brick, brick, slab, slab],
        (below, low, high, above, keep, beyond, beside),
    )
    before = shift(xh, "gx", 1)
    after = shift(xl, "gx", -1)
    fine = ((32, 32, RING), F32)
    middle = ((16, 32, RING), F32)
    inner = call(
        near_kernel,
        [((INNER[name][1], 32, RING), F32) for name in INNER],
        (keep, conc, side, xl, xh),
    )
    outer = [middle if name in MIDDLE_ARRAYS else fine for name in INNER]
    own, chunk, *outer = call(
        down_kernel,
        [((160, LANES), F32), ((32, CHUNK, LANES), BF16)] + outer[: len(KEPT)],
        (before, after) + tuple(inner),
        scratch=outer[len(KEPT) :] + [middle] * 3 + [((320, LANES), F32)],
    )
    kept = tuple(inner[: len(KEPT)]) + tuple(outer)
    place = jnp.stack([lax.axis_index("gx"), lax.axis_index("gy")]).astype(jnp.int32)
    chunk, place = lax.optimization_barrier((chunk, place))
    chunks = lax.all_to_all(chunk, ("gx", "gy"), 0, 0, tiled=True)
    plane = ((32, 16, LANES), F32)
    (out,) = call(
        up_kernel,
        [brick],
        (place, chunks, own) + kept,
        scratch=[plane] * 9
        + [brick, ((16, 32, LANES), F32), ((8, 32, LANES), F32)]
        + [middle] * 2
        + [fine] * 2,
        specs=[SMEM] + [VMEM] * (2 + len(kept)),
    )
    return out, mobility


def solution(mesh):
    return jax.shard_map(
        body,
        mesh=mesh,
        in_specs=(
            P("gx", "gy", "gz"),
            P("gx", "gy", "gz"),
            P(None, "gx", "gy", "gz"),
            P("gx", "gy", "gz", None),
        ),
        out_specs=(P("gx", "gy", "gz"), P("gx", "gy", "gz")),
        check_vma=False,
    )
```

```python
import functools

import jax
import jax.numpy as jnp
from jax import lax
from jax.experimental import pallas as pl
from jax.experimental.pallas import tpu as pltpu
from jax.sharding import PartitionSpec as P

SLOTS = 8
BRICK = 16
OMEGA = 0.8
TAU = 256.0
LANES = 128
RING = 256
F32 = jnp.float32
BF16 = jnp.bfloat16
HIGH = lax.Precision.HIGHEST
VMEM = pl.BlockSpec(memory_space=pltpu.VMEM)
HBM = pl.BlockSpec(memory_space=pltpu.MemorySpace.HBM)
SMEM = pl.BlockSpec(memory_space=pltpu.SMEM)
COARSE = 51
COARSE_LOW = 10
MIDDLE = 70
HEAD = 26
CHUNK = 64


def call(kernel, outs, args, scratch=(), specs=None, places=None, limit=16, semaphores=0):
    specs = specs or [VMEM] * len(args)
    places = places or [VMEM] * len(outs)
    args = [
        pltpu.with_memory_space_constraint(arg, pltpu.MemorySpace.HBM) if spec is HBM else arg
        for arg, spec in zip(args, specs)
    ]
    scratches = [pltpu.VMEM(shape, dtype) for shape, dtype in scratch]
    if semaphores:
        scratches.append(pltpu.SemaphoreType.DMA((semaphores,)))
    return pl.pallas_call(
        kernel,
        out_shape=[
            pltpu.MemorySpace.HBM(*out) if place is HBM else jax.ShapeDtypeStruct(*out)
            for out, place in zip(outs, places)
        ],
        in_specs=specs,
        out_specs=places,
        scratch_shapes=scratches,
        compiler_params=pltpu.CompilerParams(vmem_limit_bytes=limit << 20),
    )(*args)


def roll(x, shift, axis):
    return pltpu.roll(x, shift % x.shape[axis], axis)


def iota(shape, axis):
    return lax.broadcasted_iota(jnp.int32, shape, axis)


def select_dot(a, picks):
    picks = picks.astype(BF16)
    total = None
    for _ in range(3):
        part = a.astype(BF16)
        a = a - part.astype(F32)
        term = jnp.dot(part, picks, preferred_element_type=F32)
        total = term if total is None else total + term
    return total


def lane_ids(ids_ref):
    ids = ids_ref[0, 0].astype(F32)
    spread = (iota((8, LANES), 1) // BRICK == iota((8, LANES), 0)).astype(F32)
    grains = lax.dot_general(
        ids, spread, (((0,), (0,)), ((), ())), precision=HIGH, preferred_element_type=F32
    )
    return jnp.floor(grains + 0.5)


def split_ids(grains):
    high = jnp.floor(grains * (1.0 / 64.0))
    return jnp.concatenate([high, grains - 64.0 * high], axis=0).astype(BF16)


def join_ids(rows):
    rows = rows.astype(F32)
    return rows[:8] * 64.0 + rows[8:]


def faces_kernel(
    conc_in, side_in, order_in, ids_in,
    conc_ref, side_ref, order_ref, ids_ref, xm_ref, xp_ref, ym_ref, sems,
):
    pairs = (
        (ids_in, ids_ref), (order_in, order_ref), (conc_in, conc_ref), (side_in, side_ref),
    )
    copies = [pltpu.make_async_copy(a, b, sems.at[k]) for k, (a, b) in enumerate(pairs)]
    for copy in copies:
        copy.start()
    copies[0].wait()
    copies[1].wait()
    grains = lane_ids(ids_ref)
    packed = split_ids(grains)
    for ref in (xm_ref, xp_ref, ym_ref):
        ref[SLOTS] = packed
    for slot in range(SLOTS):
        xm_ref[slot] = order_ref[slot, 0]
        xp_ref[slot] = order_ref[slot, 15]
        ym_ref[slot] = order_ref[slot].astype(F32)[:, 0, :].astype(BF16)
    copies[2].wait()
    copies[3].wait()


def square(x):
    return x * x


def inner_kernel(
    conc_ref, order_ref, ids_ref, work, yp_ref, zm_ref, zp_ref, weights,
):
    grains = lane_ids(ids_ref)
    zm_ref[16] = split_ids(jnp.broadcast_to(grains[:, 0:1], (8, LANES)))
    zp_ref[16] = split_ids(jnp.broadcast_to(grains[:, LANES - 1 :], (8, LANES)))
    slots = iota((16, LANES), 1)
    low = [jnp.zeros((16, LANES), F32)] * 16
    high = [jnp.zeros((16, LANES), F32)] * 16
    for slot in range(SLOTS):
        cells = order_ref[slot].astype(F32)
        yp_ref[slot] = cells[:, 15, :].astype(BF16)
        for x in range(16):
            low[x] = jnp.where(slots == slot, cells[x, :, 0:1], low[x])
            high[x] = jnp.where(slots == slot, cells[x, :, LANES - 1 :], high[x])
    for x in range(16):
        zm_ref[x] = low[x].astype(BF16)
        zp_ref[x] = high[x].astype(BF16)

    own = lane_ids(ids_ref)
    lane = iota((16, LANES), 1)
    row = iota((16, LANES), 0)
    last = lane % BRICK == BRICK - 1
    edge = (last | (lane % BRICK == 0)) & (lane != 0) & (lane != LANES - 1)

    lane8 = iota((8, LANES), 1)
    beside = jnp.where(
        lane8 % BRICK == BRICK - 1, roll(own, -BRICK, 1), roll(own, BRICK, 1)
    )
    for other in range(SLOTS):
        match = (own == beside[other : other + 1]).astype(F32)
        for slot in range(SLOTS):
            weights[slot * SLOTS + other] = jnp.broadcast_to(match[slot : slot + 1], (8, LANES))

    def doubled(block):
        return jnp.concatenate([block, block], axis=0)

    def plane(x, carry_in):
        conc = conc_ref[x]
        base = 1.0 + 8.0 * square(conc * (1.0 - conc))
        along_y = jnp.zeros((16, LANES), F32)
        along_z = jnp.zeros((16, LANES), F32)
        along_x = jnp.zeros((16, LANES), F32)
        centers = []
        facing = []
        above = min(x + 1, 15)
        for slot in range(SLOTS):
            here = order_ref[slot, x].astype(F32)
            there = order_ref[slot, above].astype(F32)
            centers.append(here)
            along_x = along_x + square(there - here)
            along_y = along_y + square(roll(here, -1, 0) - here)
            right = roll(here, -1, 1)
            along_z = along_z + square(right - here)
            facing.append(jnp.where(last, right, roll(here, 1, 1)))
        along_y = jnp.where(row == 15, 0.0, along_y)
        along_z = jnp.where(last, 0.0, along_z)
        remapped = jnp.zeros((16, LANES), F32)
        for slot in range(SLOTS):
            value = None
            for other in range(SLOTS):
                term = doubled(weights[slot * SLOTS + other]) * facing[other]
                value = term if value is None else value + term
            remapped = remapped + square(value - centers[slot])
        total = base + along_y + roll(along_y, 1, 0) + along_z + roll(along_z, 1, 1)
        total = total + jnp.where(edge, remapped, 0.0) + along_x + carry_in
        work[x] = total
        return along_x

    carry = jnp.zeros((16, LANES), F32)
    for x in range(16):
        carry = plane(x, carry)

def outer_kernel(
    work, conc_ref, side_ref, order_ref, ids_ref, xm_ref, xp_ref, yp_ref,
    own_yp_ref, own_zm_ref, own_zp_ref, mob_ref, beyond_ref, zm_out, zp_out,
):
    own = lane_ids(ids_ref)
    lane = iota((16, LANES), 1)
    row = iota((16, LANES), 0)

    def across(center, ids, facing, facing_ids):
        facing = [facing(other).astype(F32) for other in range(SLOTS)]
        total = None
        for slot in range(SLOTS):
            value = None
            for other in range(SLOTS):
                match = ids[slot : slot + 1] == facing_ids[other : other + 1]
                term = match.astype(F32) * facing[other]
                value = term if value is None else value + term
            part = square(value - center(slot).astype(F32))
            total = part if total is None else total + part
        return total

    first = work[0] + across(
        lambda k: order_ref[k, 0], own, lambda k: xm_ref[k], join_ids(xm_ref[SLOTS])
    )
    final = work[15] + across(
        lambda k: order_ref[k, 15], own, lambda k: xp_ref[k], join_ids(xp_ref[SLOTS])
    )
    above_ids = join_ids(yp_ref[SLOTS])
    top = across(lambda k: own_yp_ref[k], own, lambda k: yp_ref[k], above_ids)
    beyond = across(lambda k: yp_ref[k], above_ids, lambda k: own_yp_ref[k], own)
    beyond_ref[...] = beyond
    zm_out[33] = beyond.astype(BF16)
    zp_out[33] = beyond.astype(BF16)
    for x in range(16):
        value = first if x == 0 else final if x == 15 else work[x]
        value = value + jnp.where(row == 15, top[x : x + 1], 0.0)
        mob_ref[x] = value
        conc, side = conc_ref[x], side_ref[x]
        down = jnp.where(
            lane < 43, value, jnp.where(lane < 86, roll(conc, 43, 1), roll(side, 86, 1))
        )
        zm_out[x] = down.astype(BF16)
        up = jnp.where(
            lane >= 85, value, jnp.where(lane >= 42, roll(conc, -43, 1), roll(side, -86, 1))
        )
        zp_out[x] = up.astype(BF16)
    zm_out[16:33] = own_zm_ref[...]
    zp_out[16:33] = own_zp_ref[...]


def facing_squares(near_ref, far_ref, near_lane, far_lane):
    near = near_ref[:16].reshape(256, LANES)
    far = far_ref[:16].reshape(256, LANES)
    near_ids = join_ids(near_ref[16])
    far_ids = join_ids(far_ref[16])
    diagonal = iota((8, LANES), 0) == iota((8, LANES), 1)
    slots = iota((8, LANES), 1) < SLOTS

    def squares(cells, ids, others, other_ids, target):
        along = jnp.sum(jnp.where(diagonal, ids, 0.0), axis=0, keepdims=True)
        match = ((other_ids == along) & slots).astype(F32)
        match = jnp.concatenate([match, jnp.zeros((LANES - 8, LANES), F32)], axis=0)
        seen = jnp.dot(others, match.astype(BF16), preferred_element_type=F32)
        place = (iota((LANES, LANES), 1) == target).astype(F32)
        total = select_dot(square(seen - cells.astype(F32)), place)
        return total.reshape(16, 16, LANES)

    return (
        squares(near, near_ids, far, far_ids, near_lane),
        squares(far, far_ids, near, near_ids, far_lane),
    )


def split_kernel(
    mob_ref, conc_ref, side_ref, beyond_ref, left_ref, right_ref, zm_ref, zp_ref,
    keep_ref, beside_ref, low_ref, high_ref,
):
    own_low, far_low = facing_squares(zm_ref, left_ref.at[16:33], 0, LANES - 1)
    own_high, far_high = facing_squares(zp_ref, right_ref.at[16:33], LANES - 1, 0)
    mob = mob_ref[...] + own_low + own_high
    keep_ref[...] = mob
    down = (left_ref[:16].astype(F32) + far_low).astype(BF16)
    up = (right_ref[:16].astype(F32) + far_high).astype(BF16)
    for place, value in enumerate((mob, conc_ref[...], side_ref[...], down, up)):
        planes = pl.ds(16 * place, 16)
        low_ref[planes] = value[:, :8].astype(BF16)
        high_ref[planes] = value[:, 8:].astype(BF16)
    lane = iota((16, LANES), 1)
    down, up = left_ref[33].astype(F32), right_ref[33].astype(F32)
    beside = jnp.where(lane < 43, up, jnp.where(lane >= 85, down, 0.0))
    beside_ref[...] = beside
    beyond = beyond_ref[...]
    high = beyond.astype(BF16)
    rest = (beyond - high.astype(F32)).astype(BF16)
    for k, value in enumerate((high, rest, beside.astype(BF16))):
        high_ref[80 + 2 * k] = value[:8]
        high_ref[81 + 2 * k] = value[8:]


def rows_kernel(
    below_ref, low_ref, high_ref, above_ref, mob_ref, beyond_ref, beside_ref,
    keep_ref, xl_ref, xh_ref,
):
    lane = iota((8, LANES), 1)
    first = iota((8, LANES), 0) == 0
    got = [
        jnp.concatenate([below_ref[80 + 2 * k], below_ref[81 + 2 * k]], axis=0).astype(F32)
        for k in range(3)
    ]
    missing = ((got[0] + got[1], got[2]), (beyond_ref[...], beside_ref[...]))
    for x in range(16):
        ref = xl_ref if x < 8 else xh_ref
        lines = []
        for main, beside in missing:
            main = jnp.where(first, main[x : x + 1], 0.0)
            beside = jnp.where(first, beside[x : x + 1], 0.0)
            down = jnp.where(lane >= 85, beside, 0.0)
            lines.append((main, None, None, down, jnp.where(lane < 43, beside, 0.0)))
        own = mob_ref[x, :8] + lines[0][0]
        keep_ref[x, :8] = own
        keep_ref[x, 8:] = mob_ref[x, 8:]
        for place in range(5):
            plane = 16 * place + x
            near, far = low_ref[plane], above_ref[plane]
            if place == 0:
                near = own.astype(BF16)
            elif place >= 3:
                near = (near.astype(F32) + lines[0][place]).astype(BF16)
            if place in (0, 3, 4):
                far = (far.astype(F32) + lines[1][place]).astype(BF16)
            for k, value in enumerate((below_ref[plane], near, high_ref[plane], far)):
                ref[place, x % 8, pl.ds(8 * k, 8), :] = value


def partner(x, step, axis):
    upper = (iota(x.shape, axis) & step) != 0
    return jnp.where(upper, roll(x, step, axis), roll(x, -step, axis))


def pair_sum(x, step, axis):
    return x + partner(x, step, axis)


def upper_of(x, step, axis):
    upper = (iota(x.shape, axis) & step) != 0
    return jnp.where(upper, x, roll(x, -step, axis))


def middle_cell(lane):
    cell = lane
    for place, end in enumerate((-2, -1, 64, 65, -3, 66)):
        cell = jnp.where(lane == 64 + place, end, cell)
    return cell


def groups(items, size):
    items = list(items)
    return [items[k : k + size] for k in range(0, len(items), size)]


def sweep_planes(first, last, values, source, kx, ky, kz, step, use, size=8, planes=None):
    at = (lambda x: x) if planes is None else (lambda x: x % planes)
    before = kx[at(first - 1)] * (values[at(first)] - values[at(first - 1)])
    for xs in groups(range(first, last + 1), size):
        cells = [values[at(x)] for x in xs + [xs[-1] + 1]]
        flux_z = [kz[at(x)] * (roll(v, -step, 1) - v) for x, v in zip(xs, cells)]
        back_z = [roll(flux, step, 1) for flux in flux_z]
        left = []
        for k, x in enumerate(xs):
            value = cells[k]
            flux_x = kx[at(x)] * (cells[k + 1] - value)
            flux_y = ky[at(x)] * (roll(value, -step, 0) - value)
            total = (source[at(x)] - value) + (flux_x - before)
            total = total + (flux_y - roll(flux_y, step, 0))
            left.append(total + (flux_z[k] - back_z[k]))
            before = flux_x
        for k, x in enumerate(xs):
            use(at(x), cells[k], left[k])


INNER = {
    "side": (8, 16), "kx": (8, 15), "ky": (9, 14), "kz": (9, 14), "wd": (9, 14), "v": (10, 12),
    "k1x": (4, 7), "k1y": (5, 6), "k1z": (5, 6), "wd1": (5, 6), "f1": (6, 4),
    "mob": (8, 16), "v0": (8, 16), "s1": (9, 14), "r0": (11, 10),
}
KEPT = ("side", "kx", "ky", "kz", "wd", "v", "k1x", "k1y", "k1z", "wd1", "f1")
MIDDLE_ARRAYS = ("k1x", "k1y", "k1z", "wd1", "f1")


class Inner:
    def __init__(self, name, ref):
        self.low, self.count = INNER[name]
        self.ref = ref

    def __contains__(self, x):
        return self.low <= x < self.low + self.count

    def __getitem__(self, x):
        return self.ref[x - self.low]

    def __setitem__(self, x, value):
        self.ref[x - self.low] = value


class Joined:
    def __init__(self, inner, outer):
        self.inner = inner
        self.outer = outer

    def __getitem__(self, x):
        return self.inner[x] if x in self.inner else self.outer[x]

    def __setitem__(self, x, value):
        self.outer[x] = value


def assemble(xs, parts_of, mob, v0, side):
    lane = iota((32, LANES), 1)
    for some in groups(xs, 8):
        planes = []
        for x in some:
            parts = parts_of(x)
            down, up = parts[3], parts[4]
            beyond = jnp.where(lane < 43, up, jnp.where(lane >= 85, down, 1.0))
            iterate = jnp.where(
                lane < 43, roll(up, -43, 1), jnp.where(lane >= 85, roll(down, 43, 1), 0.0)
            )
            right = jnp.where(
                lane < 42, roll(up, -86, 1), jnp.where(lane >= 86, roll(down, 86, 1), 0.0)
            )
            planes.append(zip(parts, (beyond, iterate, right)))
        for x, plane in zip(some, planes):
            for target, pair in zip((mob, v0, side), plane):
                target[x] = jnp.concatenate(pair, axis=1)


def descend(a, coeffs, sweeps, middle_x, middle, middle_f):
    half = TAU / 2
    mob, kx_ref, ky_ref, kz_ref, wd_ref = (a[k] for k in ("mob", "kx", "ky", "kz", "wd"))
    for first, last in coeffs:
        before = half * (mob[first - 1] + mob[first])
        kx_ref[first - 1] = before
        for xs in groups(range(first, last + 1), 7):
            here = [mob[x] for x in xs + [xs[-1] + 1]]
            kz = [half * (cells + roll(cells, -1, 1)) for cells in here[:-1]]
            back = [roll(k, 1, 1) for k in kz]
            done = []
            for k, x in enumerate(xs):
                kx = half * (here[k] + here[k + 1])
                ky = half * (here[k] + roll(here[k], -1, 0))
                total = (kx + before) + (ky + roll(ky, 1, 0)) + (kz[k] + back[k])
                done.append((kx, ky, OMEGA / (1.0 + total)))
                before = kx
            for k, x in enumerate(xs):
                kx_ref[x], ky_ref[x], wd_ref[x] = done[k]
                kz_ref[x] = kz[k]

    def smooth(target):
        def use(x, value, left):
            target[x] = value + wd_ref[x] * left

        return use

    def keep(x, value, left):
        a["r0"][x] = left

    steps = (("v0", smooth(a["s1"])), ("s1", smooth(a["v"])), ("v", keep))
    for (name, use), runs in zip(steps, sweeps):
        for first, last in runs:
            sweep_planes(first, last, a[name], a["side"], kx_ref, ky_ref, kz_ref, 1, use)

    def pool(x):
        return pair_sum(pair_sum(x, 1, 0), 1, 1)

    k1x_ref = a["k1x"]
    for xs in groups(middle_x, 7):
        done = [pool(kx_ref[2 * i + 1]) * (1.0 / 16.0) for i in xs]
        for i, value in zip(xs, done):
            k1x_ref[i] = value
    for xs in groups(middle, 6):
        done = []
        for i in xs:
            x = 2 * i
            along_y = pair_sum(ky_ref[x] + ky_ref[x + 1], 1, 1)
            k1y = upper_of(along_y, 1, 0) * (1.0 / 16.0)
            along_z = pair_sum(kz_ref[x] + kz_ref[x + 1], 1, 0)
            k1z = upper_of(along_z, 1, 1) * (1.0 / 16.0)
            total = k1x_ref[i] + k1x_ref[i - 1]
            total = total + (k1y + roll(k1y, 2, 0)) + (k1z + roll(k1z, 2, 1))
            done.append((k1y, k1z, OMEGA / (1.0 + total)))
        for i, value in zip(xs, done):
            a["k1y"][i], a["k1z"][i], a["wd1"][i] = value
    res = a["r0"]
    for xs in groups(middle_f, 8):
        done = [pool(res[2 * i] + res[2 * i + 1]) * 0.125 for i in xs]
        for i, value in zip(xs, done):
            a["f1"][i] = value


def selection_matrices(picks0_ref, picks1_ref, middle_ref, spread_ref):
    src = iota((RING, LANES), 0)
    dst = iota((RING, LANES), 1)
    cell = jnp.where(src < 192, src, src - RING)
    coarse = (cell + 4 * COARSE_LOW) // 4
    there = ((cell & 3) == 0) & (coarse >= 0) & (coarse < COARSE)
    head = there & (coarse < HEAD)
    tail = there & (coarse >= HEAD)
    sides = [there & (coarse == dst), there & (coarse + COARSE == dst)]
    picks0 = sides + [head & (coarse + 2 * COARSE == dst)]
    picks1 = sides + [tail & (coarse + 2 * COARSE - HEAD == dst)]
    picks0_ref[...] = jnp.concatenate([pick.astype(F32) for pick in picks0], axis=0).astype(BF16)
    picks1_ref[...] = jnp.concatenate([pick.astype(F32) for pick in picks1], axis=0).astype(BF16)
    pick_middle = (cell == 2 * middle_cell(dst)) & (dst < MIDDLE)
    middle_ref[...] = pick_middle.astype(F32).astype(BF16)
    src = iota((LANES, RING), 0)
    dst = iota((LANES, RING), 1)
    cell = jnp.where(dst < 192, dst, dst - RING)
    middle = (src < MIDDLE) & ((cell + 64) // 2 - 32 == middle_cell(src))
    coarse = (cell >= -4 * COARSE_LOW) & (src >= MIDDLE) & (src < MIDDLE + COARSE)
    coarse = coarse & ((cell + 4 * COARSE_LOW) // 4 == src - MIDDLE)
    spread_ref[...] = (middle | coarse).astype(F32).astype(BF16)


def near_kernel(mob_in, conc_in, side_in, xl_ref, xh_ref, *refs):
    a = {name: Inner(name, ref) for name, ref in zip(INNER, refs)}
    refs[len(INNER)][...] = mob_in[...]
    selection_matrices(*refs[len(INNER) + 1 :])
    own = (mob_in, conc_in, side_in)

    def parts_of(x):
        ref = xl_ref if x < 16 else xh_ref
        parts = [ref[place, x % 8].astype(F32) for place in range(5)]
        for place in range(3):
            part = parts[place]
            part = [part[:8], own[place][x - 8], part[24:]]
            parts[place] = jnp.concatenate(part, axis=0)
        return parts

    assemble(range(8, 24), parts_of, a["mob"], a["v0"], a["side"])
    descend(
        a, [(9, 22)], [[(9, 22)], [(10, 21)], [(11, 20)]], range(4, 11), range(5, 11), range(6, 10)
    )


def down_kernel(xm_ref, xp_ref, picks0_ref, picks1_ref, pick_middle_ref, *refs):
    count = len(INNER)
    inner, refs = refs[:count], refs[count:]
    own_ref, chunk_ref, *outer = refs[: 2 + count]
    e0, e1, r1, rows = refs[2 + count :]
    a = {
        name: Joined(Inner(name, near), far) for name, near, far in zip(INNER, inner, outer)
    }

    def parts_of(x):
        ref = xm_ref if x < 8 else xp_ref
        return [ref[place, x % 8].astype(F32) for place in range(5)]

    outside = list(range(8)) + list(range(24, 32))
    assemble(outside, parts_of, a["mob"], a["v0"], a["side"])
    descend(
        a,
        [(2, 8), (23, 29)],
        [[(2, 8), (23, 29)], [(3, 9), (22, 28)], [(4, 10), (21, 27)]],
        [1, 2, 3, 11, 12, 13],
        [2, 3, 4, 11, 12, 13],
        [2, 3, 4, 5, 10, 11, 12, 13],
    )
    f1_ref, k1x_ref, k1y_ref, k1z_ref, wd1_ref = (
        a[k] for k in ("f1", "k1x", "k1y", "k1z", "wd1")
    )
    for i in range(2, 14):
        e0[i] = wd1_ref[i] * f1_ref[i]

    def smooth(target, weight):
        def use(x, value, left):
            target[x] = value + weight[x] * left

        return use

    sweep_planes(3, 12, e0, f1_ref, k1x_ref, k1y_ref, k1z_ref, 2, smooth(e1, wd1_ref))

    def keep_middle(x, value, left):
        r1[x] = left

    sweep_planes(4, 11, e1, f1_ref, k1x_ref, k1y_ref, k1z_ref, 2, keep_middle)

    firsts = []
    seconds = []
    for j in range(4):
        i = 4 + 2 * j
        f2 = pair_sum(pair_sum(r1[i] + r1[i + 1], 2, 0), 2, 1) * 0.125
        k2x = pair_sum(pair_sum(k1x_ref[i + 1], 2, 0), 2, 1) * (1.0 / 16.0)
        k2y = pair_sum(k1y_ref[i] + k1y_ref[i + 1], 2, 1)
        k2y = upper_of(k2y, 2, 0) * (1.0 / 16.0)
        k2z = pair_sum(k1z_ref[i] + k1z_ref[i + 1], 2, 0)
        k2z = upper_of(k2z, 2, 1) * (1.0 / 16.0)
        f2, k2x, k2y, k2z = (cells[8:24] for cells in (f2, k2x, k2y, k2z))
        k2z = k2z.astype(BF16)
        high = f2.astype(BF16)
        low = (f2 - high.astype(F32)).astype(BF16)
        firsts.append(jnp.concatenate([high, low, k2z], axis=1))
        seconds.append(jnp.concatenate([k2x.astype(BF16), k2y.astype(BF16), k2z], axis=1))
    firsts = jnp.concatenate(firsts, axis=0)
    seconds = jnp.concatenate(seconds, axis=0)
    rows[pl.ds(0, 64), :] = jnp.dot(firsts, picks0_ref[...], preferred_element_type=F32)
    rows[pl.ds(64, 64), :] = jnp.dot(seconds, picks1_ref[...], preferred_element_type=F32)
    coarse = rows[pl.ds(0, 32, stride=4), :]
    rows[...] = select_dot(
        jnp.concatenate([e1[i] for i in range(3, 13)], axis=0), pick_middle_ref[...]
    )
    own_ref[...] = rows[pl.ds(0, 160, stride=2), :]

    blocks = [own_ref[pl.ds(16 * (1 + x) + 4, 8), :] for x in (1, 2, 5, 6)]
    for y in (1, 2):
        lines = [(x, k) for k in (y, y + 4) for x in (0, 3, 4, 7)]
        lines = [own_ref[pl.ds(16 * (1 + x) + 4 + k, 1), :] for x, k in lines]
        blocks.append(jnp.concatenate(lines, axis=0))
    narrow = iota((8, LANES), 1)
    middle = []
    for k in (0, 2, 4):
        middle.append(jnp.where(narrow < 64, blocks[k], roll(blocks[k + 1], 64, 1)))
    ends = jnp.zeros((8, LANES), F32)
    for k in range(6):
        ends = jnp.where(narrow // 4 == k, roll(blocks[k], 4 * k - 64, 1), ends)
    chunk = jnp.concatenate([coarse] + middle + [ends], axis=0).astype(BF16)
    for k in range(32):
        chunk_ref[k] = chunk


def up_kernel(
    place_ref, all_ref, own_ref, spread_ref, *refs
):
    count = len(KEPT)
    joined = [
        Joined(Inner(name, near), far)
        for name, near, far in zip(KEPT, refs[:count], refs[count : 2 * count])
    ]
    side_ref, kx_ref, ky_ref, kz_ref, wd_ref, v_ref = joined[:6]
    k1x_ref, k1y_ref, k1z_ref, wd1_ref, f1_ref = joined[6:]
    out_ref, pair0, pair1, c2x, c2y, c2z, wd2, f2, ea, eb = refs[2 * count : 2 * count + 10]
    mid, tall, lean, e1a, e1b, va, vb = refs[2 * count + 10 :]
    gx = place_ref[0]
    gy = place_ref[1]

    def source(dx, dy):
        return ((gx + dx + 8) & 7) * 4 + ((gy + dy + 4) & 3)

    for p in (0, 1, 2, 3, 4, 6, 7):
        for q in range(4):
            s = source(p - 1, q - 1)
            first = all_ref[s, pl.ds(0, 16), :].astype(F32)
            second = all_ref[s, pl.ds(16, 16), :].astype(F32)
            for i in range(4):
                pair0[4 * p + i, pl.ds(4 * q, 4), :] = first[4 * i : 4 * i + 4]
                pair1[4 * p + i, pl.ds(4 * q, 4), :] = second[4 * i : 4 * i + 4]
    for i in range(3, 13):
        mid[i] = own_ref[pl.ds(16 * (i - 3), 16), :]
    narrow = iota((8, LANES), 1)
    for p in (-1, 0, 1):
        for q in (-1, 0, 1):
            if p == 0 and q == 0:
                continue
            cells = all_ref[source(p, q), pl.ds(32, 32), :].astype(F32)
            ends = cells[24:]

            def block(k):
                main = cells[8 * (k // 2) : 8 * (k // 2) + 8]
                if k % 2:
                    main = roll(main, 64, 1)
                end = jnp.where(narrow < 68, roll(ends, 64 - 4 * k, 1), 0.0)
                return jnp.where(narrow < 64, main, end)

            for k, i in {-1: ((2, 1), (3, 2)), 0: (), 1: ((0, 13), (1, 14))}[p]:
                part = block(k)
                if q == -1:
                    mid[i, pl.ds(0, 4), :] = part[4:]
                elif q == 0:
                    mid[i, pl.ds(4, 8), :] = part
                else:
                    mid[i, pl.ds(12, 4), :] = part[:4]
            if q == 0:
                continue
            for depth in (0, 1):
                row = (1 if q == -1 else 13) + depth
                half = 4 if q == -1 else 0
                thin = block(4 + depth)
                for k, x in enumerate((0, 3, 4, 7)):
                    i = 8 * p + x + 4
                    if 3 <= i <= 12:
                        mid[i, pl.ds(row, 1), :] = thin[half + k : half + k + 1]
            if p == 0:
                for k, x in enumerate((1, 2, 5, 6)):
                    line = 5 if q == -1 else 1
                    part = block(k)
                    for depth in (0, 1):
                        row = (1 if q == -1 else 13) + depth
                        mid[x + 4, pl.ds(row, 1), :] = part[line + depth : line + depth + 1]

    used = iota((16, LANES), 1) < COARSE
    head = iota((16, LANES), 1) < HEAD
    for x in range(-6, 17):
        k = x % 32
        first = pair0[k]
        second = pair1[k]
        f2[k] = jnp.where(used, first + roll(first, -COARSE, 1), 0.0)
        c2x[k] = jnp.where(used, second, 0.0)
        c2y[k] = jnp.where(used, roll(second, -COARSE, 1), 0.0)
        last = jnp.where(
            head, roll(first, -2 * COARSE, 1), roll(second, HEAD - 2 * COARSE, 1)
        )
        c2z[k] = jnp.where(used, last, 0.0)
    for xs in groups(range(-5, 17), 11):
        done = []
        for x in xs:
            k = x % 32
            ky = c2y[k]
            kz = c2z[k]
            total = c2x[k] + c2x[(x - 1) % 32]
            total = total + (ky + roll(ky, 1, 0)) + (kz + roll(kz, 1, 1))
            weight = OMEGA / (1.0 + total)
            done.append((weight, weight * f2[k]))
        for x, value in zip(xs, done):
            wd2[x % 32], ea[x % 32] = value

    def smooth(target, weight):
        def use(x, value, left):
            target[x] = value + weight[x] * left

        return use

    old, new = ea, eb
    for reach in range(6, -1, -1):
        sweep_planes(
            2 - reach, 9 + reach, old, f2, c2x, c2y, c2z, 1, smooth(new, wd2), 10, 32
        )
        old, new = new, old

    lane = iota((8, LANES), 1)
    for j in range(8):
        line = roll(old[2 + j, pl.ds(2, 8), :], MIDDLE, 1)
        line = jnp.where((lane >= MIDDLE) & (lane < MIDDLE + COARSE), line, 0.0)
        for k in range(4):
            lean[j, pl.ds(k, 8, stride=4), :] = line
    for i in range(1, 15):
        line = mid[i]
        for k in range(2):
            tall[i, pl.ds(k, 16, stride=2), :] = line
    narrow = iota((32, LANES), 1) < MIDDLE
    packed = [jnp.where(narrow, tall[i], lean[i // 2]) for i in range(1, 15)]
    widened = select_dot(jnp.concatenate(packed, axis=0), spread_ref[...])
    for i in range(1, 15):
        e1a[i] = widened[32 * (i - 1) : 32 * i]

    sweep_planes(2, 13, e1a, f1_ref, k1x_ref, k1y_ref, k1z_ref, 2, smooth(e1b, wd1_ref))
    sweep_planes(3, 12, e1b, f1_ref, k1x_ref, k1y_ref, k1z_ref, 2, smooth(e1a, wd1_ref))
    for x in range(6, 26):
        va[x] = v_ref[x] + e1a[x // 2]
    sweep_planes(7, 24, va, side_ref, kx_ref, ky_ref, kz_ref, 1, smooth(vb, wd_ref))

    def finish(x, value, left):
        new = value + wd_ref[x] * left
        out_ref[x - 8] = new[8:24, :LANES]

    sweep_planes(8, 23, vb, side_ref, kx_ref, ky_ref, kz_ref, 1, finish)


def shift(x, axis, direction):
    count = lax.axis_size(axis)
    return lax.ppermute(x, axis, [(i, (i + direction) % count) for i in range(count)])


def body(conc, right_side, order_field, grain_ids):
    face = ((9, 16, LANES), BF16)
    zface = ((17, 16, LANES), BF16)
    brick = ((16, 16, LANES), F32)
    conc, side, order, ids, xm, xp, ym = call(
        faces_kernel,
        [brick, brick, ((8, 16, 16, LANES), BF16), ((1, 1, 8, 8), jnp.int32)] + [face] * 3,
        (conc, right_side, order_field, grain_ids),
        specs=[HBM] * 4,
        semaphores=4,
    )
    above = shift(ym, "gy", -1)
    before = shift(xp, "gx", 1)
    after = shift(xm, "gx", -1)
    inner, yp, zm, zp = call(
        inner_kernel,
        [brick, ((8, 16, LANES), BF16), zface, zface],
        (conc, order, ids),
        scratch=[((64, 8, LANES), F32)],
    )
    line = ((16, LANES), F32)
    payload = ((34, 16, LANES), BF16)
    partial, beyond, send_zm, send_zp = call(
        outer_kernel,
        [brick, line, payload, payload],
        (inner, conc, side, order, ids, before, after, above, yp, zm, zp),
    )
    left = shift(send_zp, "gz", 1)
    right = shift(send_zm, "gz", -1)
    keep, beside, low, high = call(
        split_kernel,
        [brick, line, ((80, 8, LANES), BF16), ((86, 8, LANES), BF16)],
        (partial, conc, side, beyond, left, right, zm, zp),
    )
    below = shift(high, "gy", 1)
    above = shift(low, "gy", -1)
    slab = ((5, 8, 32, LANES), BF16)
    keep, xl, xh = call(
        rows_kernel,
        [brick, slab, slab],
        (below, low, high, above, keep, beyond, beside),
    )
    before = shift(xh, "gx", 1)
    after = shift(xl, "gx", -1)
    fine = ((32, 32, RING), F32)
    middle = ((16, 32, RING), F32)
    *inner, mobility, picks0, picks1, pick_middle, spread = call(
        near_kernel,
        [((INNER[name][1], 32, RING), F32) for name in INNER]
        + [brick]
        + [((3 * RING, LANES), BF16)] * 2
        + [((RING, LANES), BF16), ((LANES, RING), BF16)],
        (keep, conc, side, xl, xh),
    )
    outer = [middle if name in MIDDLE_ARRAYS else fine for name in INNER]
    own, chunk, *outer = call(
        down_kernel,
        [((160, LANES), F32), ((32, CHUNK, LANES), BF16)] + outer[: len(KEPT)],
        (before, after, picks0, picks1, pick_middle) + tuple(inner),
        scratch=outer[len(KEPT) :] + [middle] * 3 + [((320, LANES), F32)],
    )
    kept = tuple(inner[: len(KEPT)]) + tuple(outer)
    place = jnp.stack([lax.axis_index("gx"), lax.axis_index("gy")]).astype(jnp.int32)
    chunk, place = lax.optimization_barrier((chunk, place))
    chunks = lax.all_to_all(chunk, ("gx", "gy"), 0, 0, tiled=True)
    plane = ((32, 16, LANES), F32)
    (out,) = call(
        up_kernel,
        [brick],
        (place, chunks, own, spread) + kept,
        scratch=[plane] * 9
        + [brick, ((16, 32, LANES), F32), ((8, 32, LANES), F32)]
        + [middle] * 2
        + [fine] * 2,
        specs=[SMEM] + [VMEM] * (3 + len(kept)),
    )
    return out, mobility


def solution(mesh):
    return jax.shard_map(
        body,
        mesh=mesh,
        in_specs=(
            P("gx", "gy", "gz"),
            P("gx", "gy", "gz"),
            P(None, "gx", "gy", "gz"),
            P("gx", "gy", "gz", None),
        ),
        out_specs=(P("gx", "gy", "gz"), P("gx", "gy", "gz")),
        check_vma=False,
    )
```

```python
import functools

import jax
import jax.numpy as jnp
from jax import lax
from jax.experimental import pallas as pl
from jax.experimental.pallas import tpu as pltpu
from jax.sharding import PartitionSpec as P

SLOTS = 8
BRICK = 16
OMEGA = 0.8
TAU = 256.0
LANES = 128
RING = 256
F32 = jnp.float32
BF16 = jnp.bfloat16
HIGH = lax.Precision.HIGHEST
VMEM = pl.BlockSpec(memory_space=pltpu.VMEM)
HBM = pl.BlockSpec(memory_space=pltpu.MemorySpace.HBM)
SMEM = pl.BlockSpec(memory_space=pltpu.SMEM)
COARSE = 51
COARSE_LOW = 10
MIDDLE = 70
HEAD = 26
CHUNK = 64


def call(kernel, outs, args, scratch=(), specs=None, places=None, limit=16, semaphores=0):
    specs = specs or [VMEM] * len(args)
    places = places or [VMEM] * len(outs)
    args = [
        pltpu.with_memory_space_constraint(arg, pltpu.MemorySpace.HBM) if spec is HBM else arg
        for arg, spec in zip(args, specs)
    ]
    scratches = [pltpu.VMEM(shape, dtype) for shape, dtype in scratch]
    if semaphores:
        scratches.append(pltpu.SemaphoreType.DMA((semaphores,)))
    return pl.pallas_call(
        kernel,
        out_shape=[
            pltpu.MemorySpace.HBM(*out) if place is HBM else jax.ShapeDtypeStruct(*out)
            for out, place in zip(outs, places)
        ],
        in_specs=specs,
        out_specs=places,
        scratch_shapes=scratches,
        compiler_params=pltpu.CompilerParams(vmem_limit_bytes=limit << 20),
    )(*args)


def roll(x, shift, axis):
    return pltpu.roll(x, shift % x.shape[axis], axis)


def iota(shape, axis):
    return lax.broadcasted_iota(jnp.int32, shape, axis)


def select_dot(a, picks):
    picks = picks.astype(BF16)
    total = None
    for _ in range(3):
        part = a.astype(BF16)
        a = a - part.astype(F32)
        term = jnp.dot(part, picks, preferred_element_type=F32)
        total = term if total is None else total + term
    return total


def lane_ids(ids_ref):
    ids = ids_ref[0, 0].astype(F32)
    spread = (iota((8, LANES), 1) // BRICK == iota((8, LANES), 0)).astype(F32)
    grains = lax.dot_general(
        ids, spread, (((0,), (0,)), ((), ())), precision=HIGH, preferred_element_type=F32
    )
    return jnp.floor(grains + 0.5)


def split_ids(grains):
    high = jnp.floor(grains * (1.0 / 64.0))
    return jnp.concatenate([high, grains - 64.0 * high], axis=0).astype(BF16)


def join_ids(rows):
    rows = rows.astype(F32)
    return rows[:8] * 64.0 + rows[8:]


def faces_kernel(
    place_ref, conc_in, side_in, order_in, ids_in,
    conc_ref, side_ref, order_ref, ids_ref, xa_ref, xb_ref, ym_ref, sems,
):
    odd = place_ref[0] & 1
    pairs = (
        (ids_in, ids_ref), (order_in, order_ref), (conc_in, conc_ref), (side_in, side_ref),
    )
    copies = [pltpu.make_async_copy(a, b, sems.at[k]) for k, (a, b) in enumerate(pairs)]
    for copy in copies:
        copy.start()
    copies[0].wait()
    copies[1].wait()
    grains = lane_ids(ids_ref)
    packed = split_ids(grains)
    for ref in (xa_ref, xb_ref, ym_ref):
        ref[SLOTS] = packed
    for slot in range(SLOTS):
        xa_ref[slot] = order_ref[slot, 15 * odd]
        xb_ref[slot] = order_ref[slot, 15 - 15 * odd]
        ym_ref[slot] = order_ref[slot].astype(F32)[:, 0, :].astype(BF16)
    copies[2].wait()
    copies[3].wait()


def square(x):
    return x * x


def inner_kernel(
    conc_ref, order_ref, ids_ref, work, yp_ref, zm_ref, zp_ref, weights,
):
    grains = lane_ids(ids_ref)
    zm_ref[16] = split_ids(jnp.broadcast_to(grains[:, 0:1], (8, LANES)))
    zp_ref[16] = split_ids(jnp.broadcast_to(grains[:, LANES - 1 :], (8, LANES)))
    slots = iota((16, LANES), 1)
    low = [jnp.zeros((16, LANES), F32)] * 16
    high = [jnp.zeros((16, LANES), F32)] * 16
    for slot in range(SLOTS):
        cells = order_ref[slot].astype(F32)
        yp_ref[slot] = cells[:, 15, :].astype(BF16)
        for x in range(16):
            low[x] = jnp.where(slots == slot, cells[x, :, 0:1], low[x])
            high[x] = jnp.where(slots == slot, cells[x, :, LANES - 1 :], high[x])
    for x in range(16):
        zm_ref[x] = low[x].astype(BF16)
        zp_ref[x] = high[x].astype(BF16)

    own = lane_ids(ids_ref)
    lane = iota((16, LANES), 1)
    row = iota((16, LANES), 0)
    last = lane % BRICK == BRICK - 1
    edge = (last | (lane % BRICK == 0)) & (lane != 0) & (lane != LANES - 1)

    lane8 = iota((8, LANES), 1)
    beside = jnp.where(
        lane8 % BRICK == BRICK - 1, roll(own, -BRICK, 1), roll(own, BRICK, 1)
    )
    for other in range(SLOTS):
        match = (own == beside[other : other + 1]).astype(F32)
        for slot in range(SLOTS):
            weights[slot * SLOTS + other] = jnp.broadcast_to(match[slot : slot + 1], (8, LANES))

    def doubled(block):
        return jnp.concatenate([block, block], axis=0)

    def plane(x, carry_in):
        conc = conc_ref[x]
        base = 1.0 + 8.0 * square(conc * (1.0 - conc))
        along_y = jnp.zeros((16, LANES), F32)
        along_z = jnp.zeros((16, LANES), F32)
        along_x = jnp.zeros((16, LANES), F32)
        centers = []
        facing = []
        above = min(x + 1, 15)
        for slot in range(SLOTS):
            here = order_ref[slot, x].astype(F32)
            there = order_ref[slot, above].astype(F32)
            centers.append(here)
            along_x = along_x + square(there - here)
            along_y = along_y + square(roll(here, -1, 0) - here)
            right = roll(here, -1, 1)
            along_z = along_z + square(right - here)
            facing.append(jnp.where(last, right, roll(here, 1, 1)))
        along_y = jnp.where(row == 15, 0.0, along_y)
        along_z = jnp.where(last, 0.0, along_z)
        remapped = jnp.zeros((16, LANES), F32)
        for slot in range(SLOTS):
            value = None
            for other in range(SLOTS):
                term = doubled(weights[slot * SLOTS + other]) * facing[other]
                value = term if value is None else value + term
            remapped = remapped + square(value - centers[slot])
        total = base + along_y + roll(along_y, 1, 0) + along_z + roll(along_z, 1, 1)
        total = total + jnp.where(edge, remapped, 0.0) + along_x + carry_in
        work[x] = total
        return along_x

    carry = jnp.zeros((16, LANES), F32)
    for x in range(16):
        carry = plane(x, carry)

def outer_kernel(
    place_ref, work, conc_ref, side_ref, order_ref, ids_ref, xa_ref, xb_ref, yp_ref,
    own_yp_ref, own_zm_ref, own_zp_ref, mob_ref, beyond_ref, zm_out, zp_out,
):
    own = lane_ids(ids_ref)
    lane = iota((16, LANES), 1)
    row = iota((16, LANES), 0)

    def across(center, ids, facing, facing_ids):
        facing = [facing(other).astype(F32) for other in range(SLOTS)]
        total = None
        for slot in range(SLOTS):
            value = None
            for other in range(SLOTS):
                match = ids[slot : slot + 1] == facing_ids[other : other + 1]
                term = match.astype(F32) * facing[other]
                value = term if value is None else value + term
            part = square(value - center(slot).astype(F32))
            total = part if total is None else total + part
        return total

    odd = place_ref[0] & 1
    side_a = across(
        lambda k: order_ref[k, 15 * odd], own, lambda k: xa_ref[k], join_ids(xa_ref[SLOTS])
    )
    side_b = across(
        lambda k: order_ref[k, 15 - 15 * odd], own, lambda k: xb_ref[k], join_ids(xb_ref[SLOTS])
    )
    first = work[0] + jnp.where(odd == 0, side_a, side_b)
    final = work[15] + jnp.where(odd == 0, side_b, side_a)
    above_ids = join_ids(yp_ref[SLOTS])
    top = across(lambda k: own_yp_ref[k], own, lambda k: yp_ref[k], above_ids)
    beyond = across(lambda k: yp_ref[k], above_ids, lambda k: own_yp_ref[k], own)
    beyond_ref[...] = beyond
    zm_out[33] = beyond.astype(BF16)
    zp_out[33] = beyond.astype(BF16)
    for x in range(16):
        value = first if x == 0 else final if x == 15 else work[x]
        value = value + jnp.where(row == 15, top[x : x + 1], 0.0)
        mob_ref[x] = value
        conc, side = conc_ref[x], side_ref[x]
        down = jnp.where(
            lane < 43, value, jnp.where(lane < 86, roll(conc, 43, 1), roll(side, 86, 1))
        )
        zm_out[x] = down.astype(BF16)
        up = jnp.where(
            lane >= 85, value, jnp.where(lane >= 42, roll(conc, -43, 1), roll(side, -86, 1))
        )
        zp_out[x] = up.astype(BF16)
    zm_out[16:33] = own_zm_ref[...]
    zp_out[16:33] = own_zp_ref[...]


def facing_squares(near_ref, far_ref, near_lane, far_lane):
    near = near_ref[:16].reshape(256, LANES)
    far = far_ref[:16].reshape(256, LANES)
    near_ids = join_ids(near_ref[16])
    far_ids = join_ids(far_ref[16])
    diagonal = iota((8, LANES), 0) == iota((8, LANES), 1)
    slots = iota((8, LANES), 1) < SLOTS

    def squares(cells, ids, others, other_ids, target):
        along = jnp.sum(jnp.where(diagonal, ids, 0.0), axis=0, keepdims=True)
        match = ((other_ids == along) & slots).astype(F32)
        match = jnp.concatenate([match, jnp.zeros((LANES - 8, LANES), F32)], axis=0)
        seen = jnp.dot(others, match.astype(BF16), preferred_element_type=F32)
        place = (iota((LANES, LANES), 1) == target).astype(F32)
        total = select_dot(square(seen - cells.astype(F32)), place)
        return total.reshape(16, 16, LANES)

    return (
        squares(near, near_ids, far, far_ids, near_lane),
        squares(far, far_ids, near, near_ids, far_lane),
    )


def split_kernel(
    mob_ref, conc_ref, side_ref, beyond_ref, left_ref, right_ref, zm_ref, zp_ref,
    keep_ref, beside_ref, low_ref, high_ref,
):
    own_low, far_low = facing_squares(zm_ref, left_ref.at[16:33], 0, LANES - 1)
    own_high, far_high = facing_squares(zp_ref, right_ref.at[16:33], LANES - 1, 0)
    mob = mob_ref[...] + own_low + own_high
    keep_ref[...] = mob
    down = (left_ref[:16].astype(F32) + far_low).astype(BF16)
    up = (right_ref[:16].astype(F32) + far_high).astype(BF16)
    for place, value in enumerate((mob, conc_ref[...], side_ref[...], down, up)):
        planes = pl.ds(16 * place, 16)
        low_ref[planes] = value[:, :8].astype(BF16)
        high_ref[planes] = value[:, 8:].astype(BF16)
    lane = iota((16, LANES), 1)
    down, up = left_ref[33].astype(F32), right_ref[33].astype(F32)
    beside = jnp.where(lane < 43, up, jnp.where(lane >= 85, down, 0.0))
    beside_ref[...] = beside
    beyond = beyond_ref[...]
    high = beyond.astype(BF16)
    rest = (beyond - high.astype(F32)).astype(BF16)
    for k, value in enumerate((high, rest, beside.astype(BF16))):
        high_ref[80 + 2 * k] = value[:8]
        high_ref[81 + 2 * k] = value[8:]


def rows_kernel(
    place_ref, below_ref, low_ref, high_ref, above_ref, mob_ref, beyond_ref, beside_ref,
    keep_ref, xl_ref, xh_ref, xa_ref, xb_ref,
):
    lane = iota((8, LANES), 1)
    first = iota((8, LANES), 0) == 0
    got = [
        jnp.concatenate([below_ref[80 + 2 * k], below_ref[81 + 2 * k]], axis=0).astype(F32)
        for k in range(3)
    ]
    missing = ((got[0] + got[1], got[2]), (beyond_ref[...], beside_ref[...]))
    for x in range(16):
        ref = xl_ref if x < 8 else xh_ref
        lines = []
        for main, beside in missing:
            main = jnp.where(first, main[x : x + 1], 0.0)
            beside = jnp.where(first, beside[x : x + 1], 0.0)
            down = jnp.where(lane >= 85, beside, 0.0)
            lines.append((main, None, None, down, jnp.where(lane < 43, beside, 0.0)))
        own = mob_ref[x, :8] + lines[0][0]
        keep_ref[x, :8] = own
        keep_ref[x, 8:] = mob_ref[x, 8:]
        for place in range(5):
            plane = 16 * place + x
            near, far = low_ref[plane], above_ref[plane]
            if place == 0:
                near = own.astype(BF16)
            elif place >= 3:
                near = (near.astype(F32) + lines[0][place]).astype(BF16)
            if place in (0, 3, 4):
                far = (far.astype(F32) + lines[1][place]).astype(BF16)
            for k, value in enumerate((below_ref[plane], near, high_ref[plane], far)):
                ref[place, x % 8, pl.ds(8 * k, 8), :] = value
    odd = place_ref[0] & 1

    @pl.when(odd == 0)
    def _():
        xa_ref[...] = xl_ref[...]
        xb_ref[...] = xh_ref[...]

    @pl.when(odd == 1)
    def _():
        xa_ref[...] = xh_ref[...]
        xb_ref[...] = xl_ref[...]


def partner(x, step, axis):
    upper = (iota(x.shape, axis) & step) != 0
    return jnp.where(upper, roll(x, step, axis), roll(x, -step, axis))


def pair_sum(x, step, axis):
    return x + partner(x, step, axis)


def upper_of(x, step, axis):
    upper = (iota(x.shape, axis) & step) != 0
    return jnp.where(upper, x, roll(x, -step, axis))


def middle_cell(lane):
    cell = lane
    for place, end in enumerate((-2, -1, 64, 65, -3, 66)):
        cell = jnp.where(lane == 64 + place, end, cell)
    return cell


def groups(items, size):
    items = list(items)
    return [items[k : k + size] for k in range(0, len(items), size)]


def sweep_planes(first, last, values, source, kx, ky, kz, step, use, size=8, planes=None):
    at = (lambda x: x) if planes is None else (lambda x: x % planes)
    before = kx[at(first - 1)] * (values[at(first)] - values[at(first - 1)])
    for xs in groups(range(first, last + 1), size):
        cells = [values[at(x)] for x in xs + [xs[-1] + 1]]
        flux_z = [kz[at(x)] * (roll(v, -step, 1) - v) for x, v in zip(xs, cells)]
        back_z = [roll(flux, step, 1) for flux in flux_z]
        left = []
        for k, x in enumerate(xs):
            value = cells[k]
            flux_x = kx[at(x)] * (cells[k + 1] - value)
            flux_y = ky[at(x)] * (roll(value, -step, 0) - value)
            total = (source[at(x)] - value) + (flux_x - before)
            total = total + (flux_y - roll(flux_y, step, 0))
            left.append(total + (flux_z[k] - back_z[k]))
            before = flux_x
        for k, x in enumerate(xs):
            use(at(x), cells[k], left[k])


INNER = {
    "side": (8, 16), "kx": (8, 15), "ky": (9, 14), "kz": (9, 14), "wd": (9, 14), "v": (10, 12),
    "k1x": (4, 7), "k1y": (5, 6), "k1z": (5, 6), "wd1": (5, 6), "f1": (6, 4),
    "mob": (8, 16), "v0": (8, 16), "s1": (9, 14), "r0": (11, 10),
}
KEPT = ("side", "kx", "ky", "kz", "wd", "v", "k1x", "k1y", "k1z", "wd1", "f1")
MIDDLE_ARRAYS = ("k1x", "k1y", "k1z", "wd1", "f1")


class Inner:
    def __init__(self, name, ref):
        self.low, self.count = INNER[name]
        self.ref = ref

    def __contains__(self, x):
        return self.low <= x < self.low + self.count

    def __getitem__(self, x):
        return self.ref[x - self.low]

    def __setitem__(self, x, value):
        self.ref[x - self.low] = value


class Joined:
    def __init__(self, inner, outer):
        self.inner = inner
        self.outer = outer

    def __getitem__(self, x):
        return self.inner[x] if x in self.inner else self.outer[x]

    def __setitem__(self, x, value):
        self.outer[x] = value


def assemble(xs, parts_of, mob, v0, side):
    lane = iota((32, LANES), 1)
    for some in groups(xs, 8):
        planes = []
        for x in some:
            parts = parts_of(x)
            down, up = parts[3], parts[4]
            beyond = jnp.where(lane < 43, up, jnp.where(lane >= 85, down, 1.0))
            iterate = jnp.where(
                lane < 43, roll(up, -43, 1), jnp.where(lane >= 85, roll(down, 43, 1), 0.0)
            )
            right = jnp.where(
                lane < 42, roll(up, -86, 1), jnp.where(lane >= 86, roll(down, 86, 1), 0.0)
            )
            planes.append(zip(parts, (beyond, iterate, right)))
        for x, plane in zip(some, planes):
            for target, pair in zip((mob, v0, side), plane):
                target[x] = jnp.concatenate(pair, axis=1)


def descend(a, coeffs, sweeps, middle_x, middle, middle_f):
    half = TAU / 2
    mob, kx_ref, ky_ref, kz_ref, wd_ref = (a[k] for k in ("mob", "kx", "ky", "kz", "wd"))
    for first, last in coeffs:
        before = half * (mob[first - 1] + mob[first])
        kx_ref[first - 1] = before
        for xs in groups(range(first, last + 1), 7):
            here = [mob[x] for x in xs + [xs[-1] + 1]]
            kz = [half * (cells + roll(cells, -1, 1)) for cells in here[:-1]]
            back = [roll(k, 1, 1) for k in kz]
            done = []
            for k, x in enumerate(xs):
                kx = half * (here[k] + here[k + 1])
                ky = half * (here[k] + roll(here[k], -1, 0))
                total = (kx + before) + (ky + roll(ky, 1, 0)) + (kz[k] + back[k])
                done.append((kx, ky, OMEGA / (1.0 + total)))
                before = kx
            for k, x in enumerate(xs):
                kx_ref[x], ky_ref[x], wd_ref[x] = done[k]
                kz_ref[x] = kz[k]

    def smooth(target):
        def use(x, value, left):
            target[x] = value + wd_ref[x] * left

        return use

    def keep(x, value, left):
        a["r0"][x] = left

    steps = (("v0", smooth(a["s1"])), ("s1", smooth(a["v"])), ("v", keep))
    for (name, use), runs in zip(steps, sweeps):
        for first, last in runs:
            sweep_planes(first, last, a[name], a["side"], kx_ref, ky_ref, kz_ref, 1, use)

    def pool(x):
        return pair_sum(pair_sum(x, 1, 0), 1, 1)

    k1x_ref = a["k1x"]
    for xs in groups(middle_x, 7):
        done = [pool(kx_ref[2 * i + 1]) * (1.0 / 16.0) for i in xs]
        for i, value in zip(xs, done):
            k1x_ref[i] = value
    for xs in groups(middle, 6):
        done = []
        for i in xs:
            x = 2 * i
            along_y = pair_sum(ky_ref[x] + ky_ref[x + 1], 1, 1)
            k1y = upper_of(along_y, 1, 0) * (1.0 / 16.0)
            along_z = pair_sum(kz_ref[x] + kz_ref[x + 1], 1, 0)
            k1z = upper_of(along_z, 1, 1) * (1.0 / 16.0)
            total = k1x_ref[i] + k1x_ref[i - 1]
            total = total + (k1y + roll(k1y, 2, 0)) + (k1z + roll(k1z, 2, 1))
            done.append((k1y, k1z, OMEGA / (1.0 + total)))
        for i, value in zip(xs, done):
            a["k1y"][i], a["k1z"][i], a["wd1"][i] = value
    res = a["r0"]
    for xs in groups(middle_f, 8):
        done = [pool(res[2 * i] + res[2 * i + 1]) * 0.125 for i in xs]
        for i, value in zip(xs, done):
            a["f1"][i] = value


def selection_matrices(picks0_ref, picks1_ref, middle_ref, spread_ref):
    src = iota((RING, LANES), 0)
    dst = iota((RING, LANES), 1)
    cell = jnp.where(src < 192, src, src - RING)
    coarse = (cell + 4 * COARSE_LOW) // 4
    there = ((cell & 3) == 0) & (coarse >= 0) & (coarse < COARSE)
    head = there & (coarse < HEAD)
    tail = there & (coarse >= HEAD)
    sides = [there & (coarse == dst), there & (coarse + COARSE == dst)]
    picks0 = sides + [head & (coarse + 2 * COARSE == dst)]
    picks1 = sides + [tail & (coarse + 2 * COARSE - HEAD == dst)]
    picks0_ref[...] = jnp.concatenate([pick.astype(F32) for pick in picks0], axis=0).astype(BF16)
    picks1_ref[...] = jnp.concatenate([pick.astype(F32) for pick in picks1], axis=0).astype(BF16)
    pick_middle = (cell == 2 * middle_cell(dst)) & (dst < MIDDLE)
    middle_ref[...] = pick_middle.astype(F32).astype(BF16)
    src = iota((LANES, RING), 0)
    dst = iota((LANES, RING), 1)
    cell = jnp.where(dst < 192, dst, dst - RING)
    middle = (src < MIDDLE) & ((cell + 64) // 2 - 32 == middle_cell(src))
    coarse = (cell >= -4 * COARSE_LOW) & (src >= MIDDLE) & (src < MIDDLE + COARSE)
    coarse = coarse & ((cell + 4 * COARSE_LOW) // 4 == src - MIDDLE)
    spread_ref[...] = (middle | coarse).astype(F32).astype(BF16)


def near_kernel(mob_in, conc_in, side_in, xl_ref, xh_ref, *refs):
    a = {name: Inner(name, ref) for name, ref in zip(INNER, refs)}
    refs[len(INNER)][...] = mob_in[...]
    selection_matrices(*refs[len(INNER) + 1 :])
    own = (mob_in, conc_in, side_in)

    def parts_of(x):
        ref = xl_ref if x < 16 else xh_ref
        parts = [ref[place, x % 8].astype(F32) for place in range(5)]
        for place in range(3):
            part = parts[place]
            part = [part[:8], own[place][x - 8], part[24:]]
            parts[place] = jnp.concatenate(part, axis=0)
        return parts

    assemble(range(8, 24), parts_of, a["mob"], a["v0"], a["side"])
    descend(
        a, [(9, 22)], [[(9, 22)], [(10, 21)], [(11, 20)]], range(4, 11), range(5, 11), range(6, 10)
    )


def down_kernel(place_ref, xa_ref, xb_ref, picks0_ref, picks1_ref, pick_middle_ref, *refs):
    count = len(INNER)
    inner, refs = refs[:count], refs[count:]
    own_ref, chunk_ref, *outer = refs[: 2 + count]
    e0, e1, r1, rows = refs[2 + count :]
    a = {
        name: Joined(Inner(name, near), far) for name, near, far in zip(INNER, inner, outer)
    }

    outside = list(range(8)) + list(range(24, 32))

    def fill(xm_ref, xp_ref):
        def parts_of(x):
            ref = xm_ref if x < 8 else xp_ref
            return [ref[place, x % 8].astype(F32) for place in range(5)]

        assemble(outside, parts_of, a["mob"], a["v0"], a["side"])

    odd = place_ref[0] & 1
    pl.when(odd == 0)(lambda: fill(xa_ref, xb_ref))
    pl.when(odd == 1)(lambda: fill(xb_ref, xa_ref))
    descend(
        a,
        [(2, 8), (23, 29)],
        [[(2, 8), (23, 29)], [(3, 9), (22, 28)], [(4, 10), (21, 27)]],
        [1, 2, 3, 11, 12, 13],
        [2, 3, 4, 11, 12, 13],
        [2, 3, 4, 5, 10, 11, 12, 13],
    )
    f1_ref, k1x_ref, k1y_ref, k1z_ref, wd1_ref = (
        a[k] for k in ("f1", "k1x", "k1y", "k1z", "wd1")
    )
    for i in range(2, 14):
        e0[i] = wd1_ref[i] * f1_ref[i]

    def smooth(target, weight):
        def use(x, value, left):
            target[x] = value + weight[x] * left

        return use

    sweep_planes(3, 12, e0, f1_ref, k1x_ref, k1y_ref, k1z_ref, 2, smooth(e1, wd1_ref))

    def keep_middle(x, value, left):
        r1[x] = left

    sweep_planes(4, 11, e1, f1_ref, k1x_ref, k1y_ref, k1z_ref, 2, keep_middle)

    firsts = []
    seconds = []
    for j in range(4):
        i = 4 + 2 * j
        f2 = pair_sum(pair_sum(r1[i] + r1[i + 1], 2, 0), 2, 1) * 0.125
        k2x = pair_sum(pair_sum(k1x_ref[i + 1], 2, 0), 2, 1) * (1.0 / 16.0)
        k2y = pair_sum(k1y_ref[i] + k1y_ref[i + 1], 2, 1)
        k2y = upper_of(k2y, 2, 0) * (1.0 / 16.0)
        k2z = pair_sum(k1z_ref[i] + k1z_ref[i + 1], 2, 0)
        k2z = upper_of(k2z, 2, 1) * (1.0 / 16.0)
        f2, k2x, k2y, k2z = (cells[8:24] for cells in (f2, k2x, k2y, k2z))
        k2z = k2z.astype(BF16)
        high = f2.astype(BF16)
        low = (f2 - high.astype(F32)).astype(BF16)
        firsts.append(jnp.concatenate([high, low, k2z], axis=1))
        seconds.append(jnp.concatenate([k2x.astype(BF16), k2y.astype(BF16), k2z], axis=1))
    firsts = jnp.concatenate(firsts, axis=0)
    seconds = jnp.concatenate(seconds, axis=0)
    rows[pl.ds(0, 64), :] = jnp.dot(firsts, picks0_ref[...], preferred_element_type=F32)
    rows[pl.ds(64, 64), :] = jnp.dot(seconds, picks1_ref[...], preferred_element_type=F32)
    coarse = rows[pl.ds(0, 32, stride=4), :]
    rows[...] = select_dot(
        jnp.concatenate([e1[i] for i in range(3, 13)], axis=0), pick_middle_ref[...]
    )
    own_ref[...] = rows[pl.ds(0, 160, stride=2), :]

    blocks = [own_ref[pl.ds(16 * (1 + x) + 4, 8), :] for x in (1, 2, 5, 6)]
    for y in (1, 2):
        lines = [(x, k) for k in (y, y + 4) for x in (0, 3, 4, 7)]
        lines = [own_ref[pl.ds(16 * (1 + x) + 4 + k, 1), :] for x, k in lines]
        blocks.append(jnp.concatenate(lines, axis=0))
    narrow = iota((8, LANES), 1)
    middle = []
    for k in (0, 2, 4):
        middle.append(jnp.where(narrow < 64, blocks[k], roll(blocks[k + 1], 64, 1)))
    ends = jnp.zeros((8, LANES), F32)
    for k in range(6):
        ends = jnp.where(narrow // 4 == k, roll(blocks[k], 4 * k - 64, 1), ends)
    chunk = jnp.concatenate([coarse] + middle + [ends], axis=0).astype(BF16)
    for k in range(32):
        chunk_ref[k] = chunk


def up_kernel(
    place_ref, all_ref, own_ref, spread_ref, *refs
):
    count = len(KEPT)
    joined = [
        Joined(Inner(name, near), far)
        for name, near, far in zip(KEPT, refs[:count], refs[count : 2 * count])
    ]
    side_ref, kx_ref, ky_ref, kz_ref, wd_ref, v_ref = joined[:6]
    k1x_ref, k1y_ref, k1z_ref, wd1_ref, f1_ref = joined[6:]
    out_ref, pair0, pair1, c2x, c2y, c2z, wd2, f2, ea, eb = refs[2 * count : 2 * count + 10]
    mid, tall, lean, e1a, e1b, va, vb = refs[2 * count + 10 :]
    gx = place_ref[0]
    gy = place_ref[1]

    def source(dx, dy):
        return ((gx + dx + 8) & 7) * 4 + ((gy + dy + 4) & 3)

    for p in (0, 1, 2, 3, 4, 6, 7):
        for q in range(4):
            s = source(p - 1, q - 1)
            first = all_ref[s, pl.ds(0, 16), :].astype(F32)
            second = all_ref[s, pl.ds(16, 16), :].astype(F32)
            for i in range(4):
                pair0[4 * p + i, pl.ds(4 * q, 4), :] = first[4 * i : 4 * i + 4]
                pair1[4 * p + i, pl.ds(4 * q, 4), :] = second[4 * i : 4 * i + 4]
    for i in range(3, 13):
        mid[i] = own_ref[pl.ds(16 * (i - 3), 16), :]
    narrow = iota((8, LANES), 1)
    for p in (-1, 0, 1):
        for q in (-1, 0, 1):
            if p == 0 and q == 0:
                continue
            cells = all_ref[source(p, q), pl.ds(32, 32), :].astype(F32)
            ends = cells[24:]

            def block(k):
                main = cells[8 * (k // 2) : 8 * (k // 2) + 8]
                if k % 2:
                    main = roll(main, 64, 1)
                end = jnp.where(narrow < 68, roll(ends, 64 - 4 * k, 1), 0.0)
                return jnp.where(narrow < 64, main, end)

            for k, i in {-1: ((2, 1), (3, 2)), 0: (), 1: ((0, 13), (1, 14))}[p]:
                part = block(k)
                if q == -1:
                    mid[i, pl.ds(0, 4), :] = part[4:]
                elif q == 0:
                    mid[i, pl.ds(4, 8), :] = part
                else:
                    mid[i, pl.ds(12, 4), :] = part[:4]
            if q == 0:
                continue
            for depth in (0, 1):
                row = (1 if q == -1 else 13) + depth
                half = 4 if q == -1 else 0
                thin = block(4 + depth)
                for k, x in enumerate((0, 3, 4, 7)):
                    i = 8 * p + x + 4
                    if 3 <= i <= 12:
                        mid[i, pl.ds(row, 1), :] = thin[half + k : half + k + 1]
            if p == 0:
                for k, x in enumerate((1, 2, 5, 6)):
                    line = 5 if q == -1 else 1
                    part = block(k)
                    for depth in (0, 1):
                        row = (1 if q == -1 else 13) + depth
                        mid[x + 4, pl.ds(row, 1), :] = part[line + depth : line + depth + 1]

    used = iota((16, LANES), 1) < COARSE
    head = iota((16, LANES), 1) < HEAD
    for x in range(-6, 17):
        k = x % 32
        first = pair0[k]
        second = pair1[k]
        f2[k] = jnp.where(used, first + roll(first, -COARSE, 1), 0.0)
        c2x[k] = jnp.where(used, second, 0.0)
        c2y[k] = jnp.where(used, roll(second, -COARSE, 1), 0.0)
        last = jnp.where(
            head, roll(first, -2 * COARSE, 1), roll(second, HEAD - 2 * COARSE, 1)
        )
        c2z[k] = jnp.where(used, last, 0.0)
    for xs in groups(range(-5, 17), 11):
        done = []
        for x in xs:
            k = x % 32
            ky = c2y[k]
            kz = c2z[k]
            total = c2x[k] + c2x[(x - 1) % 32]
            total = total + (ky + roll(ky, 1, 0)) + (kz + roll(kz, 1, 1))
            weight = OMEGA / (1.0 + total)
            done.append((weight, weight * f2[k]))
        for x, value in zip(xs, done):
            wd2[x % 32], ea[x % 32] = value

    def smooth(target, weight):
        def use(x, value, left):
            target[x] = value + weight[x] * left

        return use

    old, new = ea, eb
    for reach in range(6, -1, -1):
        sweep_planes(
            2 - reach, 9 + reach, old, f2, c2x, c2y, c2z, 1, smooth(new, wd2), 10, 32
        )
        old, new = new, old

    lane = iota((8, LANES), 1)
    for j in range(8):
        line = roll(old[2 + j, pl.ds(2, 8), :], MIDDLE, 1)
        line = jnp.where((lane >= MIDDLE) & (lane < MIDDLE + COARSE), line, 0.0)
        for k in range(4):
            lean[j, pl.ds(k, 8, stride=4), :] = line
    for i in range(1, 15):
        line = mid[i]
        for k in range(2):
            tall[i, pl.ds(k, 16, stride=2), :] = line
    narrow = iota((32, LANES), 1) < MIDDLE
    packed = [jnp.where(narrow, tall[i], lean[i // 2]) for i in range(1, 15)]
    widened = select_dot(jnp.concatenate(packed, axis=0), spread_ref[...])
    for i in range(1, 15):
        e1a[i] = widened[32 * (i - 1) : 32 * i]

    sweep_planes(2, 13, e1a, f1_ref, k1x_ref, k1y_ref, k1z_ref, 2, smooth(e1b, wd1_ref))
    sweep_planes(3, 12, e1b, f1_ref, k1x_ref, k1y_ref, k1z_ref, 2, smooth(e1a, wd1_ref))
    for x in range(6, 26):
        va[x] = v_ref[x] + e1a[x // 2]
    sweep_planes(7, 24, va, side_ref, kx_ref, ky_ref, kz_ref, 1, smooth(vb, wd_ref))

    def finish(x, value, left):
        new = value + wd_ref[x] * left
        out_ref[x - 8] = new[8:24, :LANES]

    sweep_planes(8, 23, vb, side_ref, kx_ref, ky_ref, kz_ref, 1, finish)


def swap(x, axis, upper):
    count = lax.axis_size(axis)
    step = 1 if upper else -1
    return lax.ppermute(
        x, axis, [(i, (i + (step if i % 2 == 0 else -step)) % count) for i in range(count)]
    )


def shift(x, axis, direction):
    count = lax.axis_size(axis)
    return lax.ppermute(x, axis, [(i, (i + direction) % count) for i in range(count)])


def body(conc, right_side, order_field, grain_ids):
    face = ((9, 16, LANES), BF16)
    zface = ((17, 16, LANES), BF16)
    brick = ((16, 16, LANES), F32)
    place = jnp.stack([lax.axis_index("gx"), lax.axis_index("gy")]).astype(jnp.int32)
    conc, side, order, ids, xa, xb, ym = call(
        faces_kernel,
        [brick, brick, ((8, 16, 16, LANES), BF16), ((1, 1, 8, 8), jnp.int32)] + [face] * 3,
        (place, conc, right_side, order_field, grain_ids),
        specs=[SMEM] + [HBM] * 4,
        semaphores=4,
    )
    beside_b = swap(xb, "gx", True)
    beside_a = swap(xa, "gx", False)
    above = shift(ym, "gy", -1)
    inner, yp, zm, zp = call(
        inner_kernel,
        [brick, ((8, 16, LANES), BF16), zface, zface],
        (conc, order, ids),
        scratch=[((64, 8, LANES), F32)],
    )
    line = ((16, LANES), F32)
    payload = ((34, 16, LANES), BF16)
    partial, beyond, send_zm, send_zp = call(
        outer_kernel,
        [brick, line, payload, payload],
        (place, inner, conc, side, order, ids, beside_a, beside_b, above, yp, zm, zp),
        specs=[SMEM] + [VMEM] * 11,
    )
    left = shift(send_zp, "gz", 1)
    right = shift(send_zm, "gz", -1)
    keep, beside, low, high = call(
        split_kernel,
        [brick, line, ((80, 8, LANES), BF16), ((86, 8, LANES), BF16)],
        (partial, conc, side, beyond, left, right, zm, zp),
    )
    below = shift(high, "gy", 1)
    above = shift(low, "gy", -1)
    slab = ((5, 8, 32, LANES), BF16)
    keep, xl, xh, xa, xb = call(
        rows_kernel,
        [brick, slab, slab, slab, slab],
        (place, below, low, high, above, keep, beyond, beside),
        specs=[SMEM] + [VMEM] * 7,
    )
    beside_b = swap(xb, "gx", True)
    beside_a = swap(xa, "gx", False)
    fine = ((32, 32, RING), F32)
    middle = ((16, 32, RING), F32)
    *inner, mobility, picks0, picks1, pick_middle, spread = call(
        near_kernel,
        [((INNER[name][1], 32, RING), F32) for name in INNER]
        + [brick]
        + [((3 * RING, LANES), BF16)] * 2
        + [((RING, LANES), BF16), ((LANES, RING), BF16)],
        (keep, conc, side, xl, xh),
    )
    outer = [middle if name in MIDDLE_ARRAYS else fine for name in INNER]
    own, chunk, *outer = call(
        down_kernel,
        [((160, LANES), F32), ((32, CHUNK, LANES), BF16)] + outer[: len(KEPT)],
        (place, beside_a, beside_b, picks0, picks1, pick_middle) + tuple(inner),
        specs=[SMEM] + [VMEM] * (5 + len(inner)),
        scratch=outer[len(KEPT) :] + [middle] * 3 + [((320, LANES), F32)],
    )
    kept = tuple(inner[: len(KEPT)]) + tuple(outer)
    chunks = lax.all_to_all(chunk, ("gx", "gy"), 0, 0, tiled=True)
    plane = ((32, 16, LANES), F32)
    (out,) = call(
        up_kernel,
        [brick],
        (place, chunks, own, spread) + kept,
        scratch=[plane] * 9
        + [brick, ((16, 32, LANES), F32), ((8, 32, LANES), F32)]
        + [middle] * 2
        + [fine] * 2,
        specs=[SMEM] + [VMEM] * (3 + len(kept)),
    )
    return out, mobility


def solution(mesh):
    return jax.shard_map(
        body,
        mesh=mesh,
        in_specs=(
            P("gx", "gy", "gz"),
            P("gx", "gy", "gz"),
            P(None, "gx", "gy", "gz"),
            P("gx", "gy", "gz", None),
        ),
        out_specs=(P("gx", "gy", "gz"), P("gx", "gy", "gz")),
        check_vma=False,
    )
```

```python
import functools

import jax
import jax.numpy as jnp
from jax import lax
from jax.experimental import pallas as pl
from jax.experimental.pallas import tpu as pltpu
from jax.sharding import PartitionSpec as P

SLOTS = 8
BRICK = 16
OMEGA = 0.8
TAU = 256.0
LANES = 128
RING = 256
F32 = jnp.float32
BF16 = jnp.bfloat16
HIGH = lax.Precision.HIGHEST
VMEM = pl.BlockSpec(memory_space=pltpu.VMEM)
HBM = pl.BlockSpec(memory_space=pltpu.MemorySpace.HBM)
SMEM = pl.BlockSpec(memory_space=pltpu.SMEM)
COARSE = 51
COARSE_LOW = 10
MIDDLE = 70
HEAD = 26
CHUNK = 64


def call(kernel, outs, args, scratch=(), specs=None, places=None, limit=16, semaphores=0):
    specs = specs or [VMEM] * len(args)
    places = places or [VMEM] * len(outs)
    args = [
        pltpu.with_memory_space_constraint(arg, pltpu.MemorySpace.HBM) if spec is HBM else arg
        for arg, spec in zip(args, specs)
    ]
    scratches = [pltpu.VMEM(shape, dtype) for shape, dtype in scratch]
    if semaphores:
        scratches.append(pltpu.SemaphoreType.DMA((semaphores,)))
    return pl.pallas_call(
        kernel,
        out_shape=[
            pltpu.MemorySpace.HBM(*out) if place is HBM else jax.ShapeDtypeStruct(*out)
            for out, place in zip(outs, places)
        ],
        in_specs=specs,
        out_specs=places,
        scratch_shapes=scratches,
        compiler_params=pltpu.CompilerParams(vmem_limit_bytes=limit << 20),
    )(*args)


def roll(x, shift, axis):
    return pltpu.roll(x, shift % x.shape[axis], axis)


def iota(shape, axis):
    return lax.broadcasted_iota(jnp.int32, shape, axis)


def select_dot(a, picks):
    picks = picks.astype(BF16)
    total = None
    for _ in range(3):
        part = a.astype(BF16)
        a = a - part.astype(F32)
        term = jnp.dot(part, picks, preferred_element_type=F32)
        total = term if total is None else total + term
    return total


def lane_ids(ids_ref):
    ids = ids_ref[0, 0].astype(F32)
    spread = (iota((8, LANES), 1) // BRICK == iota((8, LANES), 0)).astype(F32)
    grains = lax.dot_general(
        ids, spread, (((0,), (0,)), ((), ())), precision=HIGH, preferred_element_type=F32
    )
    return jnp.floor(grains + 0.5)


def split_ids(grains):
    high = jnp.floor(grains * (1.0 / 64.0))
    return jnp.concatenate([high, grains - 64.0 * high], axis=0).astype(BF16)


def join_ids(rows):
    rows = rows.astype(F32)
    return rows[:8] * 64.0 + rows[8:]


def faces_kernel(
    conc_in, side_in, order_in, ids_in,
    conc_ref, side_ref, order_ref, ids_ref, ym_ref, sems,
):
    pairs = (
        (ids_in, ids_ref), (order_in, order_ref), (conc_in, conc_ref), (side_in, side_ref),
    )
    copies = [pltpu.make_async_copy(a, b, sems.at[k]) for k, (a, b) in enumerate(pairs)]
    for copy in copies:
        copy.start()
    copies[0].wait()
    copies[1].wait()
    grains = lane_ids(ids_ref)
    packed = split_ids(grains)
    ym_ref[SLOTS] = packed
    for slot in range(SLOTS):
        ym_ref[slot] = order_ref[slot].astype(F32)[:, 0, :].astype(BF16)
    copies[2].wait()
    copies[3].wait()


def square(x):
    return x * x


def sides_kernel(order_ref, ym_ref, xm_ref, xp_ref):
    for x, ref in ((0, xm_ref), (15, xp_ref)):
        ref[SLOTS] = ym_ref[SLOTS]
        for slot in range(SLOTS):
            ref[slot] = order_ref[slot, x]


def inner_kernel(
    conc_ref, order_ref, ids_ref, work, yp_ref, zm_ref, zp_ref, weights,
):
    grains = lane_ids(ids_ref)
    zm_ref[16] = split_ids(jnp.broadcast_to(grains[:, 0:1], (8, LANES)))
    zp_ref[16] = split_ids(jnp.broadcast_to(grains[:, LANES - 1 :], (8, LANES)))
    slots = iota((16, LANES), 1)
    low = [jnp.zeros((16, LANES), F32)] * 16
    high = [jnp.zeros((16, LANES), F32)] * 16
    for slot in range(SLOTS):
        cells = order_ref[slot].astype(F32)
        yp_ref[slot] = cells[:, 15, :].astype(BF16)
        for x in range(16):
            low[x] = jnp.where(slots == slot, cells[x, :, 0:1], low[x])
            high[x] = jnp.where(slots == slot, cells[x, :, LANES - 1 :], high[x])
    for x in range(16):
        zm_ref[x] = low[x].astype(BF16)
        zp_ref[x] = high[x].astype(BF16)

    own = lane_ids(ids_ref)
    lane = iota((16, LANES), 1)
    row = iota((16, LANES), 0)
    last = lane % BRICK == BRICK - 1
    edge = (last | (lane % BRICK == 0)) & (lane != 0) & (lane != LANES - 1)

    lane8 = iota((8, LANES), 1)
    beside = jnp.where(
        lane8 % BRICK == BRICK - 1, roll(own, -BRICK, 1), roll(own, BRICK, 1)
    )
    for other in range(SLOTS):
        match = (own == beside[other : other + 1]).astype(F32)
        for slot in range(SLOTS):
            weights[slot * SLOTS + other] = jnp.broadcast_to(match[slot : slot + 1], (8, LANES))

    def doubled(block):
        return jnp.concatenate([block, block], axis=0)

    def plane(x, carry_in):
        conc = conc_ref[x]
        base = 1.0 + 8.0 * square(conc * (1.0 - conc))
        along_y = jnp.zeros((16, LANES), F32)
        along_z = jnp.zeros((16, LANES), F32)
        along_x = jnp.zeros((16, LANES), F32)
        centers = []
        facing = []
        above = min(x + 1, 15)
        for slot in range(SLOTS):
            here = order_ref[slot, x].astype(F32)
            there = order_ref[slot, above].astype(F32)
            centers.append(here)
            along_x = along_x + square(there - here)
            along_y = along_y + square(roll(here, -1, 0) - here)
            right = roll(here, -1, 1)
            along_z = along_z + square(right - here)
            facing.append(jnp.where(last, right, roll(here, 1, 1)))
        along_y = jnp.where(row == 15, 0.0, along_y)
        along_z = jnp.where(last, 0.0, along_z)
        remapped = jnp.zeros((16, LANES), F32)
        for slot in range(SLOTS):
            value = None
            for other in range(SLOTS):
                term = doubled(weights[slot * SLOTS + other]) * facing[other]
                value = term if value is None else value + term
            remapped = remapped + square(value - centers[slot])
        total = base + along_y + roll(along_y, 1, 0) + along_z + roll(along_z, 1, 1)
        total = total + jnp.where(edge, remapped, 0.0) + along_x + carry_in
        work[x] = total
        return along_x

    carry = jnp.zeros((16, LANES), F32)
    for x in range(16):
        carry = plane(x, carry)

def across(center, ids, facing, facing_ids):
    facing = [facing(other).astype(F32) for other in range(SLOTS)]
    total = None
    for slot in range(SLOTS):
        value = None
        for other in range(SLOTS):
            match = ids[slot : slot + 1] == facing_ids[other : other + 1]
            term = match.astype(F32) * facing[other]
            value = term if value is None else value + term
        part = square(value - center(slot).astype(F32))
        total = part if total is None else total + part
    return total


def upper_kernel(ids_ref, yp_ref, own_yp_ref, top_ref, beyond_ref):
    own = lane_ids(ids_ref)
    above_ids = join_ids(yp_ref[SLOTS])
    top_ref[...] = across(lambda k: own_yp_ref[k], own, lambda k: yp_ref[k], above_ids)
    beyond_ref[...] = across(lambda k: yp_ref[k], above_ids, lambda k: own_yp_ref[k], own)


def outer_kernel(
    work, conc_ref, side_ref, order_ref, ids_ref, xm_ref, xp_ref, top_ref, beyond_ref,
    own_zm_ref, own_zp_ref, mob_ref, zm_out, zp_out,
):
    own = lane_ids(ids_ref)
    lane = iota((16, LANES), 1)
    row = iota((16, LANES), 0)

    first = work[0] + across(
        lambda k: order_ref[k, 0], own, lambda k: xm_ref[k], join_ids(xm_ref[SLOTS])
    )
    final = work[15] + across(
        lambda k: order_ref[k, 15], own, lambda k: xp_ref[k], join_ids(xp_ref[SLOTS])
    )
    top = top_ref[...]
    beyond = beyond_ref[...]
    zm_out[33] = beyond.astype(BF16)
    zp_out[33] = beyond.astype(BF16)
    for x in range(16):
        value = first if x == 0 else final if x == 15 else work[x]
        value = value + jnp.where(row == 15, top[x : x + 1], 0.0)
        mob_ref[x] = value
        conc, side = conc_ref[x], side_ref[x]
        down = jnp.where(
            lane < 43, value, jnp.where(lane < 86, roll(conc, 43, 1), roll(side, 86, 1))
        )
        zm_out[x] = down.astype(BF16)
        up = jnp.where(
            lane >= 85, value, jnp.where(lane >= 42, roll(conc, -43, 1), roll(side, -86, 1))
        )
        zp_out[x] = up.astype(BF16)
    zm_out[16:33] = own_zm_ref[...]
    zp_out[16:33] = own_zp_ref[...]


def facing_squares(near_ref, far_ref, near_lane, far_lane):
    near = near_ref[:16].reshape(256, LANES)
    far = far_ref[:16].reshape(256, LANES)
    near_ids = join_ids(near_ref[16])
    far_ids = join_ids(far_ref[16])
    diagonal = iota((8, LANES), 0) == iota((8, LANES), 1)
    slots = iota((8, LANES), 1) < SLOTS

    def squares(cells, ids, others, other_ids, target):
        along = jnp.sum(jnp.where(diagonal, ids, 0.0), axis=0, keepdims=True)
        match = ((other_ids == along) & slots).astype(F32)
        match = jnp.concatenate([match, jnp.zeros((LANES - 8, LANES), F32)], axis=0)
        seen = jnp.dot(others, match.astype(BF16), preferred_element_type=F32)
        place = (iota((LANES, LANES), 1) == target).astype(F32)
        total = select_dot(square(seen - cells.astype(F32)), place)
        return total.reshape(16, 16, LANES)

    return (
        squares(near, near_ids, far, far_ids, near_lane),
        squares(far, far_ids, near, near_ids, far_lane),
    )


def split_kernel(
    mob_ref, conc_ref, side_ref, beyond_ref, left_ref, right_ref, zm_ref, zp_ref,
    keep_ref, beside_ref, low_ref, high_ref,
):
    own_low, far_low = facing_squares(zm_ref, left_ref.at[16:33], 0, LANES - 1)
    own_high, far_high = facing_squares(zp_ref, right_ref.at[16:33], LANES - 1, 0)
    mob = mob_ref[...] + own_low + own_high
    keep_ref[...] = mob
    down = (left_ref[:16].astype(F32) + far_low).astype(BF16)
    up = (right_ref[:16].astype(F32) + far_high).astype(BF16)
    for place, value in enumerate((mob, conc_ref[...], side_ref[...], down, up)):
        planes = pl.ds(16 * place, 16)
        low_ref[planes] = value[:, :8].astype(BF16)
        high_ref[planes] = value[:, 8:].astype(BF16)
    lane = iota((16, LANES), 1)
    down, up = left_ref[33].astype(F32), right_ref[33].astype(F32)
    beside = jnp.where(lane < 43, up, jnp.where(lane >= 85, down, 0.0))
    beside_ref[...] = beside
    beyond = beyond_ref[...]
    high = beyond.astype(BF16)
    rest = (beyond - high.astype(F32)).astype(BF16)
    for k, value in enumerate((high, rest, beside.astype(BF16))):
        high_ref[80 + 2 * k] = value[:8]
        high_ref[81 + 2 * k] = value[8:]


def rows_kernel(
    below_ref, low_ref, high_ref, above_ref, mob_ref, beyond_ref, beside_ref,
    keep_ref, xl_ref, xh_ref,
):
    lane = iota((8, LANES), 1)
    first = iota((8, LANES), 0) == 0
    got = [
        jnp.concatenate([below_ref[80 + 2 * k], below_ref[81 + 2 * k]], axis=0).astype(F32)
        for k in range(3)
    ]
    missing = ((got[0] + got[1], got[2]), (beyond_ref[...], beside_ref[...]))
    for x in range(16):
        ref = xl_ref if x < 8 else xh_ref
        lines = []
        for main, beside in missing:
            main = jnp.where(first, main[x : x + 1], 0.0)
            beside = jnp.where(first, beside[x : x + 1], 0.0)
            down = jnp.where(lane >= 85, beside, 0.0)
            lines.append((main, None, None, down, jnp.where(lane < 43, beside, 0.0)))
        own = mob_ref[x, :8] + lines[0][0]
        keep_ref[x, :8] = own
        keep_ref[x, 8:] = mob_ref[x, 8:]
        for place in range(5):
            plane = 16 * place + x
            near, far = low_ref[plane], above_ref[plane]
            if place == 0:
                near = own.astype(BF16)
            elif place >= 3:
                near = (near.astype(F32) + lines[0][place]).astype(BF16)
            if place in (0, 3, 4):
                far = (far.astype(F32) + lines[1][place]).astype(BF16)
            for k, value in enumerate((below_ref[plane], near, high_ref[plane], far)):
                ref[place, x % 8, pl.ds(8 * k, 8), :] = value


def partner(x, step, axis):
    upper = (iota(x.shape, axis) & step) != 0
    return jnp.where(upper, roll(x, step, axis), roll(x, -step, axis))


def pair_sum(x, step, axis):
    return x + partner(x, step, axis)


def upper_of(x, step, axis):
    upper = (iota(x.shape, axis) & step) != 0
    return jnp.where(upper, x, roll(x, -step, axis))


def middle_cell(lane):
    cell = lane
    for place, end in enumerate((-2, -1, 64, 65, -3, 66)):
        cell = jnp.where(lane == 64 + place, end, cell)
    return cell


def groups(items, size):
    items = list(items)
    return [items[k : k + size] for k in range(0, len(items), size)]


def sweep_planes(first, last, values, source, kx, ky, kz, step, use, size=8, planes=None):
    at = (lambda x: x) if planes is None else (lambda x: x % planes)
    before = kx[at(first - 1)] * (values[at(first)] - values[at(first - 1)])
    for xs in groups(range(first, last + 1), size):
        cells = [values[at(x)] for x in xs + [xs[-1] + 1]]
        flux_z = [kz[at(x)] * (roll(v, -step, 1) - v) for x, v in zip(xs, cells)]
        back_z = [roll(flux, step, 1) for flux in flux_z]
        left = []
        for k, x in enumerate(xs):
            value = cells[k]
            flux_x = kx[at(x)] * (cells[k + 1] - value)
            flux_y = ky[at(x)] * (roll(value, -step, 0) - value)
            total = (source[at(x)] - value) + (flux_x - before)
            total = total + (flux_y - roll(flux_y, step, 0))
            left.append(total + (flux_z[k] - back_z[k]))
            before = flux_x
        for k, x in enumerate(xs):
            use(at(x), cells[k], left[k])


INNER = {
    "side": (8, 16), "kx": (8, 15), "ky": (9, 14), "kz": (9, 14), "wd": (9, 14), "v": (10, 12),
    "k1x": (4, 7), "k1y": (5, 6), "k1z": (5, 6), "wd1": (5, 6), "f1": (6, 4),
    "mob": (8, 16), "v0": (8, 16), "s1": (9, 14), "r0": (11, 10),
}
KEPT = ("side", "kx", "ky", "kz", "wd", "v", "k1x", "k1y", "k1z", "wd1", "f1")
MIDDLE_ARRAYS = ("k1x", "k1y", "k1z", "wd1", "f1")


class Inner:
    def __init__(self, name, ref):
        self.low, self.count = INNER[name]
        self.ref = ref

    def __contains__(self, x):
        return self.low <= x < self.low + self.count

    def __getitem__(self, x):
        return self.ref[x - self.low]

    def __setitem__(self, x, value):
        self.ref[x - self.low] = value


class Joined:
    def __init__(self, inner, outer):
        self.inner = inner
        self.outer = outer

    def __getitem__(self, x):
        return self.inner[x] if x in self.inner else self.outer[x]

    def __setitem__(self, x, value):
        self.outer[x] = value


def assemble(xs, parts_of, mob, v0, side):
    lane = iota((32, LANES), 1)
    for some in groups(xs, 8):
        planes = []
        for x in some:
            parts = parts_of(x)
            down, up = parts[3], parts[4]
            beyond = jnp.where(lane < 43, up, jnp.where(lane >= 85, down, 1.0))
            iterate = jnp.where(
                lane < 43, roll(up, -43, 1), jnp.where(lane >= 85, roll(down, 43, 1), 0.0)
            )
            right = jnp.where(
                lane < 42, roll(up, -86, 1), jnp.where(lane >= 86, roll(down, 86, 1), 0.0)
            )
            planes.append(zip(parts, (beyond, iterate, right)))
        for x, plane in zip(some, planes):
            for target, pair in zip((mob, v0, side), plane):
                target[x] = jnp.concatenate(pair, axis=1)


def descend(a, coeffs, sweeps, middle_x, middle, middle_f):
    half = TAU / 2
    mob, kx_ref, ky_ref, kz_ref, wd_ref = (a[k] for k in ("mob", "kx", "ky", "kz", "wd"))
    for first, last in coeffs:
        before = half * (mob[first - 1] + mob[first])
        kx_ref[first - 1] = before
        for xs in groups(range(first, last + 1), 7):
            here = [mob[x] for x in xs + [xs[-1] + 1]]
            kz = [half * (cells + roll(cells, -1, 1)) for cells in here[:-1]]
            back = [roll(k, 1, 1) for k in kz]
            done = []
            for k, x in enumerate(xs):
                kx = half * (here[k] + here[k + 1])
                ky = half * (here[k] + roll(here[k], -1, 0))
                total = (kx + before) + (ky + roll(ky, 1, 0)) + (kz[k] + back[k])
                done.append((kx, ky, OMEGA / (1.0 + total)))
                before = kx
            for k, x in enumerate(xs):
                kx_ref[x], ky_ref[x], wd_ref[x] = done[k]
                kz_ref[x] = kz[k]

    def smooth(target):
        def use(x, value, left):
            target[x] = value + wd_ref[x] * left

        return use

    def keep(x, value, left):
        a["r0"][x] = left

    steps = (("v0", smooth(a["s1"])), ("s1", smooth(a["v"])), ("v", keep))
    for (name, use), runs in zip(steps, sweeps):
        for first, last in runs:
            sweep_planes(first, last, a[name], a["side"], kx_ref, ky_ref, kz_ref, 1, use)

    def pool(x):
        return pair_sum(pair_sum(x, 1, 0), 1, 1)

    k1x_ref = a["k1x"]
    for xs in groups(middle_x, 7):
        done = [pool(kx_ref[2 * i + 1]) * (1.0 / 16.0) for i in xs]
        for i, value in zip(xs, done):
            k1x_ref[i] = value
    for xs in groups(middle, 6):
        done = []
        for i in xs:
            x = 2 * i
            along_y = pair_sum(ky_ref[x] + ky_ref[x + 1], 1, 1)
            k1y = upper_of(along_y, 1, 0) * (1.0 / 16.0)
            along_z = pair_sum(kz_ref[x] + kz_ref[x + 1], 1, 0)
            k1z = upper_of(along_z, 1, 1) * (1.0 / 16.0)
            total = k1x_ref[i] + k1x_ref[i - 1]
            total = total + (k1y + roll(k1y, 2, 0)) + (k1z + roll(k1z, 2, 1))
            done.append((k1y, k1z, OMEGA / (1.0 + total)))
        for i, value in zip(xs, done):
            a["k1y"][i], a["k1z"][i], a["wd1"][i] = value
    res = a["r0"]
    for xs in groups(middle_f, 8):
        done = [pool(res[2 * i] + res[2 * i + 1]) * 0.125 for i in xs]
        for i, value in zip(xs, done):
            a["f1"][i] = value


def selection_matrices(picks0_ref, picks1_ref, middle_ref, spread_ref):
    src = iota((RING, LANES), 0)
    dst = iota((RING, LANES), 1)
    cell = jnp.where(src < 192, src, src - RING)
    coarse = (cell + 4 * COARSE_LOW) // 4
    there = ((cell & 3) == 0) & (coarse >= 0) & (coarse < COARSE)
    head = there & (coarse < HEAD)
    tail = there & (coarse >= HEAD)
    sides = [there & (coarse == dst), there & (coarse + COARSE == dst)]
    picks0 = sides + [head & (coarse + 2 * COARSE == dst)]
    picks1 = sides + [tail & (coarse + 2 * COARSE - HEAD == dst)]
    picks0_ref[...] = jnp.concatenate([pick.astype(F32) for pick in picks0], axis=0).astype(BF16)
    picks1_ref[...] = jnp.concatenate([pick.astype(F32) for pick in picks1], axis=0).astype(BF16)
    pick_middle = (cell == 2 * middle_cell(dst)) & (dst < MIDDLE)
    middle_ref[...] = pick_middle.astype(F32).astype(BF16)
    src = iota((LANES, RING), 0)
    dst = iota((LANES, RING), 1)
    cell = jnp.where(dst < 192, dst, dst - RING)
    middle = (src < MIDDLE) & ((cell + 64) // 2 - 32 == middle_cell(src))
    coarse = (cell >= -4 * COARSE_LOW) & (src >= MIDDLE) & (src < MIDDLE + COARSE)
    coarse = coarse & ((cell + 4 * COARSE_LOW) // 4 == src - MIDDLE)
    spread_ref[...] = (middle | coarse).astype(F32).astype(BF16)


def near_kernel(mob_in, conc_in, side_in, xl_ref, xh_ref, *refs):
    a = {name: Inner(name, ref) for name, ref in zip(INNER, refs)}
    refs[len(INNER)][...] = mob_in[...]
    selection_matrices(*refs[len(INNER) + 1 :])
    own = (mob_in, conc_in, side_in)

    def parts_of(x):
        ref = xl_ref if x < 16 else xh_ref
        parts = [ref[place, x % 8].astype(F32) for place in range(5)]
        for place in range(3):
            part = parts[place]
            part = [part[:8], own[place][x - 8], part[24:]]
            parts[place] = jnp.concatenate(part, axis=0)
        return parts

    assemble(range(8, 24), parts_of, a["mob"], a["v0"], a["side"])
    descend(
        a, [(9, 22)], [[(9, 22)], [(10, 21)], [(11, 20)]], range(4, 11), range(5, 11), range(6, 10)
    )


def down_kernel(xm_ref, xp_ref, picks0_ref, picks1_ref, pick_middle_ref, *refs):
    count = len(INNER)
    inner, refs = refs[:count], refs[count:]
    own_ref, chunk_ref, *outer = refs[: 2 + count]
    e0, e1, r1, rows = refs[2 + count :]
    a = {
        name: Joined(Inner(name, near), far) for name, near, far in zip(INNER, inner, outer)
    }

    def parts_of(x):
        ref = xm_ref if x < 8 else xp_ref
        return [ref[place, x % 8].astype(F32) for place in range(5)]

    outside = list(range(8)) + list(range(24, 32))
    assemble(outside, parts_of, a["mob"], a["v0"], a["side"])
    descend(
        a,
        [(2, 8), (23, 29)],
        [[(2, 8), (23, 29)], [(3, 9), (22, 28)], [(4, 10), (21, 27)]],
        [1, 2, 3, 11, 12, 13],
        [2, 3, 4, 11, 12, 13],
        [2, 3, 4, 5, 10, 11, 12, 13],
    )
    f1_ref, k1x_ref, k1y_ref, k1z_ref, wd1_ref = (
        a[k] for k in ("f1", "k1x", "k1y", "k1z", "wd1")
    )
    for i in range(2, 14):
        e0[i] = wd1_ref[i] * f1_ref[i]

    def smooth(target, weight):
        def use(x, value, left):
            target[x] = value + weight[x] * left

        return use

    sweep_planes(3, 12, e0, f1_ref, k1x_ref, k1y_ref, k1z_ref, 2, smooth(e1, wd1_ref))

    def keep_middle(x, value, left):
        r1[x] = left

    sweep_planes(4, 11, e1, f1_ref, k1x_ref, k1y_ref, k1z_ref, 2, keep_middle)

    firsts = []
    seconds = []
    for j in range(4):
        i = 4 + 2 * j
        f2 = pair_sum(pair_sum(r1[i] + r1[i + 1], 2, 0), 2, 1) * 0.125
        k2x = pair_sum(pair_sum(k1x_ref[i + 1], 2, 0), 2, 1) * (1.0 / 16.0)
        k2y = pair_sum(k1y_ref[i] + k1y_ref[i + 1], 2, 1)
        k2y = upper_of(k2y, 2, 0) * (1.0 / 16.0)
        k2z = pair_sum(k1z_ref[i] + k1z_ref[i + 1], 2, 0)
        k2z = upper_of(k2z, 2, 1) * (1.0 / 16.0)
        f2, k2x, k2y, k2z = (cells[8:24] for cells in (f2, k2x, k2y, k2z))
        k2z = k2z.astype(BF16)
        high = f2.astype(BF16)
        low = (f2 - high.astype(F32)).astype(BF16)
        firsts.append(jnp.concatenate([high, low, k2z], axis=1))
        seconds.append(jnp.concatenate([k2x.astype(BF16), k2y.astype(BF16), k2z], axis=1))
    firsts = jnp.concatenate(firsts, axis=0)
    seconds = jnp.concatenate(seconds, axis=0)
    rows[pl.ds(0, 64), :] = jnp.dot(firsts, picks0_ref[...], preferred_element_type=F32)
    rows[pl.ds(64, 64), :] = jnp.dot(seconds, picks1_ref[...], preferred_element_type=F32)
    coarse = rows[pl.ds(0, 32, stride=4), :]
    rows[...] = select_dot(
        jnp.concatenate([e1[i] for i in range(3, 13)], axis=0), pick_middle_ref[...]
    )
    own_ref[...] = rows[pl.ds(0, 160, stride=2), :]

    blocks = [own_ref[pl.ds(16 * (1 + x) + 4, 8), :] for x in (1, 2, 5, 6)]
    for y in (1, 2):
        lines = [(x, k) for k in (y, y + 4) for x in (0, 3, 4, 7)]
        lines = [own_ref[pl.ds(16 * (1 + x) + 4 + k, 1), :] for x, k in lines]
        blocks.append(jnp.concatenate(lines, axis=0))
    narrow = iota((8, LANES), 1)
    middle = []
    for k in (0, 2, 4):
        middle.append(jnp.where(narrow < 64, blocks[k], roll(blocks[k + 1], 64, 1)))
    ends = jnp.zeros((8, LANES), F32)
    for k in range(6):
        ends = jnp.where(narrow // 4 == k, roll(blocks[k], 4 * k - 64, 1), ends)
    chunk = jnp.concatenate([coarse] + middle + [ends], axis=0).astype(BF16)
    for k in range(32):
        chunk_ref[k] = chunk


def up_kernel(
    place_ref, all_ref, own_ref, spread_ref, *refs
):
    count = len(KEPT)
    joined = [
        Joined(Inner(name, near), far)
        for name, near, far in zip(KEPT, refs[:count], refs[count : 2 * count])
    ]
    side_ref, kx_ref, ky_ref, kz_ref, wd_ref, v_ref = joined[:6]
    k1x_ref, k1y_ref, k1z_ref, wd1_ref, f1_ref = joined[6:]
    out_ref, pair0, pair1, c2x, c2y, c2z, wd2, f2, ea, eb = refs[2 * count : 2 * count + 10]
    mid, tall, lean, e1a, e1b, va, vb = refs[2 * count + 10 :]
    gx = place_ref[0]
    gy = place_ref[1]

    def source(dx, dy):
        return ((gx + dx + 8) & 7) * 4 + ((gy + dy + 4) & 3)

    for p in (0, 1, 2, 3, 4, 6, 7):
        for q in range(4):
            s = source(p - 1, q - 1)
            first = all_ref[s, pl.ds(0, 16), :].astype(F32)
            second = all_ref[s, pl.ds(16, 16), :].astype(F32)
            for i in range(4):
                pair0[4 * p + i, pl.ds(4 * q, 4), :] = first[4 * i : 4 * i + 4]
                pair1[4 * p + i, pl.ds(4 * q, 4), :] = second[4 * i : 4 * i + 4]
    for i in range(3, 13):
        mid[i] = own_ref[pl.ds(16 * (i - 3), 16), :]
    narrow = iota((8, LANES), 1)
    for p in (-1, 0, 1):
        for q in (-1, 0, 1):
            if p == 0 and q == 0:
                continue
            cells = all_ref[source(p, q), pl.ds(32, 32), :].astype(F32)
            ends = cells[24:]

            def block(k):
                main = cells[8 * (k // 2) : 8 * (k // 2) + 8]
                if k % 2:
                    main = roll(main, 64, 1)
                end = jnp.where(narrow < 68, roll(ends, 64 - 4 * k, 1), 0.0)
                return jnp.where(narrow < 64, main, end)

            for k, i in {-1: ((2, 1), (3, 2)), 0: (), 1: ((0, 13), (1, 14))}[p]:
                part = block(k)
                if q == -1:
                    mid[i, pl.ds(0, 4), :] = part[4:]
                elif q == 0:
                    mid[i, pl.ds(4, 8), :] = part
                else:
                    mid[i, pl.ds(12, 4), :] = part[:4]
            if q == 0:
                continue
            for depth in (0, 1):
                row = (1 if q == -1 else 13) + depth
                half = 4 if q == -1 else 0
                thin = block(4 + depth)
                for k, x in enumerate((0, 3, 4, 7)):
                    i = 8 * p + x + 4
                    if 3 <= i <= 12:
                        mid[i, pl.ds(row, 1), :] = thin[half + k : half + k + 1]
            if p == 0:
                for k, x in enumerate((1, 2, 5, 6)):
                    line = 5 if q == -1 else 1
                    part = block(k)
                    for depth in (0, 1):
                        row = (1 if q == -1 else 13) + depth
                        mid[x + 4, pl.ds(row, 1), :] = part[line + depth : line + depth + 1]

    used = iota((16, LANES), 1) < COARSE
    head = iota((16, LANES), 1) < HEAD
    for x in range(-6, 17):
        k = x % 32
        first = pair0[k]
        second = pair1[k]
        f2[k] = jnp.where(used, first + roll(first, -COARSE, 1), 0.0)
        c2x[k] = jnp.where(used, second, 0.0)
        c2y[k] = jnp.where(used, roll(second, -COARSE, 1), 0.0)
        last = jnp.where(
            head, roll(first, -2 * COARSE, 1), roll(second, HEAD - 2 * COARSE, 1)
        )
        c2z[k] = jnp.where(used, last, 0.0)
    for xs in groups(range(-5, 17), 11):
        done = []
        for x in xs:
            k = x % 32
            ky = c2y[k]
            kz = c2z[k]
            total = c2x[k] + c2x[(x - 1) % 32]
            total = total + (ky + roll(ky, 1, 0)) + (kz + roll(kz, 1, 1))
            weight = OMEGA / (1.0 + total)
            done.append((weight, weight * f2[k]))
        for x, value in zip(xs, done):
            wd2[x % 32], ea[x % 32] = value

    def smooth(target, weight):
        def use(x, value, left):
            target[x] = value + weight[x] * left

        return use

    old, new = ea, eb
    for reach in range(6, -1, -1):
        sweep_planes(
            2 - reach, 9 + reach, old, f2, c2x, c2y, c2z, 1, smooth(new, wd2), 10, 32
        )
        old, new = new, old

    lane = iota((8, LANES), 1)
    for j in range(8):
        line = roll(old[2 + j, pl.ds(2, 8), :], MIDDLE, 1)
        line = jnp.where((lane >= MIDDLE) & (lane < MIDDLE + COARSE), line, 0.0)
        for k in range(4):
            lean[j, pl.ds(k, 8, stride=4), :] = line
    for i in range(1, 15):
        line = mid[i]
        for k in range(2):
            tall[i, pl.ds(k, 16, stride=2), :] = line
    narrow = iota((32, LANES), 1) < MIDDLE
    packed = [jnp.where(narrow, tall[i], lean[i // 2]) for i in range(1, 15)]
    widened = select_dot(jnp.concatenate(packed, axis=0), spread_ref[...])
    for i in range(1, 15):
        e1a[i] = widened[32 * (i - 1) : 32 * i]

    sweep_planes(2, 13, e1a, f1_ref, k1x_ref, k1y_ref, k1z_ref, 2, smooth(e1b, wd1_ref))
    sweep_planes(3, 12, e1b, f1_ref, k1x_ref, k1y_ref, k1z_ref, 2, smooth(e1a, wd1_ref))
    for x in range(6, 26):
        va[x] = v_ref[x] + e1a[x // 2]
    sweep_planes(7, 24, va, side_ref, kx_ref, ky_ref, kz_ref, 1, smooth(vb, wd_ref))

    def finish(x, value, left):
        new = value + wd_ref[x] * left
        out_ref[x - 8] = new[8:24, :LANES]

    sweep_planes(8, 23, vb, side_ref, kx_ref, ky_ref, kz_ref, 1, finish)


def shift(x, axis, direction):
    count = lax.axis_size(axis)
    return lax.ppermute(x, axis, [(i, (i + direction) % count) for i in range(count)])


def body(conc, right_side, order_field, grain_ids):
    face = ((9, 16, LANES), BF16)
    zface = ((17, 16, LANES), BF16)
    brick = ((16, 16, LANES), F32)
    conc, side, order, ids, ym = call(
        faces_kernel,
        [brick, brick, ((8, 16, 16, LANES), BF16), ((1, 1, 8, 8), jnp.int32), face],
        (conc, right_side, order_field, grain_ids),
        specs=[HBM] * 4,
        semaphores=4,
    )
    above = shift(ym, "gy", -1)
    xm, xp = call(sides_kernel, [face, face], (order, ym))
    before = shift(xp, "gx", 1)
    after = shift(xm, "gx", -1)
    inner, yp, zm, zp = call(
        inner_kernel,
        [brick, ((8, 16, LANES), BF16), zface, zface],
        (conc, order, ids),
        scratch=[((64, 8, LANES), F32)],
    )
    line = ((16, LANES), F32)
    payload = ((34, 16, LANES), BF16)
    top, beyond = call(upper_kernel, [line, line], (ids, above, yp))
    partial, send_zm, send_zp = call(
        outer_kernel,
        [brick, payload, payload],
        (inner, conc, side, order, ids, before, after, top, beyond, zm, zp),
    )
    left = shift(send_zp, "gz", 1)
    right = shift(send_zm, "gz", -1)
    keep, beside, low, high = call(
        split_kernel,
        [brick, line, ((80, 8, LANES), BF16), ((86, 8, LANES), BF16)],
        (partial, conc, side, beyond, left, right, zm, zp),
    )
    below = shift(high, "gy", 1)
    above = shift(low, "gy", -1)
    slab = ((5, 8, 32, LANES), BF16)
    keep, xl, xh = call(
        rows_kernel,
        [brick, slab, slab],
        (below, low, high, above, keep, beyond, beside),
    )
    before = shift(xh, "gx", 1)
    after = shift(xl, "gx", -1)
    fine = ((32, 32, RING), F32)
    middle = ((16, 32, RING), F32)
    *inner, mobility, picks0, picks1, pick_middle, spread = call(
        near_kernel,
        [((INNER[name][1], 32, RING), F32) for name in INNER]
        + [brick]
        + [((3 * RING, LANES), BF16)] * 2
        + [((RING, LANES), BF16), ((LANES, RING), BF16)],
        (keep, conc, side, xl, xh),
    )
    outer = [middle if name in MIDDLE_ARRAYS else fine for name in INNER]
    own, chunk, *outer = call(
        down_kernel,
        [((160, LANES), F32), ((32, CHUNK, LANES), BF16)] + outer[: len(KEPT)],
        (before, after, picks0, picks1, pick_middle) + tuple(inner),
        scratch=outer[len(KEPT) :] + [middle] * 3 + [((320, LANES), F32)],
    )
    kept = tuple(inner[: len(KEPT)]) + tuple(outer)
    place = jnp.stack([lax.axis_index("gx"), lax.axis_index("gy")]).astype(jnp.int32)
    chunk, place = lax.optimization_barrier((chunk, place))
    chunks = lax.all_to_all(chunk, ("gx", "gy"), 0, 0, tiled=True)
    plane = ((32, 16, LANES), F32)
    (out,) = call(
        up_kernel,
        [brick],
        (place, chunks, own, spread) + kept,
        scratch=[plane] * 9
        + [brick, ((16, 32, LANES), F32), ((8, 32, LANES), F32)]
        + [middle] * 2
        + [fine] * 2,
        specs=[SMEM] + [VMEM] * (3 + len(kept)),
    )
    return out, mobility


def solution(mesh):
    return jax.shard_map(
        body,
        mesh=mesh,
        in_specs=(
            P("gx", "gy", "gz"),
            P("gx", "gy", "gz"),
            P(None, "gx", "gy", "gz"),
            P("gx", "gy", "gz", None),
        ),
        out_specs=(P("gx", "gy", "gz"), P("gx", "gy", "gz")),
        check_vma=False,
    )
```
